768 devices in a mesh: tile: 96 (over z_lo, x, y), section: 8 (over z_hi, core).
Axes of the slice: x: 4, y: 8, z: 12 (z_hi: 4, z_lo: 3; z = z_hi * 3 + z_lo), core: 2. Of those that a mesh axis runs over, the one named last changes fastest.
Arguments:
- state: float32 [5, 2, 2304, 3072], P(None, None, 'tile', 'section'), may hold values from -6 to 6
- courant: float32 [2, 2, 2304, 3072], P(None, None, 'tile', 'section'), may hold values from -0.4 to 0.4
- nest_offset: int32 [1], replicated, may hold values from 24 to 359
Outputs:
- new_state: float32 [5, 2, 2304, 3072], P(None, None, 'tile', 'section')
The draws below stay inside these ranges and needn't reach their ends.
All inputs are finite; a program needn't handle non-finite values.
Results may differ from the reference program's by a relative error of at most 0.000053.
Values sent between devices are 32-bit elements; how exact they have to be, the bound alone decides.
A program may use at most 64 MiB of HBM per device.

```python
import jax
import jax.numpy as jnp
from jax import lax

FIELDS = 5
LEVELS = 2
ROWS_DEV = 24
RATIO = 3
ZONE = 5
NY = 2304
NXA = 3072
NXP = 768
NXN = 2304
NEST_H = 768
N_TILE = 96


def block_levels(key, shape, shards, low, top_value):
    factor_of = 1.0
    for dim, blocks in shards:
        steps = jax.random.uniform(jax.random.fold_in(jax.random.fold_in(key, 6), dim), (blocks,), jnp.float32, low / len(shards), top_value / len(shards))
        factor_of = factor_of * jnp.repeat(jnp.exp(steps), shape[dim] // blocks).reshape((-1,) + (1,) * (len(shape) - 1 - dim))
    return factor_of


def normal_values(key, shape, scale, most, cuts=(), kind=jnp.bfloat16):
    result = jax.random.normal(key, shape, jnp.float32) * scale
    if len(cuts) > 0:
        result = block_levels(key, shape, cuts, -0.22, 0.18) * result
    return jnp.clip(result, min=-most, max=most).astype(kind)


def setup_inputs(seed: int = 0) -> dict:
    seeds = jax.random.split(jax.random.key(seed), 4)
    return {
        "state": normal_values(seeds[0], (FIELDS, LEVELS, NY, NXA), 1.0, 6.0, ((2, 96), (3, 8)), jnp.float32),
        "courant": jnp.clip(jax.random.uniform(seeds[1], (2, LEVELS, NY, NXA), jnp.float32, -0.4, 0.4) * block_levels(seeds[1], (2, LEVELS, NY, NXA), ((2, 96), (3, 8)), -0.4, 0.0), -0.4, 0.4),
        "nest_offset": jax.random.randint(seeds[2], (1,), ROWS_DEV, min(NY - NEST_H - 3, ROWS_DEV * max(N_TILE // 6 - 1, 4))).astype(jnp.int32),
    }


diffusion = 0.02
mixing = 0.05


def advance(values, courant):
    padded = jnp.pad(values, ((0, 0), (1, 1), (1, 1), (1, 1)), mode="edge")
    level_below = padded[:, :-2, 1:-1, 1:-1]
    level_above = padded[:, 2:, 1:-1, 1:-1]
    south_side = padded[:, 1:-1, :-2, 1:-1]
    north_side = padded[:, 1:-1, 2:, 1:-1]
    west_side = padded[:, 1:-1, 1:-1, :-2]
    east_side = padded[:, 1:-1, 1:-1, 2:]
    speed_y = courant[0]
    speed_x = courant[1]
    transport = (jnp.maximum(speed_y, 0.0) * (values - south_side) + jnp.minimum(speed_y, 0.0) * (north_side - values)
                 + jnp.maximum(speed_x, 0.0) * (values - west_side) + jnp.minimum(speed_x, 0.0) * (east_side - values))
    spread = south_side + north_side + west_side + east_side - 4.0 * values
    column = level_below + level_above - 2.0 * values
    return values - transport + diffusion * spread + mixing * column


def upsample(values):
    return jnp.repeat(jnp.repeat(values, RATIO, axis=2), RATIO, axis=3)


def reference(state, courant, nest_offset):
    offset = nest_offset[0]
    parent = state[:, :, :, :NXP]
    nest_field = state[:, :, :, NXP:]
    parent_new = advance(parent, courant[:, :, :, :NXP])
    nest_courant = courant[:, :, :, NXP:]
    fine_old = upsample(lax.dynamic_slice_in_dim(parent, offset, NEST_H, 2))
    fine_new = upsample(lax.dynamic_slice_in_dim(parent_new, offset, NEST_H, 2))
    row_index = jnp.arange(NY)
    col_index = jnp.arange(NXN)
    row_depth = jnp.minimum(row_index, NY - 1 - row_index)
    col_depth = jnp.minimum(col_index, NXN - 1 - col_index)
    depth = jnp.minimum(row_depth[:, None], col_depth[None, :])
    weight = (jnp.maximum(ZONE - depth, 0) / ZONE).astype(state.dtype)
    for substep in range(RATIO):
        moved = advance(nest_field, nest_courant)
        fraction = (substep + 1) / RATIO
        target = fine_old + fraction * (fine_new - fine_old)
        nest_field = moved + weight * (target - moved)
    fields = state.shape[0]
    levels = state.shape[1]
    averaged = nest_field.reshape(fields, levels, NEST_H, RATIO, NXP, RATIO).sum(axis=(3, 5)) / (RATIO * RATIO)
    parent_final = lax.dynamic_update_slice_in_dim(parent_new, averaged, offset, 2)
    return jnp.concatenate([parent_final, nest_field], axis=3)
```

```python
import functools

import jax
import jax.numpy as jnp
from jax import lax
from jax.experimental import pallas as pl
from jax.experimental.pallas import tpu as pltpu
from jax.sharding import PartitionSpec as P

RATIO = 3
ZONE = 5
DIFFUSION = 0.02
MIXING = 0.05
FIELDS = 5
LEVELS = 2
ROWS = 24
COLS = 384
LANES = 128
COARSE = ROWS // RATIO
TALL = 32
WIDE = 512
PAIRS = FIELDS * LEVELS
MESH = pl.DeviceIdType.MESH
HIGHEST = lax.Precision.HIGHEST

NEAR = ((-1, 0), (-1, 0), (1, 0), (1, 0), (0, -1), (-1, -1), (1, -1), (0, 1), (-1, 1), (1, 1))
NEAR_PEERS = ((-1, 0), (1, 0), (0, -1), (-1, -1), (1, -1), (0, 1), (-1, 1), (1, 1))


def iota(shape, dim):
    return lax.broadcasted_iota(jnp.int32, shape, dim)


def pick(flag, one, other):
    return jnp.where(flag, one, other)


def kernel(
    q, tiles, sections,
    offset_ref, state, courant, out,
    strips, near_strips, slab_state, slab_speed, side_columns,
    edge_in, stage, window_in, coef, mixed, force, slope, means, mean_in, fine_end,
    near_send, near_recv, edge_send, edge_recv, window_send, window_recv, mean_send, mean_recv,
):
    tile = lax.axis_index("tile")
    section = lax.axis_index("section")
    groups = tiles // RATIO
    is_parent = section < 2
    nest = section - 2
    group = tile // RATIO
    inner = tile - group * RATIO
    rest = offset_ref[0] - q * ROWS
    rim_column = (section == 2) | (section == sections - 1)
    rim_row = (section >= 2) & ((tile == 0) | (tile == tiles - 1))
    low_window = is_parent & (tile >= q - 1) & (tile <= q + 1)
    high_window = is_parent & (tile >= q + groups - 1) & (tile <= q + groups)
    in_window = low_window | high_window
    under = is_parent & (tile >= q) & (tile <= q + groups)

    def near_peer(step):
        return (
            lax.rem(tile + step[0] + tiles, tiles),
            lax.rem(section + step[1] + sections, sections),
        )

    @pl.when(rim_row)
    def _():
        window_in[...] = jnp.zeros_like(window_in)

    barrier = pltpu.get_barrier_semaphore()

    def greet(tile_to, section_to):
        pl.semaphore_signal(
            barrier, inc=1, device_id=(tile_to, section_to), device_id_type=MESH
        )

    @pl.when(rim_column)
    def _():
        for d in range(4):
            greet(q + group + d - 1, pick(section == 2, 0, 1))

    @pl.when(rim_row)
    def _():
        for u in range(3):
            sender = pick(tile == 0, q - 1 + u, q + groups - 1 + u)
            present = (tile == 0) | (u < 2)

            @pl.when(present & (nest <= 3))
            def _():
                greet(sender, 0)

            @pl.when(present & (nest >= 2))
            def _():
                greet(sender, 1)

    for step in NEAR_PEERS:
        greet(*near_peer(step))

    for late in range(2):
        @pl.when(is_parent & (tile - q - late >= 0) & (tile - q - late < groups))
        def _():
            for b in range(RATIO):
                for third in range(RATIO):
                    greet((tile - q - late) * RATIO + b, 2 + RATIO * section + third)

    lane = iota((ROWS, LANES), 1)
    left = jnp.zeros((ROWS, LANES), jnp.float32)
    right = jnp.zeros((ROWS, LANES), jnp.float32)
    for g in range(3 * PAIRS):
        kind, pair = g // PAIRS, g % PAIRS
        f, l = pair // LEVELS, pair % LEVELS
        source = state.at[f, l] if kind == 0 else courant.at[kind - 1, l]
        here = (lane >= 3 * g) & (lane < 3 * g + 3)
        first = source[:, :LANES]
        last = source[:, COLS - LANES :]
        left = jnp.where(here, pltpu.roll(first, 3 * g, 1) if g else first, left)
        right = jnp.where(here, pltpu.roll(last, 3 * g + 3, 1), right)
    strips[0] = left
    strips[1] = right

    @pl.when(in_window)
    def _():
        start = rest + pick(low_window, -1 - ROWS * (tile - q), 21 - ROWS * (tile - q - groups + 1))
        for j in range(4):
            row = start + j
            owned = jnp.where((row >= 0) & (row < ROWS), 1.0, 0.0)
            row = jnp.clip(row, 0, ROWS - 1)
            for l in range(LEVELS):
                place = slice(4 * l + j, 4 * l + j + 1)
                for f in range(FIELDS):
                    stage[f, place, :] = state[f, l, pl.ds(row, 1), :] * owned
                for d in range(2):
                    stage[FIELDS + d, place, :] = courant[d, l, pl.ds(row, 1), :] * owned

    force[...] = jnp.zeros_like(force)
    slope[...] = jnp.zeros_like(slope)

    edge_targets = sum(
        jnp.where((tile - q + 1 - d >= 0) & (tile - q + 1 - d < groups), RATIO, 0) for d in range(4)
    )
    waited = len(NEAR_PEERS) + pick(is_parent, edge_targets + pick(in_window, 4, 0), 2)
    pl.semaphore_wait(barrier, waited)

    def remote(source, target, send, recv, device):
        return pltpu.make_async_remote_copy(
            src_ref=source, dst_ref=target, send_sem=send, recv_sem=recv,
            device_id=device, device_id_type=MESH,
        )

    def edge_copy(d, b):
        target = (tile - q + 1 - d) * RATIO + b
        return remote(
            strips.at[pick(section == 0, 0, 1)], edge_in.at[pl.ds(ROWS * d, ROWS)],
            edge_send.at[d, b], edge_recv.at[d],
            (target, pick(section == 0, 2, sections - 1)),
        )

    def edge_present(d):
        aim = tile - q + 1 - d
        return is_parent & (aim >= 0) & (aim < groups)

    for d in range(4):
        @pl.when(edge_present(d))
        def _():
            for b in range(RATIO):
                edge_copy(d, b).start()

    def window_copy(k, dn):
        slot = 1 - dn
        u = pick(low_window, tile - q + 1, tile - q - groups + 1)
        return remote(
            stage.at[:, :, pl.ds(LANES * k, LANES)],
            window_in.at[u, :, :, pl.ds(LANES * slot, LANES)],
            window_send.at[k, dn + 1], window_recv.at[u, slot],
            (pick(low_window, 0, tiles - 1), 2 + RATIO * section + k + dn),
        )

    def window_present(k, dn):
        aim = RATIO * section + k + dn
        return in_window & (aim >= 0) & (aim <= 5)

    for k in range(3):
        for dn in range(-1, 2):
            @pl.when(window_present(k, dn))
            def _():
                window_copy(k, dn).start()

    def near_copy(i):
        source, target = (
            (state.at[:, :, 0:8, :], slab_state.at[0]),
            (courant.at[:, :, 0:8, :], slab_speed.at[0]),
            (state.at[:, :, 16:24, :], slab_state.at[1]),
            (courant.at[:, :, 16:24, :], slab_speed.at[1]),
            (strips.at[0], near_strips.at[0, 0:24]),
            (strips.at[0, 0:8], near_strips.at[0, 24:32]),
            (strips.at[0, 16:24], near_strips.at[0, 32:40]),
            (strips.at[1], near_strips.at[1, 0:24]),
            (strips.at[1, 0:8], near_strips.at[1, 24:32]),
            (strips.at[1, 16:24], near_strips.at[1, 32:40]),
        )[i]
        return remote(source, target, near_send.at[i], near_recv.at[i], near_peer(NEAR[i]))

    order = (4, 5, 6, 7, 8, 9, 1, 3, 0, 2)
    for i in order:
        near_copy(i).start()

    row = iota((TALL, WIDE), 0)
    col = iota((TALL, WIDE), 1)
    row = tile * ROWS + jnp.where(row < 28, row, row - TALL)
    col = pick(is_parent, section, nest) * COLS + jnp.where(col < 448, col, col - WIDE)
    last_row = tiles * ROWS - 1
    last_col = pick(is_parent, 2, 6) * COLS - 1
    depth = jnp.minimum(jnp.minimum(row, last_row - row), jnp.minimum(col, last_col - col))
    strength = pick(is_parent, 0.0, 1.0 / ZONE)
    weight = jnp.clip(ZONE - depth, 0, ZONE).astype(jnp.float32) * strength
    mixed[0] = weight
    mixed[1] = MIXING * (1.0 - weight)

    for i in (4, 5, 6, 7, 8, 9, 1, 3):
        near_copy(i).wait_recv()

    upper = iota((8, LANES), 0) < 4
    beside = []
    for side in range(2):
        corner = jnp.where(upper, near_strips[side, 24:32, :], near_strips[side, 32:40, :])
        beside.append(jnp.concatenate([near_strips[side, 0:24, :], corner], axis=0))
    from_right = iota((TALL, LANES), 1) < 64
    for i, g in enumerate(list(range(PAIRS)) + [10, 11, 20, 21]):
        right_part = pltpu.roll(beside[0], LANES - 3 * g, 1) if g else beside[0]
        left_part = pltpu.roll(beside[1], LANES - 3 * g - 3, 1)
        side_columns[i] = jnp.where(from_right, right_part, left_part)

    upper_rows = iota((8, COLS), 0) < 4

    def whole(own, slab_low, slab_high, sides):
        tall = jnp.concatenate([own, jnp.where(upper_rows, slab_low, slab_high)], axis=0)
        return jnp.concatenate([tall, sides], axis=1)

    keep = 1.0 - weight
    for l in range(LEVELS):
        speed_y, speed_x = (
            whole(courant[d, l], slab_speed[0, d, l], slab_speed[1, d, l], side_columns[PAIRS + 2 * d + l])
            for d in range(2)
        )
        south = jnp.where(row == 0, 0.0, jnp.maximum(speed_y, 0.0) + DIFFUSION) * keep
        north = jnp.where(row == last_row, 0.0, DIFFUSION - jnp.minimum(speed_y, 0.0)) * keep
        west = jnp.where(col == 0, 0.0, jnp.maximum(speed_x, 0.0) + DIFFUSION) * keep
        east = jnp.where(col == last_col, 0.0, DIFFUSION - jnp.minimum(speed_x, 0.0)) * keep
        coef[l, 0] = (1.0 - MIXING) * keep - south - north - west - east
        coef[l, 1] = south
        coef[l, 2] = north
        coef[l, 3] = west
        coef[l, 4] = east

    @pl.when(rim_column)
    def _():
        for d in range(4):
            pltpu.make_async_copy(strips.at[0], edge_in.at[pl.ds(ROWS * d, ROWS)], edge_recv.at[d]).wait()
        shape = (4 * ROWS, LANES)
        value = edge_in[...]
        speed_y = pltpu.roll(value, LANES - 3 * PAIRS, 1)
        speed_x = pltpu.roll(value, LANES - 6 * PAIRS, 1)
        place = iota(shape, 1)
        trio = (place * 171) >> 9
        within = place - 3 * trio
        level = trio & 1
        partner = jnp.where(level == 0, pltpu.roll(value, LANES - 3, 1), pltpu.roll(value, 3, 1))
        change = (
            (jnp.maximum(speed_y, 0.0) + DIFFUSION) * (pltpu.roll(value, 1, 0) - value)
            + (DIFFUSION - jnp.minimum(speed_y, 0.0)) * (pltpu.roll(value, 4 * ROWS - 1, 0) - value)
            + jnp.where(within == 0, 0.0, jnp.maximum(speed_x, 0.0) + DIFFUSION) * (pltpu.roll(value, 1, 1) - value)
            + jnp.where(within == 2, 0.0, DIFFUSION - jnp.minimum(speed_x, 0.0))
            * (pltpu.roll(value, LANES - 1, 1) - value)
            + MIXING * (partner - value)
        ) * (1.0 / RATIO)
        tall_row = iota((TALL, 4 * ROWS), 0)
        tall_row = jnp.where(tall_row < 28, tall_row, tall_row - TALL) + RATIO
        coarse = ((tall_row * 171) >> 9) - 1
        wanted = coarse + (ROWS + rest + COARSE * inner)
        select = (iota((TALL, 4 * ROWS), 1) == wanted).astype(jnp.float32)
        both = jnp.concatenate([value, change], axis=1)
        spread = jnp.dot(select, both, precision=HIGHEST, preferred_element_type=jnp.float32)
        column = iota((TALL, LANES), 1)
        block = pl.ds(pl.multiple_of(pick(section == 2, 0, COLS - LANES), LANES), LANES)
        share = mixed[0, :, block]
        for which, target in ((0, force), (1, slope)):
            for pair in range(PAIRS):
                at = LANES * which + 3 * pair
                lead, middle, trail = (
                    jnp.broadcast_to(spread[:, at + c : at + c + 1], (TALL, LANES)) for c in range(3)
                )
                filled = jnp.where(column < 3, lead, jnp.where(column < 125, middle, trail))
                target[pair, :, block] = share * filled

    @pl.when(rim_row)
    def _():
        for u in range(3):
            for slot in range(3):
                @pl.when(((tile == 0) | (u < 2)) & (nest + slot >= 1) & (nest + slot <= 6))
                def _():
                    lanes = pl.ds(LANES * slot, LANES)
                    pltpu.make_async_copy(
                        stage.at[:, :, lanes], window_in.at[u, :, :, lanes], window_recv.at[u, slot]
                    ).wait()
        shape = (8, COLS)
        speed_y = window_in[0, FIELDS] + window_in[1, FIELDS] + window_in[2, FIELDS]
        speed_x = window_in[0, FIELDS + 1] + window_in[1, FIELDS + 1] + window_in[2, FIELDS + 1]
        parent_col = iota(shape, 1) + LANES * (nest - 1)
        south = jnp.maximum(speed_y, 0.0) + DIFFUSION
        north = DIFFUSION - jnp.minimum(speed_y, 0.0)
        west = jnp.where(parent_col == 0, 0.0, jnp.maximum(speed_x, 0.0) + DIFFUSION)
        east = jnp.where(parent_col == 2 * COLS - 1, 0.0, DIFFUSION - jnp.minimum(speed_x, 0.0))
        values, changes = [], []
        for f in range(FIELDS):
            value = window_in[0, f] + window_in[1, f] + window_in[2, f]
            change = (
                south * (pltpu.roll(value, 1, 0) - value)
                + north * (pltpu.roll(value, 7, 0) - value)
                + west * (pltpu.roll(value, 1, 1) - value)
                + east * (pltpu.roll(value, COLS - 1, 1) - value)
                + MIXING * (pltpu.roll(value, 4, 0) - value)
            ) * (1.0 / RATIO)
            values.append(value)
            changes.append(change)
        fine = iota((COLS, WIDE), 1)
        fine = jnp.where(fine < 448, fine, fine - WIDE)
        ahead = fine - RATIO * (iota((COLS, WIDE), 0) - LANES)
        widen = ((ahead >= 0) & (ahead < RATIO)).astype(jnp.float32)
        stacked = jnp.concatenate(values + changes, axis=0)
        spread = jnp.dot(stacked, widen, precision=HIGHEST, preferred_element_type=jnp.float32)
        at_top = tile == 0
        sub = iota((8, WIDE), 0)
        first = sub < pick(at_top, 3, 5)
        in_zone = (sub >= pick(at_top, 0, 3)) & (sub < pick(at_top, 5, 8))
        block = pl.ds(pl.multiple_of(pick(at_top, 0, 16), 8), 8)
        share = mixed[0, block, :]
        for which, target in ((0, force), (1, slope)):
            for pair in range(PAIRS):
                f, l = pair // LEVELS, pair % LEVELS
                at = 8 * (FIELDS * which + f) + 4 * l + 1
                filled = jnp.where(first, spread[at : at + 1, :], spread[at + 1 : at + 2, :])
                target[pair, block, :] = jnp.where(in_zone, share * filled, target[pair, block, :])

    near_copy(0).wait_recv()
    near_copy(2).wait_recv()

    def load_field(f):
        return [
            whole(state[f, l], slab_state[0, f, l], slab_state[1, f, l], side_columns[2 * f + l])
            for l in range(LEVELS)
        ]

    def advance(pair):
        mix = mixed[1]
        result = []
        for l in range(LEVELS):
            value = pair[l]
            result.append(
                coef[l, 0] * value
                + coef[l, 1] * pltpu.roll(value, 1, 0)
                + coef[l, 2] * pltpu.roll(value, TALL - 1, 0)
                + coef[l, 3] * pltpu.roll(value, 1, 1)
                + coef[l, 4] * pltpu.roll(value, WIDE - 1, 1)
                + mix * pair[1 - l]
            )
        return result

    @pl.when(is_parent)
    def _():
        @pl.loop(0, FIELDS)
        def _(f):
            pair = advance(load_field(f))
            for l in range(LEVELS):
                out[f, l] = pair[l][:ROWS, :COLS]

    @pl.when(jnp.logical_not(is_parent))
    def _():
        @pl.loop(0, FIELDS)
        def _(f):
            pair = load_field(f)
            for k in range(RATIO):
                pair = advance(pair)
                pair = [
                    pair[l] + (force[2 * f + l] + (k + 1.0) * slope[2 * f + l]) for l in range(LEVELS)
                ]
            for l in range(LEVELS):
                out[f, l] = pair[l][:ROWS, :COLS]
                for c in range(RATIO):
                    fine_end[c, LEVELS * f + l] = pair[l][:ROWS, LANES * c : LANES * (c + 1)]

        ahead = iota((COLS, LANES), 0) - RATIO * iota((COLS, LANES), 1)
        gather = ((ahead >= 0) & (ahead < RATIO)).astype(jnp.float32)
        sums = [
            sum(fine_end[c, :, pl.ds(k, COARSE, stride=RATIO), :] for k in range(RATIO))
            .reshape(PAIRS * COARSE, LANES)
            for c in range(RATIO)
        ]
        block = jnp.dot(
            jnp.concatenate(sums, axis=1), gather, precision=HIGHEST, preferred_element_type=jnp.float32
        ) * (1.0 / (RATIO * RATIO))
        for pair in range(PAIRS):
            means[pair] = block[COARSE * pair : COARSE * (pair + 1), :]

    third = lax.rem(lax.max(nest, 0), RATIO)
    owner = lax.max(nest, 0) // RATIO

    def mean_copy(late):
        first_row = pl.multiple_of(pick(late == 1, 0, ROWS) + COARSE * inner, COARSE)
        first_col = pl.multiple_of(LANES * third, LANES)
        return remote(
            means, mean_in.at[:, pl.ds(first_row, COARSE), pl.ds(first_col, LANES)],
            mean_send.at[late], mean_recv.at[late, inner, third],
            (q + group + late, owner),
        )

    @pl.when(jnp.logical_not(is_parent))
    def _():
        for late in range(2):
            mean_copy(late).start()

    for i in order:
        near_copy(i).wait_send()
    for d in range(4):
        @pl.when(edge_present(d))
        def _():
            for b in range(RATIO):
                edge_copy(d, b).wait_send()
    for k in range(3):
        for dn in range(-1, 2):
            @pl.when(window_present(k, dn))
            def _():
                window_copy(k, dn).wait_send()

    @pl.when(jnp.logical_not(is_parent))
    def _():
        for late in range(2):
            mean_copy(late).wait_send()

    @pl.when(under)
    def _():
        for late in range(2):
            @pl.when((tile - q - late >= 0) & (tile - q - late < groups))
            def _():
                for b in range(RATIO):
                    for c in range(RATIO):
                        rows = pl.ds(ROWS * (1 - late) + COARSE * b, COARSE)
                        pltpu.make_async_copy(
                            means, mean_in.at[:, rows, pl.ds(LANES * c, LANES)], mean_recv.at[late, b, c]
                        ).wait()
        coarse_row = ROWS * (tile - q) - rest + iota((ROWS, COLS), 0)
        covered = (coarse_row >= 0) & (coarse_row < ROWS * groups)

        @pl.loop(0, PAIRS)
        def _(pair):
            f = pair // LEVELS
            l = pair - f * LEVELS
            fed = pltpu.roll(mean_in[pair], rest + ROWS, 0)[:ROWS, :]
            out[f, l] = jnp.where(covered, fed, out[f, l])


def solution(mesh):
    tiles = mesh.shape["tile"]
    sections = mesh.shape["section"]
    choices = max(tiles // 6 - 1, 4) - 1
    vmem = pl.BlockSpec(memory_space=pltpu.VMEM)

    def call(q, state, courant, nest_offset):
        def space(*shape):
            return pltpu.VMEM(shape, jnp.float32)

        def copies(*shape):
            return pltpu.SemaphoreType.DMA(shape)

        return pl.pallas_call(
            functools.partial(kernel, q, tiles, sections),
            out_shape=jax.ShapeDtypeStruct(state.shape, state.dtype),
            in_specs=[pl.BlockSpec(memory_space=pltpu.SMEM), vmem, vmem],
            out_specs=vmem,
            scratch_shapes=[
                space(2, ROWS, LANES),
                space(2, ROWS + 16, LANES),
                space(2, FIELDS, LEVELS, 8, COLS),
                space(2, 2, LEVELS, 8, COLS),
                space(PAIRS + 4, TALL, LANES),
                space(4 * ROWS, LANES),
                space(FIELDS + 2, 8, COLS),
                space(3, FIELDS + 2, 8, COLS),
                space(LEVELS, 5, TALL, WIDE),
                space(2, TALL, WIDE),
                space(PAIRS, TALL, WIDE),
                space(PAIRS, TALL, WIDE),
                space(PAIRS, COARSE, LANES),
                space(PAIRS, 2 * ROWS, COLS),
                space(RATIO, PAIRS, ROWS, LANES),
                copies(10), copies(10), copies(4, RATIO), copies(4),
                copies(3, 3), copies(3, 3), copies(2), copies(2, RATIO, RATIO),
            ],
            compiler_params=pltpu.CompilerParams(collective_id=q, has_side_effects=True),
            name=f"nested_step_{q}",
        )(nest_offset, state, courant)

    def on_device(state, courant, nest_offset):
        branches = [functools.partial(call, q) for q in range(1, choices + 1)]
        choice = jnp.clip(nest_offset[0] // ROWS - 1, 0, choices - 1)
        return lax.switch(choice, branches, state, courant, nest_offset)

    return jax.shard_map(
        on_device,
        mesh=mesh,
        in_specs=(P(None, None, "tile", "section"), P(None, None, "tile", "section"), P()),
        out_specs=P(None, None, "tile", "section"),
        check_vma=False,
    )
```

```python
import functools

import jax
import jax.numpy as jnp
from jax import lax
from jax.experimental import pallas as pl
from jax.experimental.pallas import tpu as pltpu
from jax.sharding import PartitionSpec as P

RATIO = 3
ZONE = 5
DIFFUSION = 0.02
MIXING = 0.05
FIELDS = 5
LEVELS = 2
ROWS = 24
COLS = 384
LANES = 128
COARSE = ROWS // RATIO
TALL = 32
WIDE = 512
PAIRS = FIELDS * LEVELS
PLANES = FIELDS + 2
MESH = pl.DeviceIdType.MESH

NEAR = ((-1, 0), (1, 0), (0, -1), (-1, -1), (1, -1), (0, 1), (-1, 1), (1, 1))


def iota(shape, dim):
    return lax.broadcasted_iota(jnp.int32, shape, dim)


def pick(flag, one, other):
    return jnp.where(flag, one, other)


def thirds(value):
    high = value.astype(jnp.bfloat16)
    rest = value - high.astype(jnp.float32)
    middle = rest.astype(jnp.bfloat16)
    low = (rest - middle.astype(jnp.float32)).astype(jnp.bfloat16)
    return [high, middle, low]


def dot_ones(value, ones):
    rows = value.shape[0]
    parts = jnp.dot(jnp.concatenate(thirds(value), axis=0), ones, preferred_element_type=jnp.float32)
    return parts[:rows] + parts[rows : 2 * rows] + parts[2 * rows :]


def kernel(
    q, tiles, sections,
    offset_ref, state_in, courant_in, out,
    state, courant, strips, near_strips, slabs, near_slabs, side_columns,
    edge_in, spread, stage, stage_side, window_in, window_side, coef, mixed, force, slope, work,
    fine, means, relay_in, relay_out, mean_in,
    load_sem, near_send, near_recv, edge_send, edge_recv, window_send, window_recv,
    relay_send, relay_recv, mean_send, mean_recv,
):
    tile = lax.axis_index("tile")
    section = lax.axis_index("section")
    groups = tiles // RATIO
    is_parent = section < 2
    is_nest = section >= 2
    nest = section - 2
    group = tile // RATIO
    inner = tile - group * RATIO
    rest = offset_ref[0] - q * ROWS
    rim_column = (section == 2) | (section == sections - 1)
    at_top = tile == 0
    rim_row = is_nest & (at_top | (tile == tiles - 1))
    low_window = is_parent & (tile >= q - 1) & (tile <= q + 1)
    high_window = is_parent & (tile >= q + groups - 1) & (tile <= q + groups)
    in_window = low_window | high_window
    under = is_parent & (tile >= q) & (tile <= q + groups)

    def relay_tile(a):
        return lax.min(a, groups - 1) * RATIO // groups * groups + lax.rem(q + a, groups)

    turn = lax.rem(tile - q + tiles, groups)
    wrapped = (turn == 0) & (tile // groups == RATIO - 1)
    task = pick(wrapped, groups, turn)
    is_relay = is_nest & (relay_tile(task) == tile)

    def near_peer(step):
        return (
            lax.rem(tile + step[0] + tiles, tiles),
            lax.rem(section + step[1] + sections, sections),
        )

    loads = [
        pltpu.make_async_copy(state_in, state, load_sem.at[0]),
        pltpu.make_async_copy(courant_in, courant, load_sem.at[1]),
    ]
    for load in loads:
        load.start()

    @pl.when(rim_row)
    def _():
        @pl.loop(0, 3)
        def _(u):
            window_in[u] = jnp.zeros((PLANES, 8, LANES), jnp.float32)
            window_side[u] = jnp.zeros((2, 8, LANES), jnp.float32)

    barrier = pltpu.get_barrier_semaphore()

    def greet(tile_to, section_to):
        pl.semaphore_signal(
            barrier, inc=1, device_id=(tile_to, section_to), device_id_type=MESH
        )

    @pl.when(rim_column)
    def _():
        @pl.loop(0, 4)
        def _(d):
            greet(q + group + d - 1, pick(section == 2, 0, 1))

    @pl.when(rim_row)
    def _():
        @pl.loop(0, pick(at_top, 3, 2))
        def _(u):
            sender = pick(at_top, q - 1, q + groups - 1) + u

            @pl.when(nest <= 3)
            def _():
                greet(sender, 0)

            @pl.when(nest >= 2)
            def _():
                greet(sender, 1)

    for step in NEAR:
        greet(*near_peer(step))

    def relay_source(late):
        return (task - late >= 0) & (task - late < groups)

    @pl.when(is_relay)
    def _():
        @pl.loop(0, 2)
        def _(late):
            @pl.when(relay_source(late))
            def _():
                @pl.loop(0, RATIO)
                def _(b):
                    source = (task - late) * RATIO + b

                    @pl.when(source != tile)
                    def _():
                        greet(source, section)

    @pl.when(under)
    def _():
        @pl.loop(0, RATIO)
        def _(third):
            greet(relay_tile(tile - q), 2 + RATIO * section + third)

    @pl.loop(0, PAIRS)
    def _(pair):
        force[pair] = jnp.zeros((TALL, WIDE), jnp.float32)
        slope[pair] = jnp.zeros((TALL, WIDE), jnp.float32)

    for load in loads:
        load.wait()

    upper = iota((8, COLS), 0) < 4

    def pack_rows(plane, first, second):
        slabs[0, plane] = jnp.where(upper, first[0:8, :], pltpu.roll(second[0:8, :], 4, 0))
        slabs[1, plane] = jnp.where(upper, pltpu.roll(first[16:24, :], 4, 0), second[16:24, :])

    @pl.loop(0, FIELDS)
    def _(f):
        pack_rows(f, state[f, 0], state[f, 1])

    @pl.loop(0, 2)
    def _(d):
        pack_rows(FIELDS + d, courant[d, 0], courant[d, 1])

    lane = iota((ROWS, LANES), 1)

    def pack_columns(f, packed):
        left, right = packed
        for l in range(LEVELS):
            for kind in range(3):
                g = PAIRS * kind + LEVELS * f + l
                source = state.at[f, l] if kind == 0 else courant.at[kind - 1, l]
                here = (lane >= 3 * g) & (lane < 3 * g + 3)
                left = jnp.where(here, pltpu.roll(source[:, :LANES], 3 * g, 1), left)
                right = jnp.where(here, pltpu.roll(source[:, COLS - LANES :], 3 * g + 3, 1), right)
        return left, right

    blank = jnp.zeros((ROWS, LANES), jnp.float32)
    left, right = lax.fori_loop(0, FIELDS, pack_columns, (blank, blank))
    strips[0] = left
    strips[1] = right

    @pl.when(in_window)
    def _():
        start = rest + pick(low_window, -1 - ROWS * (tile - q), 21 - ROWS * (tile - q - groups + 1))
        sub = iota((8, COLS), 0)

        def window_rows(plane, source):
            value = jnp.zeros((8, COLS), jnp.float32)
            for l in range(LEVELS):
                for j in range(4):
                    row = start + j
                    owned = (row >= 0) & (row < ROWS)
                    line = source(l)[pl.ds(jnp.clip(row, 0, ROWS - 1), 1), :] * jnp.where(owned, 1.0, 0.0)
                    value = jnp.where(sub == 4 * l + j, line, value)
            for k in range(3):
                stage[k, plane] = value[:, LANES * k : LANES * (k + 1)]

        @pl.loop(0, FIELDS)
        def _(f):
            window_rows(f, lambda l: state.at[f, l])

        @pl.loop(0, 2)
        def _(d):
            window_rows(FIELDS + d, lambda l: courant.at[d, l])

        place = iota((8, LANES), 1)

        @pl.loop(0, 3)
        def _(k):
            def pack_sides(plane, packed):
                low, high = packed
                value = stage[k, plane]
                here = (place >= 2 * plane) & (place < 2 * plane + 2)
                low = jnp.where(here, pltpu.roll(value, 2 * plane, 1), low)
                high = jnp.where(here, pltpu.roll(value, 2 * plane + 2, 1), high)
                return low, high

            empty = jnp.zeros((8, LANES), jnp.float32)
            low, high = lax.fori_loop(0, PLANES, pack_sides, (empty, empty))
            stage_side[k, 0] = high
            stage_side[k, 1] = low

    edge_targets = sum(
        jnp.where((tile - q + 1 - d >= 0) & (tile - q + 1 - d < groups), RATIO, 0) for d in range(4)
    )
    relay_targets = (
        sum(jnp.where(relay_tile(group + late) != tile, 1, 0) for late in range(2))
        + jnp.where(is_relay, 1, 0)
    )
    waited = len(NEAR) + pick(is_parent, edge_targets + jnp.where(in_window, 4, 0), relay_targets)
    pl.semaphore_wait(barrier, waited)

    def remote(source, target, send, recv, device):
        return pltpu.make_async_remote_copy(
            src_ref=source, dst_ref=target, send_sem=send, recv_sem=recv,
            device_id=device, device_id_type=MESH,
        )

    window_to = pick(at_top | low_window, 0, tiles - 1)
    window_slot = pick(low_window, tile - q + 1, tile - q - groups + 1)

    def window_copy(k):
        return remote(
            stage.at[k], window_in.at[window_slot], window_send.at[k], window_recv.at[window_slot],
            (window_to, 2 + RATIO * section + k),
        )

    def window_side_copy(k, side):
        return remote(
            stage_side.at[k, side], window_side.at[window_slot, side],
            window_send.at[3 + 2 * k + side], window_recv.at[3 + 2 * window_slot + side],
            (window_to, 2 + RATIO * section + k + 1 - 2 * side),
        )

    def for_windows(act):
        @pl.when(in_window)
        def _():
            @pl.loop(0, 3)
            def _(k):
                act(window_copy(k))
                for side in range(2):
                    aim = RATIO * section + k + 1 - 2 * side

                    @pl.when((aim >= 0) & (aim <= 5))
                    def _():
                        act(window_side_copy(k, side))

    for_windows(lambda copy: copy.start())

    def for_edges(act):
        @pl.when(is_parent)
        def _():
            @pl.loop(0, 4)
            def _(d):
                aim = tile - q + 1 - d

                @pl.when((aim >= 0) & (aim < groups))
                def _():
                    @pl.loop(0, RATIO)
                    def _(b):
                        act(
                            remote(
                                strips.at[section], edge_in.at[d], edge_send.at[d, b], edge_recv.at[d],
                                (aim * RATIO + b, pick(section == 0, 2, sections - 1)),
                            )
                        )

    for_edges(lambda copy: copy.start())

    def near_copy(i):
        source, target = (
            (slabs.at[0], near_slabs.at[0]),
            (slabs.at[1], near_slabs.at[1]),
            (strips.at[0], near_strips.at[0, 0:24]),
            (strips.at[0, 0:8], near_strips.at[0, 24:32]),
            (strips.at[0, 16:24], near_strips.at[0, 32:40]),
            (strips.at[1], near_strips.at[1, 0:24]),
            (strips.at[1, 0:8], near_strips.at[1, 24:32]),
            (strips.at[1, 16:24], near_strips.at[1, 32:40]),
        )[i]
        return remote(source, target, near_send.at[i], near_recv.at[i], near_peer(NEAR[i]))

    order = (2, 3, 4, 5, 6, 7, 0, 1)
    for i in order:
        near_copy(i).start()

    row = iota((TALL, WIDE), 0)
    col = iota((TALL, WIDE), 1)
    row = tile * ROWS + jnp.where(row < 28, row, row - TALL)
    col = pick(is_parent, section, nest) * COLS + jnp.where(col < 448, col, col - WIDE)
    last_row = tiles * ROWS - 1
    last_col = pick(is_parent, 2, 6) * COLS - 1
    depth = jnp.minimum(jnp.minimum(row, last_row - row), jnp.minimum(col, last_col - col))
    strength = pick(is_parent, 0.0, 1.0 / ZONE)
    mixed[0] = jnp.clip(ZONE - depth, 0, ZONE).astype(jnp.float32) * strength

    for i in order:
        near_copy(i).wait_recv()

    half = iota((8, LANES), 0) < 4
    beside = []
    for side in range(2):
        corner = jnp.where(half, near_strips[side, 24:32, :], near_strips[side, 32:40, :])
        beside.append(jnp.concatenate([near_strips[side, 0:24, :], corner], axis=0))
    from_right = iota((TALL, LANES), 1) < 64

    @pl.loop(0, PAIRS + 4)
    def _(i):
        g = i + jnp.where(i >= PAIRS + 2, PAIRS - 2, 0)
        right_part = pltpu.roll(beside[0], lax.rem(LANES - 3 * g, LANES), 1)
        left_part = pltpu.roll(beside[1], LANES - 3 * g - 3, 1)
        side_columns[i] = jnp.where(from_right, right_part, left_part)

    def whole(own, plane, l, sides):
        below, above = near_slabs[0, plane], near_slabs[1, plane]
        below = jnp.where(l == 0, below, pltpu.roll(below, 4, 0))
        above = jnp.where(l == 0, pltpu.roll(above, 4, 0), above)
        tall = jnp.concatenate([own, jnp.where(upper, below, above)], axis=0)
        return jnp.concatenate([tall, sides], axis=1)

    @pl.loop(0, LEVELS)
    def _(l):
        keep = 1.0 - mixed[0]
        speed_y, speed_x = (
            whole(courant[d, l], FIELDS + d, l, side_columns[PAIRS + 2 * d + l]) for d in range(2)
        )
        south = jnp.where(row == 0, 0.0, jnp.maximum(speed_y, 0.0) + DIFFUSION) * keep
        north = jnp.where(row == last_row, 0.0, DIFFUSION - jnp.minimum(speed_y, 0.0)) * keep
        west = jnp.where(col == 0, 0.0, jnp.maximum(speed_x, 0.0) + DIFFUSION) * keep
        east = jnp.where(col == last_col, 0.0, DIFFUSION - jnp.minimum(speed_x, 0.0)) * keep
        coef[l, 0] = (1.0 - MIXING) * keep - south - north - west - east
        coef[l, 1] = south
        coef[l, 2] = north
        coef[l, 3] = west
        coef[l, 4] = east
        mixed[1] = MIXING * keep

    @pl.when(rim_column)
    def _():
        for d in range(4):
            pltpu.make_async_copy(strips.at[0], edge_in.at[d], edge_recv.at[d]).wait()
        shape = (4 * ROWS, LANES)
        value = edge_in[...].reshape(shape)
        speed_y = pltpu.roll(value, LANES - 3 * PAIRS, 1)
        speed_x = pltpu.roll(value, LANES - 6 * PAIRS, 1)
        place = iota(shape, 1)
        trio = (place * 171) >> 9
        within = place - 3 * trio
        partner = jnp.where((trio & 1) == 0, pltpu.roll(value, LANES - 3, 1), pltpu.roll(value, 3, 1))
        change = (
            (jnp.maximum(speed_y, 0.0) + DIFFUSION) * (pltpu.roll(value, 1, 0) - value)
            + (DIFFUSION - jnp.minimum(speed_y, 0.0)) * (pltpu.roll(value, 4 * ROWS - 1, 0) - value)
            + jnp.where(within == 0, 0.0, jnp.maximum(speed_x, 0.0) + DIFFUSION) * (pltpu.roll(value, 1, 1) - value)
            + jnp.where(within == 2, 0.0, DIFFUSION - jnp.minimum(speed_x, 0.0))
            * (pltpu.roll(value, LANES - 1, 1) - value)
            + MIXING * (partner - value)
        ) * (1.0 / RATIO)
        wide = (TALL, 12 * ROWS)
        tall_row = iota(wide, 0)
        tall_row = jnp.where(tall_row < 28, tall_row, tall_row - TALL) + RATIO
        wanted = ((tall_row * 171) >> 9) - 1 + (ROWS + rest + COARSE * inner)
        source = iota(wide, 1)
        select = (source == wanted) | (source == wanted + 4 * ROWS) | (source == wanted + 8 * ROWS)
        both = jnp.concatenate([value, change], axis=1)
        rows = jnp.dot(
            jnp.where(select, 1.0, 0.0).astype(jnp.bfloat16),
            jnp.concatenate(thirds(both), axis=0),
            preferred_element_type=jnp.float32,
        )
        spread[0] = rows[:, :LANES]
        spread[1] = rows[:, LANES:]
        column = iota((TALL, LANES), 1)
        block = pl.ds(pl.multiple_of(pick(section == 2, 0, COLS - LANES), LANES), LANES)
        share = mixed[0, :, block]

        @pl.loop(0, PAIRS)
        def _(pair):
            for which, target in ((0, force), (1, slope)):
                turned = pltpu.roll(spread[which], lax.rem(LANES - 3 * pair, LANES), 1)
                lead, middle, trail = (
                    jnp.broadcast_to(turned[:, c : c + 1], (TALL, LANES)) for c in range(3)
                )
                filled = jnp.where(column < 3, lead, jnp.where(column < 125, middle, trail))
                target[pair, :, block] = share * filled

    @pl.when(rim_row)
    def _():
        @pl.loop(0, pick(at_top, 3, 2))
        def _(u):
            pltpu.make_async_copy(stage.at[0], window_in.at[u], window_recv.at[u]).wait()
            for side in range(2):
                @pl.when((nest - 1 + 2 * side >= 0) & (nest - 1 + 2 * side <= 5))
                def _():
                    pltpu.make_async_copy(
                        stage_side.at[0, side], window_side.at[u, side], window_recv.at[3 + 2 * u + side]
                    ).wait()

        sides = [window_side[0, side] + window_side[1, side] + window_side[2, side] for side in range(2)]

        def window(plane):
            centre = window_in[0, plane] + window_in[1, plane] + window_in[2, plane]
            before = pltpu.roll(sides[0], LANES - 2 * plane - 2, 1)
            after = pltpu.roll(sides[1], LANES - 2 * plane, 1) if plane else sides[1]
            return jnp.concatenate([before, centre, after], axis=1)

        speed_y, speed_x = window(FIELDS), window(FIELDS + 1)
        parent_col = iota((8, COLS), 1) + LANES * (nest - 1)
        south = jnp.maximum(speed_y, 0.0) + DIFFUSION
        north = DIFFUSION - jnp.minimum(speed_y, 0.0)
        west = jnp.where(parent_col == 0, 0.0, jnp.maximum(speed_x, 0.0) + DIFFUSION)
        east = jnp.where(parent_col == 2 * COLS - 1, 0.0, DIFFUSION - jnp.minimum(speed_x, 0.0))
        values, changes = [], []
        for f in range(FIELDS):
            value = window(f)
            change = (
                south * (pltpu.roll(value, 1, 0) - value)
                + north * (pltpu.roll(value, 7, 0) - value)
                + west * (pltpu.roll(value, 1, 1) - value)
                + east * (pltpu.roll(value, COLS - 1, 1) - value)
                + MIXING * (pltpu.roll(value, 4, 0) - value)
            ) * (1.0 / RATIO)
            values.append(value)
            changes.append(change)
        stacked = jnp.concatenate(values + changes, axis=0)
        sub = iota((8, LANES), 0)
        first = sub < pick(at_top, 3, 5)
        in_zone = (sub >= pick(at_top, 0, 3)) & (sub < pick(at_top, 5, 8))
        block = pl.ds(pl.multiple_of(pick(at_top, 0, 16), 8), 8)

        @pl.loop(0, 4)
        def _(k):
            column = iota((COLS, LANES), 1) + LANES * k
            column = jnp.where(column < 448, column, column - WIDE)
            ahead = column - RATIO * (iota((COLS, LANES), 0) - LANES)
            widen = jnp.where((ahead >= 0) & (ahead < RATIO), 1.0, 0.0).astype(jnp.bfloat16)
            rows = dot_ones(stacked, widen)
            lanes = pl.ds(pl.multiple_of(LANES * k, LANES), LANES)
            share = mixed[0, block, lanes]
            for which, target in ((0, force), (1, slope)):
                for pair in range(PAIRS):
                    f, l = pair // LEVELS, pair % LEVELS
                    at = 8 * (FIELDS * which + f) + 4 * l + 1
                    filled = jnp.where(first, rows[at : at + 1, :], rows[at + 1 : at + 2, :])
                    target[pair, block, lanes] = jnp.where(in_zone, share * filled, target[pair, block, lanes])

    ahead = iota((COLS, LANES), 0) - RATIO * iota((COLS, LANES), 1)
    gather = jnp.where((ahead >= 0) & (ahead < RATIO), 1.0, 0.0).astype(jnp.bfloat16)

    def for_relays(f, act, act_local):
        @pl.loop(0, 2)
        def _(late):
            target = relay_tile(group + late)

            @pl.when(target != tile)
            def _():
                act(
                    remote(
                        means.at[f], relay_in.at[f, late, inner], relay_send.at[f, late],
                        relay_recv.at[f, late, inner], (target, section),
                    )
                )

            if act_local is not None:
                @pl.when(target == tile)
                def _():
                    act_local(
                        pltpu.make_async_copy(
                            means.at[f], relay_in.at[f, late, inner], relay_recv.at[f, late, inner]
                        )
                    )

    steps = pick(is_parent, 1, RATIO)

    @pl.loop(0, FIELDS)
    def _(f):
        for l in range(LEVELS):
            work[l] = whole(state[f, l], f, l, side_columns[LEVELS * f + l])

        @pl.loop(0, steps)
        def _(k):
            fraction = (k + 1).astype(jnp.float32)
            pair = [work[l] for l in range(LEVELS)]
            mix = mixed[1]
            for l in range(LEVELS):
                value = pair[l]
                work[l] = (
                    coef[l, 0] * value
                    + coef[l, 1] * pltpu.roll(value, 1, 0)
                    + coef[l, 2] * pltpu.roll(value, TALL - 1, 0)
                    + coef[l, 3] * pltpu.roll(value, 1, 1)
                    + coef[l, 4] * pltpu.roll(value, WIDE - 1, 1)
                    + mix * pair[1 - l]
                    + (force[LEVELS * f + l] + fraction * slope[LEVELS * f + l])
                )

        for l in range(LEVELS):
            out[f, l] = work[l, :ROWS, :COLS]

        @pl.when(is_nest)
        def _():
            for l in range(LEVELS):
                for c in range(RATIO):
                    fine[c, l] = work[l, :ROWS, LANES * c : LANES * (c + 1)]
            sums = [
                sum(fine[c, :, pl.ds(k, COARSE, stride=RATIO), :] for k in range(RATIO))
                .reshape(LEVELS * COARSE, LANES)
                for c in range(RATIO)
            ]
            block = dot_ones(jnp.concatenate(sums, axis=1), gather) * (1.0 / (RATIO * RATIO))
            means[f] = block.reshape(LEVELS, COARSE, LANES)
            for_relays(f, lambda copy: copy.start(), lambda copy: copy.start())

    third = lax.rem(lax.max(nest, 0), RATIO)
    owner = lax.max(nest, 0) // RATIO

    def mean_copy(f):
        return remote(
            relay_out.at[f], mean_in.at[f, third], mean_send.at[f], mean_recv.at[f, third],
            (q + task, owner),
        )

    @pl.when(is_relay)
    def _():
        @pl.loop(0, FIELDS)
        def _(f):
            @pl.loop(0, 2)
            def _(late):
                @pl.when(relay_source(late))
                def _():
                    @pl.loop(0, RATIO)
                    def _(b):
                        pltpu.make_async_copy(
                            means.at[f], relay_in.at[f, late, b], relay_recv.at[f, late, b]
                        ).wait()
            for l in range(LEVELS):
                lined = jnp.concatenate(
                    [relay_in[f, late, b, l] for late in (1, 0) for b in range(RATIO)], axis=0
                )
                relay_out[f, l] = pltpu.roll(lined, rest + ROWS, 0)[:ROWS, :]
            mean_copy(f).start()

    @pl.when(under)
    def _():
        coarse_row = ROWS * (tile - q) - rest + iota((ROWS, COLS), 0)
        covered = (coarse_row >= 0) & (coarse_row < ROWS * groups)

        @pl.loop(0, FIELDS)
        def _(f):
            for c in range(RATIO):
                pltpu.make_async_copy(relay_out.at[f], mean_in.at[f, c], mean_recv.at[f, c]).wait()
            for l in range(LEVELS):
                fed = jnp.concatenate([mean_in[f, c, l] for c in range(RATIO)], axis=1)
                out[f, l] = jnp.where(covered, fed, out[f, l])

    for i in order:
        near_copy(i).wait_send()
    for_windows(lambda copy: copy.wait_send())
    for_edges(lambda copy: copy.wait_send())

    @pl.when(is_nest)
    def _():
        @pl.loop(0, FIELDS)
        def _(f):
            for_relays(f, lambda copy: copy.wait_send(), None)

    @pl.when(is_relay)
    def _():
        @pl.loop(0, FIELDS)
        def _(f):
            mean_copy(f).wait_send()


def solution(mesh):
    tiles = mesh.shape["tile"]
    sections = mesh.shape["section"]
    choices = max(tiles // 6 - 1, 4) - 1
    vmem = pl.BlockSpec(memory_space=pltpu.VMEM)
    anywhere = pl.BlockSpec(memory_space=pl.ANY)

    def call(q, state, courant, nest_offset):
        def space(*shape):
            return pltpu.VMEM(shape, jnp.float32)

        def copies(*shape):
            return pltpu.SemaphoreType.DMA(shape)

        return pl.pallas_call(
            functools.partial(kernel, q, tiles, sections),
            out_shape=jax.ShapeDtypeStruct(state.shape, state.dtype),
            in_specs=[pl.BlockSpec(memory_space=pltpu.SMEM), anywhere, anywhere],
            out_specs=vmem,
            scratch_shapes=[
                space(FIELDS, LEVELS, ROWS, COLS),
                space(2, LEVELS, ROWS, COLS),
                space(2, ROWS, LANES),
                space(2, ROWS + 16, LANES),
                space(2, PLANES, 8, COLS),
                space(2, PLANES, 8, COLS),
                space(PAIRS + 4, TALL, LANES),
                space(4, ROWS, LANES),
                space(2, TALL, LANES),
                space(3, PLANES, 8, LANES),
                space(3, 2, 8, LANES),
                space(3, PLANES, 8, LANES),
                space(3, 2, 8, LANES),
                space(LEVELS, 5, TALL, WIDE),
                space(2, TALL, WIDE),
                space(PAIRS, TALL, WIDE),
                space(PAIRS, TALL, WIDE),
                space(LEVELS, TALL, WIDE),
                space(RATIO, LEVELS, ROWS, LANES),
                space(FIELDS, LEVELS, COARSE, LANES),
                space(FIELDS, 2, RATIO, LEVELS, COARSE, LANES),
                space(FIELDS, LEVELS, ROWS, LANES),
                space(FIELDS, RATIO, LEVELS, ROWS, LANES),
                copies(2), copies(8), copies(8), copies(4, RATIO), copies(4),
                copies(9), copies(9), copies(FIELDS, 2), copies(FIELDS, 2, RATIO),
                copies(FIELDS), copies(FIELDS, RATIO),
            ],
            compiler_params=pltpu.CompilerParams(collective_id=q, has_side_effects=True),
            name=f"nested_step_{q}",
        )(nest_offset, state, courant)

    def on_device(state, courant, nest_offset):
        branches = [functools.partial(call, q) for q in range(1, choices + 1)]
        choice = jnp.clip(nest_offset[0] // ROWS - 1, 0, choices - 1)
        return lax.switch(choice, branches, state, courant, nest_offset)

    return jax.shard_map(
        on_device,
        mesh=mesh,
        in_specs=(P(None, None, "tile", "section"), P(None, None, "tile", "section"), P()),
        out_specs=P(None, None, "tile", "section"),
        check_vma=False,
    )
```

```python
import functools

import jax
import jax.numpy as jnp
from jax import lax
from jax.experimental import pallas as pl
from jax.experimental.pallas import tpu as pltpu
from jax.sharding import PartitionSpec as P

RATIO = 3
ZONE = 5
DIFFUSION = 0.02
MIXING = 0.05
FIELDS = 5
LEVELS = 2
ROWS = 24
COLS = 384
LANES = 128
COARSE = ROWS // RATIO
TALL = 32
WIDE = 512
PAIRS = FIELDS * LEVELS
PLANES = FIELDS + 2
MESH = pl.DeviceIdType.MESH

NEAR = ((-1, 0), (1, 0), (0, -1), (-1, -1), (1, -1), (0, 1), (-1, 1), (1, 1))


def iota(shape, dim):
    return lax.broadcasted_iota(jnp.int32, shape, dim)


def pick(flag, one, other):
    return jnp.where(flag, one, other)


def thirds(value):
    high = value.astype(jnp.bfloat16)
    rest = value - high.astype(jnp.float32)
    middle = rest.astype(jnp.bfloat16)
    low = (rest - middle.astype(jnp.float32)).astype(jnp.bfloat16)
    return [high, middle, low]


def dot_ones(value, ones):
    rows = value.shape[0]
    parts = jnp.dot(jnp.concatenate(thirds(value), axis=0), ones, preferred_element_type=jnp.float32)
    return parts[:rows] + parts[rows : 2 * rows] + parts[2 * rows :]


def kernel(
    q, tiles, sections,
    offset_ref, state_in, courant_in, out,
    state, courant, strips, near_strips, slabs, near_slabs, side_columns,
    edge_in, spread, spread_in, stage, window_in, rows_out, rows_in,
    coef, mixed, force, slope, work,
    fine, means, relay_in, relay_out, mean_in,
    load_sem, near_send, near_recv, edge_send, edge_recv, window_send, window_recv,
    spread_send, spread_recv, rows_send, rows_recv, edge_ready, rows_ready,
    relay_send, relay_recv, mean_send, mean_recv,
):
    tile = lax.axis_index("tile")
    section = lax.axis_index("section")
    groups = tiles // RATIO
    is_parent = section < 2
    is_nest = section >= 2
    nest = section - 2
    group = tile // RATIO
    inner = tile - group * RATIO
    rest = offset_ref[0] - q * ROWS
    rim_column = (section == 2) | (section == sections - 1)
    at_top = tile == 0
    at_end = at_top | (tile == tiles - 1)
    rim_row = is_nest & at_end
    row_relay = is_parent & at_end
    has_left = (section != 0) & (section != 2)
    has_right = (section != 1) & (section != sections - 1)
    low_window = is_parent & (tile >= q - 1) & (tile <= q + 1)
    high_window = is_parent & (tile >= q + groups - 1) & (tile <= q + groups)
    in_window = low_window | high_window
    window_to = pick(low_window, 0, tiles - 1)
    window_slot = pick(low_window, tile - q + 1, tile - q - groups + 1)
    window_first = pick(at_top, q - 1, q + groups - 1)
    window_count = pick(at_top, 3, 2)
    under = is_parent & (tile >= q) & (tile <= q + groups)
    third = lax.rem(lax.max(nest, 0), RATIO)
    owner = lax.max(nest, 0) // RATIO

    def relay_tile(a):
        return lax.min(a, groups - 1) * RATIO // groups * groups + lax.rem(q + a, groups)

    turn = lax.rem(tile - q + tiles, groups)
    wrapped = (turn == 0) & (tile // groups == RATIO - 1)
    task = pick(wrapped, groups, turn)
    is_relay = is_nest & (relay_tile(task) == tile)

    def near_peer(step):
        return lax.rem(tile + step[0] + tiles, tiles), section + step[1]

    loads = [
        pltpu.make_async_copy(state_in, state, load_sem.at[0]),
        pltpu.make_async_copy(courant_in, courant, load_sem.at[1]),
    ]
    for load in loads:
        load.start()

    @pl.when(row_relay)
    def _():
        @pl.loop(0, 3)
        def _(u):
            @pl.loop(0, 5)
            def _(slot):
                window_in[u, slot] = jnp.zeros((PLANES, 8, LANES), jnp.float32)

    near_strips[...] = jnp.zeros_like(near_strips)

    barrier = pltpu.get_barrier_semaphore()

    def greet(tile_to, section_to):
        pl.semaphore_signal(
            barrier, inc=1, device_id=(tile_to, section_to), device_id_type=MESH
        )

    rim_section = pick(section == 0, 2, sections - 1)

    @pl.when(is_parent)
    def _():
        greet(tile, rim_section)

        @pl.loop(0, 4)
        def _(d):
            sender = q + group + d - 1

            @pl.when(sender != tile)
            def _():
                greet(sender, section)

    @pl.when(row_relay)
    def _():
        @pl.loop(0, RATIO)
        def _(k):
            greet(tile, 2 + RATIO * section + k)

        @pl.loop(0, window_count)
        def _(u):
            greet(window_first + u, 1 - section)

            @pl.when(window_first + u != tile)
            def _():
                greet(window_first + u, section)

    for step in NEAR[:2]:
        greet(*near_peer(step))

    @pl.when(has_left)
    def _():
        for step in NEAR[2:5]:
            greet(*near_peer(step))

    @pl.when(has_right)
    def _():
        for step in NEAR[5:]:
            greet(*near_peer(step))

    def relay_source(late):
        return (task - late >= 0) & (task - late < groups)

    @pl.when(is_relay)
    def _():
        @pl.loop(0, 2)
        def _(late):
            @pl.when(relay_source(late))
            def _():
                @pl.loop(0, RATIO)
                def _(b):
                    source = (task - late) * RATIO + b

                    @pl.when(source != tile)
                    def _():
                        greet(source, section)

    @pl.when(under)
    def _():
        @pl.loop(0, RATIO)
        def _(third):
            greet(relay_tile(tile - q), 2 + RATIO * section + third)

    @pl.loop(0, PAIRS)
    def _(pair):
        force[pair] = jnp.zeros((TALL, WIDE), jnp.float32)
        slope[pair] = jnp.zeros((TALL, WIDE), jnp.float32)

    for load in loads:
        load.wait()

    upper = iota((8, COLS), 0) < 4

    def pack_rows(plane, first, second):
        slabs[0, plane] = jnp.where(upper, first[0:8, :], pltpu.roll(second[0:8, :], 4, 0))
        slabs[1, plane] = jnp.where(upper, pltpu.roll(first[16:24, :], 4, 0), second[16:24, :])

    @pl.loop(0, FIELDS)
    def _(f):
        pack_rows(f, state[f, 0], state[f, 1])

    @pl.loop(0, 2)
    def _(d):
        pack_rows(FIELDS + d, courant[d, 0], courant[d, 1])

    lane = iota((ROWS, LANES), 1)

    def pack_columns(f, packed):
        left, right = packed
        for l in range(LEVELS):
            for kind in range(3):
                g = PAIRS * kind + LEVELS * f + l
                source = state.at[f, l] if kind == 0 else courant.at[kind - 1, l]
                here = (lane >= 3 * g) & (lane < 3 * g + 3)
                left = jnp.where(here, pltpu.roll(source[:, :LANES], 3 * g, 1), left)
                right = jnp.where(here, pltpu.roll(source[:, COLS - LANES :], 3 * g + 3, 1), right)
        return left, right

    blank = jnp.zeros((ROWS, LANES), jnp.float32)
    left, right = lax.fori_loop(0, FIELDS, pack_columns, (blank, blank))
    strips[0] = left
    strips[1] = right

    @pl.when(in_window)
    def _():
        start = rest + pick(low_window, -1 - ROWS * (tile - q), 21 - ROWS * (tile - q - groups + 1))
        sub = iota((8, COLS), 0)

        def window_rows(plane, source):
            value = jnp.zeros((8, COLS), jnp.float32)
            for l in range(LEVELS):
                for j in range(4):
                    row = start + j
                    owned = (row >= 0) & (row < ROWS)
                    line = source(l)[pl.ds(jnp.clip(row, 0, ROWS - 1), 1), :] * jnp.where(owned, 1.0, 0.0)
                    value = jnp.where(sub == 4 * l + j, line, value)
            for k in range(3):
                stage[k, plane] = value[:, LANES * k : LANES * (k + 1)]

        @pl.loop(0, FIELDS)
        def _(f):
            window_rows(f, lambda l: state.at[f, l])

        @pl.loop(0, 2)
        def _(d):
            window_rows(FIELDS + d, lambda l: courant.at[d, l])

    edge_targets = sum(
        jnp.where((tile - q + 1 - d >= 0) & (tile - q + 1 - d < groups), RATIO, 0)
        - jnp.where(tile - q + 1 - d == group, 1, 0)
        for d in range(4)
    )
    window_targets = jnp.where(in_window, 1, 0) + jnp.where(in_window & (window_to != tile), 1, 0)
    relay_targets = (
        sum(jnp.where(relay_tile(group + late) != tile, 1, 0) for late in range(2))
        + jnp.where(is_relay, 1, 0)
        + jnp.where(rim_column, 1, 0)
        + jnp.where(rim_row, 1, 0)
    )
    near_targets = 2 + jnp.where(has_left, 3, 0) + jnp.where(has_right, 3, 0)
    waited = near_targets + pick(is_parent, edge_targets + window_targets, relay_targets)
    pl.semaphore_wait(barrier, waited)

    @pl.when(rim_column)
    def _():
        pl.semaphore_signal(
            edge_ready, inc=1, device_id=(tile, pick(section == 2, 0, 1)), device_id_type=MESH
        )

    @pl.when(rim_row)
    def _():
        pl.semaphore_signal(rows_ready.at[third], inc=1, device_id=(tile, owner), device_id_type=MESH)

    def remote(source, target, send, recv, device):
        return pltpu.make_async_remote_copy(
            src_ref=source, dst_ref=target, send_sem=send, recv_sem=recv,
            device_id=device, device_id_type=MESH,
        )

    def start(copy):
        copy.start()

    def wait_send(copy):
        copy.wait_send()

    def for_windows(act, act_local):
        @pl.when(in_window)
        def _():
            target = window_in.at[window_slot, 1:4]
            arrived = window_recv.at[window_slot, 0]

            @pl.when(window_to != tile)
            def _():
                act(remote(stage, target, window_send.at[0], arrived, (window_to, section)))

            if act_local is not None:
                @pl.when(window_to == tile)
                def _():
                    act_local(pltpu.make_async_copy(stage, target, arrived))

            act(
                remote(
                    stage.at[pick(section == 0, 2, 0)],
                    window_in.at[window_slot, pick(section == 0, 0, 4)],
                    window_send.at[1], window_recv.at[window_slot, 1], (window_to, 1 - section),
                )
            )

    for_windows(start, start)

    def for_edges(act, act_local):
        @pl.when(is_parent)
        def _():
            @pl.loop(0, 4)
            def _(d):
                aim = tile - q + 1 - d

                @pl.when((aim >= 0) & (aim < groups))
                def _():
                    @pl.loop(0, RATIO)
                    def _(b):
                        target = aim * RATIO + b

                        @pl.when(target != tile)
                        def _():
                            act(
                                remote(
                                    strips.at[section], edge_in.at[d], edge_send.at[d, b],
                                    edge_recv.at[d], (target, section),
                                )
                            )

                        if act_local is not None:
                            @pl.when(target == tile)
                            def _():
                                act_local(
                                    pltpu.make_async_copy(strips.at[section], edge_in.at[d], edge_recv.at[d])
                                )

    for_edges(start, start)

    def near_copy(i):
        source, target = (
            (slabs.at[0], near_slabs.at[0]),
            (slabs.at[1], near_slabs.at[1]),
            (strips.at[0], near_strips.at[0, 0:24]),
            (strips.at[0, 0:8], near_strips.at[0, 24:32]),
            (strips.at[0, 16:24], near_strips.at[0, 32:40]),
            (strips.at[1], near_strips.at[1, 0:24]),
            (strips.at[1, 0:8], near_strips.at[1, 24:32]),
            (strips.at[1, 16:24], near_strips.at[1, 32:40]),
        )[i]
        return remote(source, target, near_send.at[i], near_recv.at[i], near_peer(NEAR[i]))

    def for_near(act, left_exists, right_exists):
        @pl.when(left_exists)
        def _():
            for i in (2, 3, 4):
                act(near_copy(i))

        @pl.when(right_exists)
        def _():
            for i in (5, 6, 7):
                act(near_copy(i))

        for i in (0, 1):
            act(near_copy(i))

    for_near(start, has_left, has_right)

    def spread_copy():
        return remote(spread, spread_in, spread_send, spread_recv, (tile, rim_section))

    def rows_copy(k):
        return remote(
            rows_out.at[k], rows_in, rows_send.at[k], rows_recv, (tile, 2 + RATIO * section + k)
        )

    @pl.when(is_parent)
    def _():
        for d in range(4):
            pltpu.make_async_copy(strips.at[0], edge_in.at[d], edge_recv.at[d]).wait()
        shape = (4 * ROWS, LANES)
        value = edge_in[...].reshape(shape)
        speed_y = pltpu.roll(value, LANES - 3 * PAIRS, 1)
        speed_x = pltpu.roll(value, LANES - 6 * PAIRS, 1)
        place = iota(shape, 1)
        trio = (place * 171) >> 9
        within = place - 3 * trio
        partner = jnp.where((trio & 1) == 0, pltpu.roll(value, LANES - 3, 1), pltpu.roll(value, 3, 1))
        change = (
            (jnp.maximum(speed_y, 0.0) + DIFFUSION) * (pltpu.roll(value, 1, 0) - value)
            + (DIFFUSION - jnp.minimum(speed_y, 0.0)) * (pltpu.roll(value, 4 * ROWS - 1, 0) - value)
            + jnp.where(within == 0, 0.0, jnp.maximum(speed_x, 0.0) + DIFFUSION) * (pltpu.roll(value, 1, 1) - value)
            + jnp.where(within == 2, 0.0, DIFFUSION - jnp.minimum(speed_x, 0.0))
            * (pltpu.roll(value, LANES - 1, 1) - value)
            + MIXING * (partner - value)
        ) * (1.0 / RATIO)
        wide = (TALL, 12 * ROWS)
        tall_row = iota(wide, 0)
        tall_row = jnp.where(tall_row < 28, tall_row, tall_row - TALL) + RATIO
        wanted = ((tall_row * 171) >> 9) - 1 + (ROWS + rest + COARSE * inner)
        source = iota(wide, 1)
        select = (source == wanted) | (source == wanted + 4 * ROWS) | (source == wanted + 8 * ROWS)
        both = jnp.concatenate([value, change], axis=1)
        rows = jnp.dot(
            jnp.where(select, 1.0, 0.0).astype(jnp.bfloat16),
            jnp.concatenate(thirds(both), axis=0),
            preferred_element_type=jnp.float32,
        )
        spread[0] = rows[:, :LANES]
        spread[1] = rows[:, LANES:]
        pl.semaphore_wait(edge_ready, 1)
        spread_copy().start()

    @pl.when(row_relay)
    def _():
        @pl.loop(0, window_count)
        def _(u):
            beside_slot = pick(section == 0, 4, 0)
            pltpu.make_async_copy(stage, window_in.at[u, 1:4], window_recv.at[u, 0]).wait()
            pltpu.make_async_copy(stage.at[0], window_in.at[u, beside_slot], window_recv.at[u, 1]).wait()

        def window(plane):
            return jnp.concatenate([sum(window_in[u, k, plane] for u in range(3)) for k in range(5)], axis=1)

        shape = (8, 5 * LANES)
        speed_y, speed_x = window(FIELDS), window(FIELDS + 1)
        parent_col = iota(shape, 1) + (COLS * section - LANES)
        south = jnp.maximum(speed_y, 0.0) + DIFFUSION
        north = DIFFUSION - jnp.minimum(speed_y, 0.0)
        west = jnp.where(parent_col == 0, 0.0, jnp.maximum(speed_x, 0.0) + DIFFUSION)
        east = jnp.where(parent_col == 2 * COLS - 1, 0.0, DIFFUSION - jnp.minimum(speed_x, 0.0))
        within = iota(shape, 0) & 3
        is_value = (within == 1) | (within == 2)

        @pl.loop(0, FIELDS)
        def _(f):
            value = window(f)
            change = (
                south * (pltpu.roll(value, 1, 0) - value)
                + north * (pltpu.roll(value, 7, 0) - value)
                + west * (pltpu.roll(value, 1, 1) - value)
                + east * (pltpu.roll(value, 5 * LANES - 1, 1) - value)
                + MIXING * (pltpu.roll(value, 4, 0) - value)
            ) * (1.0 / RATIO)
            both = jnp.where(is_value, value, pltpu.roll(change, 2, 0))
            for k in range(RATIO):
                rows_out[k, f, :, 0:COLS] = both[:, LANES * k : LANES * k + COLS]

        stacked = rows_out[:, :, :, 0:COLS].reshape(RATIO * FIELDS * 8, COLS)

        @pl.loop(0, WIDE // LANES)
        def _(k):
            column = iota((COLS, LANES), 1) + LANES * k
            column = jnp.where(column < 448, column, column - WIDE)
            ahead = column - RATIO * (iota((COLS, LANES), 0) - LANES)
            widen = jnp.where((ahead >= 0) & (ahead < RATIO), 1.0, 0.0).astype(jnp.bfloat16)
            lanes = pl.ds(pl.multiple_of(LANES * k, LANES), LANES)
            rows_out[:, :, :, lanes] = dot_ones(stacked, widen).reshape(RATIO, FIELDS, 8, LANES)

        @pl.loop(0, RATIO)
        def _(k):
            pl.semaphore_wait(rows_ready.at[k], 1)
            rows_copy(k).start()
    row = iota((TALL, WIDE), 0)
    col = iota((TALL, WIDE), 1)
    row = tile * ROWS + jnp.where(row < 28, row, row - TALL)
    col = pick(is_parent, section, nest) * COLS + jnp.where(col < 448, col, col - WIDE)
    last_row = tiles * ROWS - 1
    last_col = pick(is_parent, 2, 6) * COLS - 1
    depth = jnp.minimum(jnp.minimum(row, last_row - row), jnp.minimum(col, last_col - col))
    strength = pick(is_parent, 0.0, 1.0 / ZONE)
    mixed[0] = jnp.clip(ZONE - depth, 0, ZONE).astype(jnp.float32) * strength

    for_near(lambda copy: copy.wait_recv(), has_right, has_left)

    half = iota((8, LANES), 0) < 4
    beside = []
    for side in range(2):
        corner = jnp.where(half, near_strips[side, 24:32, :], near_strips[side, 32:40, :])
        beside.append(jnp.concatenate([near_strips[side, 0:24, :], corner], axis=0))
    from_right = iota((TALL, LANES), 1) < 64

    @pl.loop(0, PAIRS + 4)
    def _(i):
        g = i + jnp.where(i >= PAIRS + 2, PAIRS - 2, 0)
        right_part = pltpu.roll(beside[0], lax.rem(LANES - 3 * g, LANES), 1)
        left_part = pltpu.roll(beside[1], LANES - 3 * g - 3, 1)
        side_columns[i] = jnp.where(from_right, right_part, left_part)

    def whole(own, plane, l, sides):
        below, above = near_slabs[0, plane], near_slabs[1, plane]
        below = jnp.where(l == 0, below, pltpu.roll(below, 4, 0))
        above = jnp.where(l == 0, pltpu.roll(above, 4, 0), above)
        tall = jnp.concatenate([own, jnp.where(upper, below, above)], axis=0)
        return jnp.concatenate([tall, sides], axis=1)

    @pl.loop(0, LEVELS)
    def _(l):
        keep = 1.0 - mixed[0]
        speed_y, speed_x = (
            whole(courant[d, l], FIELDS + d, l, side_columns[PAIRS + 2 * d + l]) for d in range(2)
        )
        south = jnp.where(row == 0, 0.0, jnp.maximum(speed_y, 0.0) + DIFFUSION) * keep
        north = jnp.where(row == last_row, 0.0, DIFFUSION - jnp.minimum(speed_y, 0.0)) * keep
        west = jnp.where(col == 0, 0.0, jnp.maximum(speed_x, 0.0) + DIFFUSION) * keep
        east = jnp.where(col == last_col, 0.0, DIFFUSION - jnp.minimum(speed_x, 0.0)) * keep
        coef[l, 0] = (1.0 - MIXING) * keep - south - north - west - east
        coef[l, 1] = south
        coef[l, 2] = north
        coef[l, 3] = west
        coef[l, 4] = east
        mixed[1] = MIXING * keep

    @pl.when(rim_column)
    def _():
        pltpu.make_async_copy(spread, spread_in, spread_recv).wait()
        column = iota((TALL, LANES), 1)
        block = pl.ds(pl.multiple_of(pick(section == 2, 0, COLS - LANES), LANES), LANES)
        share = mixed[0, :, block]

        @pl.loop(0, PAIRS)
        def _(pair):
            for which, target in ((0, force), (1, slope)):
                turned = pltpu.roll(spread_in[which], lax.rem(LANES - 3 * pair, LANES), 1)
                lead, middle, trail = (
                    jnp.broadcast_to(turned[:, c : c + 1], (TALL, LANES)) for c in range(3)
                )
                filled = jnp.where(column < 3, lead, jnp.where(column < 125, middle, trail))
                target[pair, :, block] = share * filled

    @pl.when(rim_row)
    def _():
        pltpu.make_async_copy(rows_out.at[0], rows_in, rows_recv).wait()
        sub = iota((8, WIDE), 0)
        first = sub < pick(at_top, 3, 5)
        in_zone = (sub >= pick(at_top, 0, 3)) & (sub < pick(at_top, 5, 8))
        block = pl.ds(pl.multiple_of(pick(at_top, 0, 16), 8), 8)
        share = mixed[0, block, :]

        @pl.loop(0, FIELDS)
        def _(f):
            rows = rows_in[f]
            for l in range(LEVELS):
                for target, one, two in ((force, 4 * l + 1, 4 * l + 2), (slope, 4 * l + 3, (4 * l + 4) % 8)):
                    filled = jnp.where(first, rows[one : one + 1, :], rows[two : two + 1, :])
                    old = target[LEVELS * f + l, block, :]
                    target[LEVELS * f + l, block, :] = jnp.where(in_zone, share * filled, old)

    ahead = iota((COLS, LANES), 0) - RATIO * iota((COLS, LANES), 1)
    gather = jnp.where((ahead >= 0) & (ahead < RATIO), 1.0, 0.0).astype(jnp.bfloat16)

    def for_relays(f, act, act_local):
        @pl.loop(0, 2)
        def _(late):
            target = relay_tile(group + late)

            @pl.when(target != tile)
            def _():
                act(
                    remote(
                        means.at[f], relay_in.at[f, late, inner], relay_send.at[f, late],
                        relay_recv.at[f, late, inner], (target, section),
                    )
                )

            if act_local is not None:
                @pl.when(target == tile)
                def _():
                    act_local(
                        pltpu.make_async_copy(
                            means.at[f], relay_in.at[f, late, inner], relay_recv.at[f, late, inner]
                        )
                    )

    steps = pick(is_parent, 1, RATIO)

    @pl.loop(0, FIELDS)
    def _(f):
        for l in range(LEVELS):
            work[l] = whole(state[f, l], f, l, side_columns[LEVELS * f + l])

        @pl.loop(0, steps)
        def _(k):
            fraction = (k + 1).astype(jnp.float32)
            pair = [work[l] for l in range(LEVELS)]
            mix = mixed[1]
            for l in range(LEVELS):
                value = pair[l]
                work[l] = (
                    coef[l, 0] * value
                    + coef[l, 1] * pltpu.roll(value, 1, 0)
                    + coef[l, 2] * pltpu.roll(value, TALL - 1, 0)
                    + coef[l, 3] * pltpu.roll(value, 1, 1)
                    + coef[l, 4] * pltpu.roll(value, WIDE - 1, 1)
                    + mix * pair[1 - l]
                    + (force[LEVELS * f + l] + fraction * slope[LEVELS * f + l])
                )

        for l in range(LEVELS):
            out[f, l] = work[l, :ROWS, :COLS]

        @pl.when(is_nest)
        def _():
            for l in range(LEVELS):
                for c in range(RATIO):
                    fine[c, l] = work[l, :ROWS, LANES * c : LANES * (c + 1)]
            sums = [
                sum(fine[c, :, pl.ds(k, COARSE, stride=RATIO), :] for k in range(RATIO))
                .reshape(LEVELS * COARSE, LANES)
                for c in range(RATIO)
            ]
            block = dot_ones(jnp.concatenate(sums, axis=1), gather) * (1.0 / (RATIO * RATIO))
            means[f] = block.reshape(LEVELS, COARSE, LANES)
            for_relays(f, start, start)

    def mean_copy(f):
        return remote(
            relay_out.at[f], mean_in.at[f, third], mean_send.at[f], mean_recv.at[f, third],
            (q + task, owner),
        )

    @pl.when(is_relay)
    def _():
        @pl.loop(0, FIELDS)
        def _(f):
            @pl.loop(0, 2)
            def _(late):
                @pl.when(relay_source(late))
                def _():
                    @pl.loop(0, RATIO)
                    def _(b):
                        pltpu.make_async_copy(
                            means.at[f], relay_in.at[f, late, b], relay_recv.at[f, late, b]
                        ).wait()
            for l in range(LEVELS):
                lined = jnp.concatenate(
                    [relay_in[f, late, b, l] for late in (1, 0) for b in range(RATIO)], axis=0
                )
                relay_out[f, l] = pltpu.roll(lined, rest + ROWS, 0)[:ROWS, :]
            mean_copy(f).start()

    @pl.when(under)
    def _():
        coarse_row = ROWS * (tile - q) - rest + iota((ROWS, COLS), 0)
        covered = (coarse_row >= 0) & (coarse_row < ROWS * groups)

        @pl.loop(0, FIELDS)
        def _(f):
            for c in range(RATIO):
                pltpu.make_async_copy(relay_out.at[f], mean_in.at[f, c], mean_recv.at[f, c]).wait()
            for l in range(LEVELS):
                fed = jnp.concatenate([mean_in[f, c, l] for c in range(RATIO)], axis=1)
                out[f, l] = jnp.where(covered, fed, out[f, l])

    for_near(wait_send, has_left, has_right)
    for_windows(wait_send, None)
    for_edges(wait_send, None)

    @pl.when(is_parent)
    def _():
        spread_copy().wait_send()

    @pl.when(row_relay)
    def _():
        @pl.loop(0, RATIO)
        def _(k):
            rows_copy(k).wait_send()

    @pl.when(is_nest)
    def _():
        @pl.loop(0, FIELDS)
        def _(f):
            for_relays(f, wait_send, None)

    @pl.when(is_relay)
    def _():
        @pl.loop(0, FIELDS)
        def _(f):
            mean_copy(f).wait_send()


def solution(mesh):
    tiles = mesh.shape["tile"]
    sections = mesh.shape["section"]
    choices = max(tiles // 6 - 1, 4) - 1
    vmem = pl.BlockSpec(memory_space=pltpu.VMEM)
    anywhere = pl.BlockSpec(memory_space=pl.ANY)

    def call(q, state, courant, nest_offset):
        def space(*shape):
            return pltpu.VMEM(shape, jnp.float32)

        def copies(*shape):
            return pltpu.SemaphoreType.DMA(shape)

        return pl.pallas_call(
            functools.partial(kernel, q, tiles, sections),
            out_shape=jax.ShapeDtypeStruct(state.shape, state.dtype),
            in_specs=[pl.BlockSpec(memory_space=pltpu.SMEM), anywhere, anywhere],
            out_specs=vmem,
            scratch_shapes=[
                space(FIELDS, LEVELS, ROWS, COLS),
                space(2, LEVELS, ROWS, COLS),
                space(2, ROWS, LANES),
                space(2, ROWS + 16, LANES),
                space(2, PLANES, 8, COLS),
                space(2, PLANES, 8, COLS),
                space(PAIRS + 4, TALL, LANES),
                space(4, ROWS, LANES),
                space(2, TALL, LANES),
                space(2, TALL, LANES),
                space(3, PLANES, 8, LANES),
                space(3, 5, PLANES, 8, LANES),
                space(RATIO, FIELDS, 8, WIDE),
                space(FIELDS, 8, WIDE),
                space(LEVELS, 5, TALL, WIDE),
                space(2, TALL, WIDE),
                space(PAIRS, TALL, WIDE),
                space(PAIRS, TALL, WIDE),
                space(LEVELS, TALL, WIDE),
                space(RATIO, LEVELS, ROWS, LANES),
                space(FIELDS, LEVELS, COARSE, LANES),
                space(FIELDS, 2, RATIO, LEVELS, COARSE, LANES),
                space(FIELDS, LEVELS, ROWS, LANES),
                space(FIELDS, RATIO, LEVELS, ROWS, LANES),
                copies(2), copies(8), copies(8), copies(4, RATIO), copies(4), copies(2), copies(3, 2),
                pltpu.SemaphoreType.DMA, pltpu.SemaphoreType.DMA, copies(RATIO), pltpu.SemaphoreType.DMA,
                pltpu.SemaphoreType.REGULAR, pltpu.SemaphoreType.REGULAR((RATIO,)),
                copies(FIELDS, 2), copies(FIELDS, 2, RATIO), copies(FIELDS), copies(FIELDS, RATIO),
            ],
            compiler_params=pltpu.CompilerParams(collective_id=q, has_side_effects=True),
            name=f"nested_step_{q}",
        )(nest_offset, state, courant)

    def on_device(state, courant, nest_offset):
        branches = [functools.partial(call, q) for q in range(1, choices + 1)]
        choice = jnp.clip(nest_offset[0] // ROWS - 1, 0, choices - 1)
        return lax.switch(choice, branches, state, courant, nest_offset)

    return jax.shard_map(
        on_device,
        mesh=mesh,
        in_specs=(P(None, None, "tile", "section"), P(None, None, "tile", "section"), P()),
        out_specs=P(None, None, "tile", "section"),
        check_vma=False,
    )
```

```python
import functools

import jax
import jax.numpy as jnp
from jax import lax
from jax.experimental import pallas as pl
from jax.experimental.pallas import tpu as pltpu
from jax.sharding import PartitionSpec as P

RATIO = 3
ZONE = 5
DIFFUSION = 0.02
MIXING = 0.05
FIELDS = 5
LEVELS = 2
ROWS = 24
COLS = 384
LANES = 128
COARSE = ROWS // RATIO
TALL = 32
WIDE = 512
PAIRS = FIELDS * LEVELS
PLANES = FIELDS + 2
MESH = pl.DeviceIdType.MESH

NEAR = ((-1, 0), (1, 0), (0, -1), (-1, -1), (1, -1), (0, 1), (-1, 1), (1, 1))


def iota(shape, dim):
    return lax.broadcasted_iota(jnp.int32, shape, dim)


def pick(flag, one, other):
    return jnp.where(flag, one, other)


def thirds(value):
    high = value.astype(jnp.bfloat16)
    rest = value - high.astype(jnp.float32)
    middle = rest.astype(jnp.bfloat16)
    low = (rest - middle.astype(jnp.float32)).astype(jnp.bfloat16)
    return [high, middle, low]


def dot_ones(value, ones):
    rows = value.shape[0]
    parts = jnp.dot(jnp.concatenate(thirds(value), axis=0), ones, preferred_element_type=jnp.float32)
    return parts[:rows] + parts[rows : 2 * rows] + parts[2 * rows :]


def kernel(
    q, tiles, sections,
    offset_ref, state_in, courant_in, out,
    state, courant, strips, near_strips, slabs, near_slabs, side_columns,
    edge_in, spread, spread_in, stage, window_in, rows_out, rows_in,
    coef, mixed, force, slope, work,
    fine, means, relay_in, relay_out, mean_in,
    load_sem, near_send, near_recv, edge_send, edge_recv, window_send, window_recv,
    spread_send, spread_recv, rows_send, rows_recv, edge_ready, rows_ready,
    relay_send, relay_recv, mean_send, mean_recv,
):
    tile = lax.axis_index("tile")
    section = lax.axis_index("section")
    groups = tiles // RATIO
    is_parent = section < 2
    is_nest = section >= 2
    nest = section - 2
    group = tile // RATIO
    inner = tile - group * RATIO
    rest = offset_ref[0] - q * ROWS
    rim_column = (section == 2) | (section == sections - 1)
    at_top = tile == 0
    at_end = at_top | (tile == tiles - 1)
    rim_row = is_nest & at_end
    top_relay = tile == (RATIO - 1) * groups
    row_relay = is_parent & (top_relay | (tile == tiles - 1))
    rows_tile = pick(at_top, (RATIO - 1) * groups, tiles - 1)
    rows_to = pick(top_relay, 0, tiles - 1)
    has_left = (section != 0) & (section != 2)
    has_right = (section != 1) & (section != sections - 1)
    low_window = is_parent & (tile >= q - 1) & (tile <= q + 1)
    high_window = is_parent & (tile >= q + groups - 1) & (tile <= q + groups)
    in_window = low_window | high_window
    window_to = pick(low_window, (RATIO - 1) * groups, tiles - 1)
    window_slot = pick(low_window, tile - q + 1, tile - q - groups + 1)
    window_first = pick(top_relay, q - 1, q + groups - 1)
    window_count = pick(top_relay, 3, 2)
    under = is_parent & (tile >= q) & (tile <= q + groups)
    third = lax.rem(lax.max(nest, 0), RATIO)
    owner = lax.max(nest, 0) // RATIO

    def relay_tile(a):
        return lax.min(a, groups - 1) * RATIO // groups * groups + lax.rem(q + a, groups)

    turn = lax.rem(tile - q + tiles, groups)
    wrapped = (turn == 0) & (tile // groups == RATIO - 1)
    task = pick(wrapped, groups, turn)
    is_relay = is_nest & (relay_tile(task) == tile)

    def near_peer(step):
        return lax.rem(tile + step[0] + tiles, tiles), section + step[1]

    loads = [
        pltpu.make_async_copy(state_in, state, load_sem.at[0]),
        pltpu.make_async_copy(courant_in, courant, load_sem.at[1]),
    ]
    for load in loads:
        load.start()

    @pl.when(row_relay)
    def _():
        @pl.loop(0, 3)
        def _(u):
            @pl.loop(0, 5)
            def _(slot):
                window_in[u, slot] = jnp.zeros((PLANES, 8, LANES), jnp.float32)

    near_strips[...] = jnp.zeros_like(near_strips)

    barrier = pltpu.get_barrier_semaphore()

    def greet(tile_to, section_to):
        pl.semaphore_signal(
            barrier, inc=1, device_id=(tile_to, section_to), device_id_type=MESH
        )

    rim_section = pick(section == 0, sections - 1, 2)

    @pl.when(is_parent)
    def _():
        greet(tile, rim_section)

        @pl.loop(0, 4)
        def _(d):
            greet(q + group + d - 1, 1 - section)

    @pl.when(row_relay)
    def _():
        @pl.loop(0, RATIO)
        def _(k):
            greet(rows_to, 2 + RATIO * section + k)

        @pl.loop(0, window_count)
        def _(u):
            greet(window_first + u, 0)
            greet(window_first + u, 1)

    for step in NEAR[:2]:
        greet(*near_peer(step))

    @pl.when(has_left)
    def _():
        for step in NEAR[2:5]:
            greet(*near_peer(step))

    @pl.when(has_right)
    def _():
        for step in NEAR[5:]:
            greet(*near_peer(step))

    def relay_source(late):
        return (task - late >= 0) & (task - late < groups)

    @pl.when(is_relay)
    def _():
        @pl.loop(0, 2)
        def _(late):
            @pl.when(relay_source(late))
            def _():
                @pl.loop(0, RATIO)
                def _(b):
                    source = (task - late) * RATIO + b

                    @pl.when(source != tile)
                    def _():
                        greet(source, section)

    @pl.when(under)
    def _():
        @pl.loop(0, RATIO)
        def _(third):
            greet(relay_tile(tile - q), 2 + RATIO * section + third)

    @pl.loop(0, PAIRS)
    def _(pair):
        force[pair] = jnp.zeros((TALL, WIDE), jnp.float32)
        slope[pair] = jnp.zeros((TALL, WIDE), jnp.float32)

    for load in loads:
        load.wait()

    upper = iota((8, COLS), 0) < 4

    def pack_rows(plane, first, second):
        slabs[0, plane] = jnp.where(upper, first[0:8, :], pltpu.roll(second[0:8, :], 4, 0))
        slabs[1, plane] = jnp.where(upper, pltpu.roll(first[16:24, :], 4, 0), second[16:24, :])

    @pl.loop(0, FIELDS)
    def _(f):
        pack_rows(f, state[f, 0], state[f, 1])

    @pl.loop(0, 2)
    def _(d):
        pack_rows(FIELDS + d, courant[d, 0], courant[d, 1])

    lane = iota((ROWS, LANES), 1)

    def pack_columns(f, packed):
        left, right = packed
        for l in range(LEVELS):
            for kind in range(3):
                g = PAIRS * kind + LEVELS * f + l
                source = state.at[f, l] if kind == 0 else courant.at[kind - 1, l]
                here = (lane >= 3 * g) & (lane < 3 * g + 3)
                left = jnp.where(here, pltpu.roll(source[:, :LANES], 3 * g, 1), left)
                right = jnp.where(here, pltpu.roll(source[:, COLS - LANES :], 3 * g + 3, 1), right)
        return left, right

    blank = jnp.zeros((ROWS, LANES), jnp.float32)
    left, right = lax.fori_loop(0, FIELDS, pack_columns, (blank, blank))
    strips[0] = left
    strips[1] = right

    @pl.when(in_window)
    def _():
        start = rest + pick(low_window, -1 - ROWS * (tile - q), 21 - ROWS * (tile - q - groups + 1))
        sub = iota((8, COLS), 0)

        def window_rows(plane, source):
            value = jnp.zeros((8, COLS), jnp.float32)
            for l in range(LEVELS):
                for j in range(4):
                    row = start + j
                    owned = (row >= 0) & (row < ROWS)
                    line = source(l)[pl.ds(jnp.clip(row, 0, ROWS - 1), 1), :] * jnp.where(owned, 1.0, 0.0)
                    value = jnp.where(sub == 4 * l + j, line, value)
            for k in range(3):
                stage[k, plane] = value[:, LANES * k : LANES * (k + 1)]

        @pl.loop(0, FIELDS)
        def _(f):
            window_rows(f, lambda l: state.at[f, l])

        @pl.loop(0, 2)
        def _(d):
            window_rows(FIELDS + d, lambda l: courant.at[d, l])

    edge_targets = sum(
        jnp.where((tile - q + 1 - d >= 0) & (tile - q + 1 - d < groups), RATIO, 0) for d in range(4)
    )
    window_targets = jnp.where(in_window, 2, 0)
    relay_targets = (
        sum(jnp.where(relay_tile(group + late) != tile, 1, 0) for late in range(2))
        + jnp.where(is_relay, 1, 0)
        + jnp.where(rim_column, 1, 0)
        + jnp.where(rim_row, 1, 0)
    )
    near_targets = 2 + jnp.where(has_left, 3, 0) + jnp.where(has_right, 3, 0)
    waited = near_targets + pick(is_parent, edge_targets + window_targets, relay_targets)
    pl.semaphore_wait(barrier, waited)

    @pl.when(rim_column)
    def _():
        pl.semaphore_signal(
            edge_ready, inc=1, device_id=(tile, pick(section == 2, 1, 0)), device_id_type=MESH
        )

    @pl.when(rim_row)
    def _():
        pl.semaphore_signal(rows_ready.at[third], inc=1, device_id=(rows_tile, owner), device_id_type=MESH)

    def remote(source, target, send, recv, device):
        return pltpu.make_async_remote_copy(
            src_ref=source, dst_ref=target, send_sem=send, recv_sem=recv,
            device_id=device, device_id_type=MESH,
        )

    def whole_wait(source, semaphore):
        pltpu.make_async_copy(source, source, semaphore).wait()

    @pl.when(in_window)
    def _():
        remote(
            stage, window_in.at[window_slot, 1:4], window_send, window_recv, (window_to, section)
        ).start()
        remote(
            stage.at[pick(section == 0, 2, 0)], window_in.at[window_slot, pick(section == 0, 0, 4)],
            window_send, window_recv, (window_to, 1 - section),
        ).start()

    def for_edges(act):
        @pl.when(is_parent)
        def _():
            @pl.loop(0, 4)
            def _(d):
                aim = tile - q + 1 - d

                @pl.when((aim >= 0) & (aim < groups))
                def _():
                    act(d, aim)

    def send_edges(d, aim):
        @pl.loop(0, RATIO)
        def _(b):
            remote(
                strips.at[section], edge_in.at[d], edge_send.at[d], edge_recv, (aim * RATIO + b, 1 - section)
            ).start()

    for_edges(send_edges)

    def near_copy(i):
        source, target = (
            (slabs.at[0], near_slabs.at[0]),
            (slabs.at[1], near_slabs.at[1]),
            (strips.at[0], near_strips.at[0, 0:24]),
            (strips.at[0, 0:8], near_strips.at[0, 24:32]),
            (strips.at[0, 16:24], near_strips.at[0, 32:40]),
            (strips.at[1], near_strips.at[1, 0:24]),
            (strips.at[1, 0:8], near_strips.at[1, 24:32]),
            (strips.at[1, 16:24], near_strips.at[1, 32:40]),
        )[i]
        kind = (0, 0, 1, 1, 1, 2, 2, 2)[i]
        return remote(source, target, near_send.at[kind], near_recv.at[kind], near_peer(NEAR[i]))

    @pl.when(has_left)
    def _():
        for i in (2, 3, 4):
            near_copy(i).start()

    @pl.when(has_right)
    def _():
        for i in (5, 6, 7):
            near_copy(i).start()

    for i in (0, 1):
        near_copy(i).start()

    def near_wait(semaphores, first_exists, second_exists):
        @pl.when(first_exists)
        def _():
            whole_wait(near_strips.at[0], semaphores.at[1])

        @pl.when(second_exists)
        def _():
            whole_wait(near_strips.at[1], semaphores.at[2])

        whole_wait(near_slabs, semaphores.at[0])

    def spread_copy():
        return remote(spread, spread_in, spread_send, spread_recv, (tile, rim_section))

    def rows_copy(k):
        return remote(
            rows_out.at[k], rows_in, rows_send, rows_recv, (rows_to, 2 + RATIO * section + k)
        )

    @pl.when(is_parent)
    def _():
        whole_wait(edge_in, edge_recv)
        shape = (4 * ROWS, LANES)
        value = edge_in[...].reshape(shape)
        speed_y = pltpu.roll(value, LANES - 3 * PAIRS, 1)
        speed_x = pltpu.roll(value, LANES - 6 * PAIRS, 1)
        place = iota(shape, 1)
        trio = (place * 171) >> 9
        within = place - 3 * trio
        partner = jnp.where((trio & 1) == 0, pltpu.roll(value, LANES - 3, 1), pltpu.roll(value, 3, 1))
        change = (
            (jnp.maximum(speed_y, 0.0) + DIFFUSION) * (pltpu.roll(value, 1, 0) - value)
            + (DIFFUSION - jnp.minimum(speed_y, 0.0)) * (pltpu.roll(value, 4 * ROWS - 1, 0) - value)
            + jnp.where(within == 0, 0.0, jnp.maximum(speed_x, 0.0) + DIFFUSION) * (pltpu.roll(value, 1, 1) - value)
            + jnp.where(within == 2, 0.0, DIFFUSION - jnp.minimum(speed_x, 0.0))
            * (pltpu.roll(value, LANES - 1, 1) - value)
            + MIXING * (partner - value)
        ) * (1.0 / RATIO)
        wide = (TALL, 12 * ROWS)
        tall_row = iota(wide, 0)
        tall_row = jnp.where(tall_row < 28, tall_row, tall_row - TALL) + RATIO
        wanted = ((tall_row * 171) >> 9) - 1 + (ROWS + rest + COARSE * inner)
        source = iota(wide, 1)
        select = (source == wanted) | (source == wanted + 4 * ROWS) | (source == wanted + 8 * ROWS)
        both = jnp.concatenate([value, change], axis=1)
        rows = jnp.dot(
            jnp.where(select, 1.0, 0.0).astype(jnp.bfloat16),
            jnp.concatenate(thirds(both), axis=0),
            preferred_element_type=jnp.float32,
        )
        spread[0] = rows[:, :LANES]
        spread[1] = rows[:, LANES:]
        pl.semaphore_wait(edge_ready, 1)
        spread_copy().start()

    @pl.when(row_relay)
    def _():
        @pl.when(top_relay)
        def _():
            whole_wait(window_in.at[:, 0:4], window_recv)

        @pl.when(jnp.logical_not(top_relay))
        def _():
            whole_wait(window_in.at[0:2, 0:4], window_recv)

        def window(plane):
            return jnp.concatenate([sum(window_in[u, k, plane] for u in range(3)) for k in range(5)], axis=1)

        shape = (8, 5 * LANES)
        speed_y, speed_x = window(FIELDS), window(FIELDS + 1)
        parent_col = iota(shape, 1) + (COLS * section - LANES)
        south = jnp.maximum(speed_y, 0.0) + DIFFUSION
        north = DIFFUSION - jnp.minimum(speed_y, 0.0)
        west = jnp.where(parent_col == 0, 0.0, jnp.maximum(speed_x, 0.0) + DIFFUSION)
        east = jnp.where(parent_col == 2 * COLS - 1, 0.0, DIFFUSION - jnp.minimum(speed_x, 0.0))
        within = iota(shape, 0) & 3
        is_value = (within == 1) | (within == 2)

        @pl.loop(0, FIELDS)
        def _(f):
            value = window(f)
            change = (
                south * (pltpu.roll(value, 1, 0) - value)
                + north * (pltpu.roll(value, 7, 0) - value)
                + west * (pltpu.roll(value, 1, 1) - value)
                + east * (pltpu.roll(value, 5 * LANES - 1, 1) - value)
                + MIXING * (pltpu.roll(value, 4, 0) - value)
            ) * (1.0 / RATIO)
            both = jnp.where(is_value, value, pltpu.roll(change, 2, 0))
            for k in range(RATIO):
                rows_out[k, f, :, 0:COLS] = both[:, LANES * k : LANES * k + COLS]

        stacked = rows_out[:, :, :, 0:COLS].reshape(RATIO * FIELDS * 8, COLS)

        @pl.loop(0, WIDE // LANES)
        def _(k):
            column = iota((COLS, LANES), 1) + LANES * k
            column = jnp.where(column < 448, column, column - WIDE)
            ahead = column - RATIO * (iota((COLS, LANES), 0) - LANES)
            widen = jnp.where((ahead >= 0) & (ahead < RATIO), 1.0, 0.0).astype(jnp.bfloat16)
            lanes = pl.ds(pl.multiple_of(LANES * k, LANES), LANES)
            rows_out[:, :, :, lanes] = dot_ones(stacked, widen).reshape(RATIO, FIELDS, 8, LANES)

        @pl.loop(0, RATIO)
        def _(k):
            pl.semaphore_wait(rows_ready.at[k], 1)
            rows_copy(k).start()
    row = iota((TALL, WIDE), 0)
    col = iota((TALL, WIDE), 1)
    row = tile * ROWS + jnp.where(row < 28, row, row - TALL)
    col = pick(is_parent, section, nest) * COLS + jnp.where(col < 448, col, col - WIDE)
    last_row = tiles * ROWS - 1
    last_col = pick(is_parent, 2, 6) * COLS - 1
    depth = jnp.minimum(jnp.minimum(row, last_row - row), jnp.minimum(col, last_col - col))
    strength = pick(is_parent, 0.0, 1.0 / ZONE)
    mixed[0] = jnp.clip(ZONE - depth, 0, ZONE).astype(jnp.float32) * strength

    near_wait(near_recv, has_right, has_left)

    half = iota((8, LANES), 0) < 4
    beside = []
    for side in range(2):
        corner = jnp.where(half, near_strips[side, 24:32, :], near_strips[side, 32:40, :])
        beside.append(jnp.concatenate([near_strips[side, 0:24, :], corner], axis=0))
    from_right = iota((TALL, LANES), 1) < 64

    @pl.loop(0, PAIRS + 4)
    def _(i):
        g = i + jnp.where(i >= PAIRS + 2, PAIRS - 2, 0)
        right_part = pltpu.roll(beside[0], lax.rem(LANES - 3 * g, LANES), 1)
        left_part = pltpu.roll(beside[1], LANES - 3 * g - 3, 1)
        side_columns[i] = jnp.where(from_right, right_part, left_part)

    def whole(own, plane, l, sides):
        below, above = near_slabs[0, plane], near_slabs[1, plane]
        below = jnp.where(l == 0, below, pltpu.roll(below, 4, 0))
        above = jnp.where(l == 0, pltpu.roll(above, 4, 0), above)
        tall = jnp.concatenate([own, jnp.where(upper, below, above)], axis=0)
        return jnp.concatenate([tall, sides], axis=1)

    @pl.loop(0, LEVELS)
    def _(l):
        keep = 1.0 - mixed[0]
        speed_y, speed_x = (
            whole(courant[d, l], FIELDS + d, l, side_columns[PAIRS + 2 * d + l]) for d in range(2)
        )
        south = jnp.where(row == 0, 0.0, jnp.maximum(speed_y, 0.0) + DIFFUSION) * keep
        north = jnp.where(row == last_row, 0.0, DIFFUSION - jnp.minimum(speed_y, 0.0)) * keep
        west = jnp.where(col == 0, 0.0, jnp.maximum(speed_x, 0.0) + DIFFUSION) * keep
        east = jnp.where(col == last_col, 0.0, DIFFUSION - jnp.minimum(speed_x, 0.0)) * keep
        coef[l, 0] = (1.0 - MIXING) * keep - south - north - west - east
        coef[l, 1] = south
        coef[l, 2] = north
        coef[l, 3] = west
        coef[l, 4] = east
        mixed[1] = MIXING * keep

    @pl.when(rim_column)
    def _():
        pltpu.make_async_copy(spread, spread_in, spread_recv).wait()
        column = iota((TALL, LANES), 1)
        block = pl.ds(pl.multiple_of(pick(section == 2, 0, COLS - LANES), LANES), LANES)
        share = mixed[0, :, block]

        @pl.loop(0, PAIRS)
        def _(pair):
            for which, target in ((0, force), (1, slope)):
                turned = pltpu.roll(spread_in[which], lax.rem(LANES - 3 * pair, LANES), 1)
                lead, middle, trail = (
                    jnp.broadcast_to(turned[:, c : c + 1], (TALL, LANES)) for c in range(3)
                )
                filled = jnp.where(column < 3, lead, jnp.where(column < 125, middle, trail))
                target[pair, :, block] = share * filled

    @pl.when(rim_row)
    def _():
        pltpu.make_async_copy(rows_out.at[0], rows_in, rows_recv).wait()
        sub = iota((8, WIDE), 0)
        first = sub < pick(at_top, 3, 5)
        in_zone = (sub >= pick(at_top, 0, 3)) & (sub < pick(at_top, 5, 8))
        block = pl.ds(pl.multiple_of(pick(at_top, 0, 16), 8), 8)
        share = mixed[0, block, :]

        @pl.loop(0, FIELDS)
        def _(f):
            rows = rows_in[f]
            for l in range(LEVELS):
                for target, one, two in ((force, 4 * l + 1, 4 * l + 2), (slope, 4 * l + 3, (4 * l + 4) % 8)):
                    filled = jnp.where(first, rows[one : one + 1, :], rows[two : two + 1, :])
                    old = target[LEVELS * f + l, block, :]
                    target[LEVELS * f + l, block, :] = jnp.where(in_zone, share * filled, old)

    ahead = iota((COLS, LANES), 0) - RATIO * iota((COLS, LANES), 1)
    gather = jnp.where((ahead >= 0) & (ahead < RATIO), 1.0, 0.0).astype(jnp.bfloat16)

    def send_means(f):
        @pl.loop(0, 2)
        def _(late):
            target = relay_tile(group + late)

            @pl.when(target != tile)
            def _():
                remote(
                    means.at[f], relay_in.at[f, late, inner], relay_send.at[late], relay_recv.at[f],
                    (target, section),
                ).start()

            @pl.when(target == tile)
            def _():
                pltpu.make_async_copy(means.at[f], relay_in.at[f, late, inner], relay_recv.at[f]).start()

    steps = pick(is_parent, 1, RATIO)

    @pl.loop(0, FIELDS)
    def _(f):
        for l in range(LEVELS):
            work[l] = whole(state[f, l], f, l, side_columns[LEVELS * f + l])

        @pl.loop(0, steps)
        def _(k):
            fraction = (k + 1).astype(jnp.float32)
            pair = [work[l] for l in range(LEVELS)]
            mix = mixed[1]
            for l in range(LEVELS):
                value = pair[l]
                work[l] = (
                    coef[l, 0] * value
                    + coef[l, 1] * pltpu.roll(value, 1, 0)
                    + coef[l, 2] * pltpu.roll(value, TALL - 1, 0)
                    + coef[l, 3] * pltpu.roll(value, 1, 1)
                    + coef[l, 4] * pltpu.roll(value, WIDE - 1, 1)
                    + mix * pair[1 - l]
                    + (force[LEVELS * f + l] + fraction * slope[LEVELS * f + l])
                )

        for l in range(LEVELS):
            out[f, l] = work[l, :ROWS, :COLS]

        @pl.when(is_nest)
        def _():
            for l in range(LEVELS):
                for c in range(RATIO):
                    fine[c, l] = work[l, :ROWS, LANES * c : LANES * (c + 1)]
            sums = [
                sum(fine[c, :, pl.ds(k, COARSE, stride=RATIO), :] for k in range(RATIO))
                .reshape(LEVELS * COARSE, LANES)
                for c in range(RATIO)
            ]
            block = dot_ones(jnp.concatenate(sums, axis=1), gather) * (1.0 / (RATIO * RATIO))
            means[f] = block.reshape(LEVELS, COARSE, LANES)
            send_means(f)

    def mean_copy(f):
        return remote(
            relay_out.at[f], mean_in.at[f, third], mean_send, mean_recv.at[f],
            (q + task, owner),
        )

    @pl.when(is_relay)
    def _():
        @pl.loop(0, FIELDS)
        def _(f):
            full = (task >= 1) & (task < groups)

            @pl.when(full)
            def _():
                whole_wait(relay_in.at[f], relay_recv.at[f])

            @pl.when(jnp.logical_not(full))
            def _():
                whole_wait(relay_in.at[f, 0], relay_recv.at[f])

            for l in range(LEVELS):
                lined = jnp.concatenate(
                    [relay_in[f, late, b, l] for late in (1, 0) for b in range(RATIO)], axis=0
                )
                relay_out[f, l] = pltpu.roll(lined, rest + ROWS, 0)[:ROWS, :]
            mean_copy(f).start()

    @pl.when(under)
    def _():
        coarse_row = ROWS * (tile - q) - rest + iota((ROWS, COLS), 0)
        covered = (coarse_row >= 0) & (coarse_row < ROWS * groups)

        @pl.loop(0, FIELDS)
        def _(f):
            whole_wait(mean_in.at[f], mean_recv.at[f])
            for l in range(LEVELS):
                fed = jnp.concatenate([mean_in[f, c, l] for c in range(RATIO)], axis=1)
                out[f, l] = jnp.where(covered, fed, out[f, l])

    near_wait(near_send, has_left, has_right)

    @pl.when(in_window)
    def _():
        whole_wait(window_in.at[0, 0:4], window_send)

    for_edges(lambda d, aim: whole_wait(edge_in.at[0:RATIO], edge_send.at[d]))

    @pl.when(is_parent)
    def _():
        spread_copy().wait_send()

    @pl.when(row_relay)
    def _():
        whole_wait(rows_out, rows_send)

    @pl.when(is_nest)
    def _():
        @pl.loop(0, 2)
        def _(late):
            @pl.when(relay_tile(group + late) != tile)
            def _():
                whole_wait(means, relay_send.at[late])

    @pl.when(is_relay)
    def _():
        whole_wait(relay_out, mean_send)


def solution(mesh):
    tiles = mesh.shape["tile"]
    sections = mesh.shape["section"]
    choices = max(tiles // 6 - 1, 4) - 1
    vmem = pl.BlockSpec(memory_space=pltpu.VMEM)
    anywhere = pl.BlockSpec(memory_space=pl.ANY)

    def call(q, state, courant, nest_offset):
        def space(*shape):
            return pltpu.VMEM(shape, jnp.float32)

        def copies(*shape):
            return pltpu.SemaphoreType.DMA(shape)

        one = pltpu.SemaphoreType.DMA
        return pl.pallas_call(
            functools.partial(kernel, q, tiles, sections),
            out_shape=jax.ShapeDtypeStruct(state.shape, state.dtype),
            in_specs=[pl.BlockSpec(memory_space=pltpu.SMEM), anywhere, anywhere],
            out_specs=vmem,
            scratch_shapes=[
                space(FIELDS, LEVELS, ROWS, COLS),
                space(2, LEVELS, ROWS, COLS),
                space(2, ROWS, LANES),
                space(2, ROWS + 16, LANES),
                space(2, PLANES, 8, COLS),
                space(2, PLANES, 8, COLS),
                space(PAIRS + 4, TALL, LANES),
                space(4, ROWS, LANES),
                space(2, TALL, LANES),
                space(2, TALL, LANES),
                space(3, PLANES, 8, LANES),
                space(3, 5, PLANES, 8, LANES),
                space(RATIO, FIELDS, 8, WIDE),
                space(FIELDS, 8, WIDE),
                space(LEVELS, 5, TALL, WIDE),
                space(2, TALL, WIDE),
                space(PAIRS, TALL, WIDE),
                space(PAIRS, TALL, WIDE),
                space(LEVELS, TALL, WIDE),
                space(RATIO, LEVELS, ROWS, LANES),
                space(FIELDS, LEVELS, COARSE, LANES),
                space(FIELDS, 2, RATIO, LEVELS, COARSE, LANES),
                space(FIELDS, LEVELS, ROWS, LANES),
                space(FIELDS, RATIO, LEVELS, ROWS, LANES),
                copies(2), copies(3), copies(3), copies(4), one, one, one,
                one, one, one, one, pltpu.SemaphoreType.REGULAR, pltpu.SemaphoreType.REGULAR((RATIO,)),
                copies(2), copies(FIELDS), one, copies(FIELDS),
            ],
            compiler_params=pltpu.CompilerParams(collective_id=q, has_side_effects=True),
            name=f"nested_step_{q}",
        )(nest_offset, state, courant)

    def on_device(state, courant, nest_offset):
        branches = [functools.partial(call, q) for q in range(1, choices + 1)]
        choice = jnp.clip(nest_offset[0] // ROWS - 1, 0, choices - 1)
        return lax.switch(choice, branches, state, courant, nest_offset)

    return jax.shard_map(
        on_device,
        mesh=mesh,
        in_specs=(P(None, None, "tile", "section"), P(None, None, "tile", "section"), P()),
        out_specs=P(None, None, "tile", "section"),
        check_vma=False,
    )
```

```python
import functools

import jax
import jax.numpy as jnp
from jax import lax
from jax.experimental import pallas as pl
from jax.experimental.pallas import tpu as pltpu
from jax.sharding import PartitionSpec as P

RATIO = 3
ZONE = 5
DIFFUSION = 0.02
MIXING = 0.05
FIELDS = 5
LEVELS = 2
ROWS = 24
COLS = 384
LANES = 128
COARSE = ROWS // RATIO
TALL = 32
WIDE = 512
PAIRS = FIELDS * LEVELS
PLANES = FIELDS + 2
MESH = pl.DeviceIdType.MESH

NEAR = ((-1, 0), (1, 0), (0, -1), (-1, -1), (1, -1), (0, 1), (-1, 1), (1, 1))


def iota(shape, dim):
    return lax.broadcasted_iota(jnp.int32, shape, dim)


def pick(flag, one, other):
    return jnp.where(flag, one, other)


def thirds(value):
    high = value.astype(jnp.bfloat16)
    rest = value - high.astype(jnp.float32)
    middle = rest.astype(jnp.bfloat16)
    low = (rest - middle.astype(jnp.float32)).astype(jnp.bfloat16)
    return [high, middle, low]


def dot_ones(value, ones):
    rows = value.shape[0]
    parts = jnp.dot(jnp.concatenate(thirds(value), axis=0), ones, preferred_element_type=jnp.float32)
    return parts[:rows] + parts[rows : 2 * rows] + parts[2 * rows :]


def kernel(
    q, tiles, sections,
    offset_ref, state_in, courant_in, out,
    state, courant, strips, near_strips, slabs, near_slabs, side_columns,
    edge_in, spread, spread_in, stage, window_in, rows_out, rows_in,
    coef, mixed, force, slope, work,
    fine, means, relay_in, relay_out, mean_in,
    load_sem, near_send, near_recv, edge_send, edge_recv, window_send, window_recv,
    spread_send, spread_recv, rows_send, rows_recv, edge_ready, rows_ready,
    relay_send, relay_recv, mean_send, mean_recv,
):
    tile = lax.axis_index("tile")
    section = lax.axis_index("section")
    groups = tiles // RATIO
    is_parent = section < 2
    is_nest = section >= 2
    nest = section - 2
    group = tile // RATIO
    inner = tile - group * RATIO
    rest = offset_ref[0] - q * ROWS
    rim_column = (section == 2) | (section == sections - 1)
    at_top = tile == 0
    at_end = at_top | (tile == tiles - 1)
    rim_row = is_nest & at_end
    top_relay = tile == (RATIO - 1) * groups
    row_relay = is_parent & (top_relay | (tile == groups - 1))
    rows_tile = pick(at_top, (RATIO - 1) * groups, groups - 1)
    rows_to = pick(top_relay, 0, tiles - 1)
    has_left = (section != 0) & (section != 2)
    has_right = (section != 1) & (section != sections - 1)
    low_window = is_parent & (tile >= q - 1) & (tile <= q + 1)
    high_window = is_parent & (tile >= q + groups - 1) & (tile <= q + groups)
    in_window = low_window | high_window
    window_to = pick(low_window, (RATIO - 1) * groups, groups - 1)
    window_slot = pick(low_window, tile - q + 1, tile - q - groups + 1)
    window_first = pick(top_relay, q - 1, q + groups - 1)
    window_count = pick(top_relay, 3, 2)
    under = is_parent & (tile >= q) & (tile <= q + groups)
    third = lax.rem(lax.max(nest, 0), RATIO)
    owner = lax.max(nest, 0) // RATIO

    middle = (section == 4) | (section == 5)

    def relay_tile(a, middle):
        plane = lax.min(a, groups - 1) * RATIO // groups
        plane = pick(middle & (a == 0), 1, pick(middle & (a == groups), 0, plane))
        return plane * groups + lax.rem(q + a, groups)

    turn = lax.rem(tile - q + tiles, groups)
    wrapped = (turn == 0) & (tile // groups == pick(middle, 0, RATIO - 1))
    task = pick(wrapped, groups, turn)
    is_relay = is_nest & (relay_tile(task, middle) == tile)

    def near_peer(step):
        return lax.rem(tile + step[0] + tiles, tiles), section + step[1]

    loads = [
        pltpu.make_async_copy(state_in, state, load_sem.at[0]),
        pltpu.make_async_copy(courant_in, courant, load_sem.at[1]),
    ]
    for load in loads:
        load.start()

    @pl.when(row_relay)
    def _():
        @pl.loop(0, 3)
        def _(u):
            @pl.loop(0, 5)
            def _(slot):
                window_in[u, slot] = jnp.zeros((PLANES, 8, LANES), jnp.float32)

    near_strips[...] = jnp.zeros_like(near_strips)

    barrier = pltpu.get_barrier_semaphore()

    def greet(tile_to, section_to):
        pl.semaphore_signal(
            barrier, inc=1, device_id=(tile_to, section_to), device_id_type=MESH
        )

    rim_section = pick(section == 0, sections - 1, 2)

    @pl.when(is_parent)
    def _():
        greet(tile, rim_section)

        @pl.loop(0, 4)
        def _(d):
            greet(q + group + d - 1, 1 - section)

    @pl.when(row_relay)
    def _():
        @pl.loop(0, RATIO)
        def _(k):
            greet(rows_to, 2 + RATIO * section + k)

        @pl.loop(0, window_count)
        def _(u):
            greet(window_first + u, 0)
            greet(window_first + u, 1)

    for step in NEAR[:2]:
        greet(*near_peer(step))

    @pl.when(has_left)
    def _():
        for step in NEAR[2:5]:
            greet(*near_peer(step))

    @pl.when(has_right)
    def _():
        for step in NEAR[5:]:
            greet(*near_peer(step))

    def relay_source(late):
        return (task - late >= 0) & (task - late < groups)

    @pl.when(is_relay)
    def _():
        @pl.loop(0, 2)
        def _(late):
            @pl.when(relay_source(late))
            def _():
                @pl.loop(0, RATIO)
                def _(b):
                    source = (task - late) * RATIO + b

                    @pl.when(source != tile)
                    def _():
                        greet(source, section)

    @pl.when(under)
    def _():
        @pl.loop(0, RATIO)
        def _(third):
            mate = 2 + RATIO * section + third
            greet(relay_tile(tile - q, (mate == 4) | (mate == 5)), mate)

    @pl.loop(0, PAIRS)
    def _(pair):
        force[pair] = jnp.zeros((TALL, WIDE), jnp.float32)
        slope[pair] = jnp.zeros((TALL, WIDE), jnp.float32)

    for load in loads:
        load.wait()

    upper = iota((8, COLS), 0) < 4

    def pack_rows(plane, first, second):
        slabs[0, plane] = jnp.where(upper, first[0:8, :], pltpu.roll(second[0:8, :], 4, 0))
        slabs[1, plane] = jnp.where(upper, pltpu.roll(first[16:24, :], 4, 0), second[16:24, :])

    @pl.loop(0, FIELDS)
    def _(f):
        pack_rows(f, state[f, 0], state[f, 1])

    @pl.loop(0, 2)
    def _(d):
        pack_rows(FIELDS + d, courant[d, 0], courant[d, 1])

    lane = iota((ROWS, LANES), 1)

    def pack_columns(f, packed):
        left, right = packed
        for l in range(LEVELS):
            for kind in range(3):
                g = PAIRS * kind + LEVELS * f + l
                source = state.at[f, l] if kind == 0 else courant.at[kind - 1, l]
                here = (lane >= 3 * g) & (lane < 3 * g + 3)
                left = jnp.where(here, pltpu.roll(source[:, :LANES], 3 * g, 1), left)
                right = jnp.where(here, pltpu.roll(source[:, COLS - LANES :], 3 * g + 3, 1), right)
        return left, right

    blank = jnp.zeros((ROWS, LANES), jnp.float32)
    left, right = lax.fori_loop(0, FIELDS, pack_columns, (blank, blank))
    strips[0] = left
    strips[1] = right

    @pl.when(in_window)
    def _():
        start = rest + pick(low_window, -1 - ROWS * (tile - q), 21 - ROWS * (tile - q - groups + 1))
        sub = iota((8, COLS), 0)

        def window_rows(plane, source):
            value = jnp.zeros((8, COLS), jnp.float32)
            for l in range(LEVELS):
                for j in range(4):
                    row = start + j
                    owned = (row >= 0) & (row < ROWS)
                    line = source(l)[pl.ds(jnp.clip(row, 0, ROWS - 1), 1), :] * jnp.where(owned, 1.0, 0.0)
                    value = jnp.where(sub == 4 * l + j, line, value)
            for k in range(3):
                stage[k, plane] = value[:, LANES * k : LANES * (k + 1)]

        @pl.loop(0, FIELDS)
        def _(f):
            window_rows(f, lambda l: state.at[f, l])

        @pl.loop(0, 2)
        def _(d):
            window_rows(FIELDS + d, lambda l: courant.at[d, l])

    edge_targets = sum(
        jnp.where((tile - q + 1 - d >= 0) & (tile - q + 1 - d < groups), RATIO, 0) for d in range(4)
    )
    window_targets = jnp.where(in_window, 2, 0)
    relay_targets = (
        sum(jnp.where(relay_tile(group + late, middle) != tile, 1, 0) for late in range(2))
        + jnp.where(is_relay, 1, 0)
        + jnp.where(rim_column, 1, 0)
        + jnp.where(rim_row, 1, 0)
    )
    near_targets = 2 + jnp.where(has_left, 3, 0) + jnp.where(has_right, 3, 0)
    waited = near_targets + pick(is_parent, edge_targets + window_targets, relay_targets)
    pl.semaphore_wait(barrier, waited)

    @pl.when(rim_column)
    def _():
        pl.semaphore_signal(
            edge_ready, inc=1, device_id=(tile, pick(section == 2, 1, 0)), device_id_type=MESH
        )

    @pl.when(rim_row)
    def _():
        pl.semaphore_signal(rows_ready.at[third], inc=1, device_id=(rows_tile, owner), device_id_type=MESH)

    def remote(source, target, send, recv, device):
        return pltpu.make_async_remote_copy(
            src_ref=source, dst_ref=target, send_sem=send, recv_sem=recv,
            device_id=device, device_id_type=MESH,
        )

    def whole_wait(source, semaphore):
        pltpu.make_async_copy(source, source, semaphore).wait()

    @pl.when(in_window)
    def _():
        remote(
            stage, window_in.at[window_slot, 1:4], window_send, window_recv, (window_to, section)
        ).start()
        remote(
            stage.at[pick(section == 0, 2, 0)], window_in.at[window_slot, pick(section == 0, 0, 4)],
            window_send, window_recv, (window_to, 1 - section),
        ).start()

    def for_edges(act):
        @pl.when(is_parent)
        def _():
            @pl.loop(0, 4)
            def _(d):
                aim = tile - q + 1 - d

                @pl.when((aim >= 0) & (aim < groups))
                def _():
                    act(d, aim)

    def send_edges(d, aim):
        @pl.loop(0, RATIO)
        def _(b):
            remote(
                strips.at[section], edge_in.at[d], edge_send.at[d], edge_recv, (aim * RATIO + b, 1 - section)
            ).start()

    for_edges(send_edges)

    def near_copy(i):
        source, target = (
            (slabs.at[0], near_slabs.at[0]),
            (slabs.at[1], near_slabs.at[1]),
            (strips.at[0], near_strips.at[0, 0:24]),
            (strips.at[0, 0:8], near_strips.at[0, 24:32]),
            (strips.at[0, 16:24], near_strips.at[0, 32:40]),
            (strips.at[1], near_strips.at[1, 0:24]),
            (strips.at[1, 0:8], near_strips.at[1, 24:32]),
            (strips.at[1, 16:24], near_strips.at[1, 32:40]),
        )[i]
        kind = (0, 0, 1, 1, 1, 2, 2, 2)[i]
        return remote(source, target, near_send.at[kind], near_recv.at[kind], near_peer(NEAR[i]))

    @pl.when(has_left)
    def _():
        for i in (2, 3, 4):
            near_copy(i).start()

    @pl.when(has_right)
    def _():
        for i in (5, 6, 7):
            near_copy(i).start()

    for i in (0, 1):
        near_copy(i).start()

    def near_wait(semaphores, first_exists, second_exists):
        @pl.when(first_exists)
        def _():
            whole_wait(near_strips.at[0], semaphores.at[1])

        @pl.when(second_exists)
        def _():
            whole_wait(near_strips.at[1], semaphores.at[2])

        whole_wait(near_slabs, semaphores.at[0])

    def spread_copy():
        return remote(spread, spread_in, spread_send, spread_recv, (tile, rim_section))

    def rows_copy(k):
        return remote(
            rows_out.at[k], rows_in, rows_send, rows_recv, (rows_to, 2 + RATIO * section + k)
        )

    @pl.when(is_parent)
    def _():
        whole_wait(edge_in, edge_recv)
        shape = (4 * ROWS, LANES)
        value = edge_in[...].reshape(shape)
        speed_y = pltpu.roll(value, LANES - 3 * PAIRS, 1)
        speed_x = pltpu.roll(value, LANES - 6 * PAIRS, 1)
        place = iota(shape, 1)
        trio = (place * 171) >> 9
        within = place - 3 * trio
        partner = jnp.where((trio & 1) == 0, pltpu.roll(value, LANES - 3, 1), pltpu.roll(value, 3, 1))
        change = (
            (jnp.maximum(speed_y, 0.0) + DIFFUSION) * (pltpu.roll(value, 1, 0) - value)
            + (DIFFUSION - jnp.minimum(speed_y, 0.0)) * (pltpu.roll(value, 4 * ROWS - 1, 0) - value)
            + jnp.where(within == 0, 0.0, jnp.maximum(speed_x, 0.0) + DIFFUSION) * (pltpu.roll(value, 1, 1) - value)
            + jnp.where(within == 2, 0.0, DIFFUSION - jnp.minimum(speed_x, 0.0))
            * (pltpu.roll(value, LANES - 1, 1) - value)
            + MIXING * (partner - value)
        ) * (1.0 / RATIO)
        wide = (TALL, 12 * ROWS)
        tall_row = iota(wide, 0)
        tall_row = jnp.where(tall_row < 28, tall_row, tall_row - TALL) + RATIO
        wanted = ((tall_row * 171) >> 9) - 1 + (ROWS + rest + COARSE * inner)
        source = iota(wide, 1)
        select = (source == wanted) | (source == wanted + 4 * ROWS) | (source == wanted + 8 * ROWS)
        both = jnp.concatenate([value, change], axis=1)
        rows = jnp.dot(
            jnp.where(select, 1.0, 0.0).astype(jnp.bfloat16),
            jnp.concatenate(thirds(both), axis=0),
            preferred_element_type=jnp.float32,
        )
        spread[0] = rows[:, :LANES]
        spread[1] = rows[:, LANES:]
    @pl.when(row_relay)
    def _():
        @pl.when(top_relay)
        def _():
            whole_wait(window_in.at[:, 0:4], window_recv)

        @pl.when(jnp.logical_not(top_relay))
        def _():
            whole_wait(window_in.at[0:2, 0:4], window_recv)

        def window(plane):
            return jnp.concatenate([sum(window_in[u, k, plane] for u in range(3)) for k in range(5)], axis=1)

        shape = (8, 5 * LANES)
        speed_y, speed_x = window(FIELDS), window(FIELDS + 1)
        parent_col = iota(shape, 1) + (COLS * section - LANES)
        south = jnp.maximum(speed_y, 0.0) + DIFFUSION
        north = DIFFUSION - jnp.minimum(speed_y, 0.0)
        west = jnp.where(parent_col == 0, 0.0, jnp.maximum(speed_x, 0.0) + DIFFUSION)
        east = jnp.where(parent_col == 2 * COLS - 1, 0.0, DIFFUSION - jnp.minimum(speed_x, 0.0))
        within = iota(shape, 0) & 3
        is_value = (within == 1) | (within == 2)

        @pl.loop(0, FIELDS)
        def _(f):
            value = window(f)
            change = (
                south * (pltpu.roll(value, 1, 0) - value)
                + north * (pltpu.roll(value, 7, 0) - value)
                + west * (pltpu.roll(value, 1, 1) - value)
                + east * (pltpu.roll(value, 5 * LANES - 1, 1) - value)
                + MIXING * (pltpu.roll(value, 4, 0) - value)
            ) * (1.0 / RATIO)
            both = jnp.where(is_value, value, pltpu.roll(change, 2, 0))
            for k in range(RATIO):
                rows_out[k, f, :, 0:COLS] = both[:, LANES * k : LANES * k + COLS]

        stacked = rows_out[:, :, :, 0:COLS].reshape(RATIO * FIELDS * 8, COLS)

        @pl.loop(0, WIDE // LANES)
        def _(k):
            column = iota((COLS, LANES), 1) + LANES * k
            column = jnp.where(column < 448, column, column - WIDE)
            ahead = column - RATIO * (iota((COLS, LANES), 0) - LANES)
            widen = jnp.where((ahead >= 0) & (ahead < RATIO), 1.0, 0.0).astype(jnp.bfloat16)
            lanes = pl.ds(pl.multiple_of(LANES * k, LANES), LANES)
            rows_out[:, :, :, lanes] = dot_ones(stacked, widen).reshape(RATIO, FIELDS, 8, LANES)

    @pl.when(row_relay)
    def _():
        @pl.loop(0, RATIO)
        def _(k):
            pl.semaphore_wait(rows_ready.at[k], 1)
            rows_copy(k).start()

    @pl.when(is_parent)
    def _():
        pl.semaphore_wait(edge_ready, 1)
        spread_copy().start()

    row = iota((TALL, WIDE), 0)
    col = iota((TALL, WIDE), 1)
    row = tile * ROWS + jnp.where(row < 28, row, row - TALL)
    col = pick(is_parent, section, nest) * COLS + jnp.where(col < 448, col, col - WIDE)
    last_row = tiles * ROWS - 1
    last_col = pick(is_parent, 2, 6) * COLS - 1
    depth = jnp.minimum(jnp.minimum(row, last_row - row), jnp.minimum(col, last_col - col))
    strength = pick(is_parent, 0.0, 1.0 / ZONE)
    mixed[0] = jnp.clip(ZONE - depth, 0, ZONE).astype(jnp.float32) * strength

    near_wait(near_recv, has_right, has_left)

    half = iota((8, LANES), 0) < 4
    beside = []
    for side in range(2):
        corner = jnp.where(half, near_strips[side, 24:32, :], near_strips[side, 32:40, :])
        beside.append(jnp.concatenate([near_strips[side, 0:24, :], corner], axis=0))
    from_right = iota((TALL, LANES), 1) < 64

    @pl.loop(0, PAIRS + 4)
    def _(i):
        g = i + jnp.where(i >= PAIRS + 2, PAIRS - 2, 0)
        right_part = pltpu.roll(beside[0], lax.rem(LANES - 3 * g, LANES), 1)
        left_part = pltpu.roll(beside[1], LANES - 3 * g - 3, 1)
        side_columns[i] = jnp.where(from_right, right_part, left_part)

    def whole(own, plane, l, sides):
        below, above = near_slabs[0, plane], near_slabs[1, plane]
        below = jnp.where(l == 0, below, pltpu.roll(below, 4, 0))
        above = jnp.where(l == 0, pltpu.roll(above, 4, 0), above)
        tall = jnp.concatenate([own, jnp.where(upper, below, above)], axis=0)
        return jnp.concatenate([tall, sides], axis=1)

    @pl.loop(0, LEVELS)
    def _(l):
        keep = 1.0 - mixed[0]
        speed_y, speed_x = (
            whole(courant[d, l], FIELDS + d, l, side_columns[PAIRS + 2 * d + l]) for d in range(2)
        )
        south = jnp.where(row == 0, 0.0, jnp.maximum(speed_y, 0.0) + DIFFUSION) * keep
        north = jnp.where(row == last_row, 0.0, DIFFUSION - jnp.minimum(speed_y, 0.0)) * keep
        west = jnp.where(col == 0, 0.0, jnp.maximum(speed_x, 0.0) + DIFFUSION) * keep
        east = jnp.where(col == last_col, 0.0, DIFFUSION - jnp.minimum(speed_x, 0.0)) * keep
        coef[l, 0] = (1.0 - MIXING) * keep - south - north - west - east
        coef[l, 1] = south
        coef[l, 2] = north
        coef[l, 3] = west
        coef[l, 4] = east
        mixed[1] = MIXING * keep

    @pl.when(rim_column)
    def _():
        pltpu.make_async_copy(spread, spread_in, spread_recv).wait()
        column = iota((TALL, LANES), 1)
        block = pl.ds(pl.multiple_of(pick(section == 2, 0, COLS - LANES), LANES), LANES)
        share = mixed[0, :, block]

        @pl.loop(0, PAIRS)
        def _(pair):
            for which, target in ((0, force), (1, slope)):
                turned = pltpu.roll(spread_in[which], lax.rem(LANES - 3 * pair, LANES), 1)
                lead, middle, trail = (
                    jnp.broadcast_to(turned[:, c : c + 1], (TALL, LANES)) for c in range(3)
                )
                filled = jnp.where(column < 3, lead, jnp.where(column < 125, middle, trail))
                target[pair, :, block] = share * filled

    @pl.when(rim_row)
    def _():
        pltpu.make_async_copy(rows_out.at[0], rows_in, rows_recv).wait()
        sub = iota((8, WIDE), 0)
        first = sub < pick(at_top, 3, 5)
        in_zone = (sub >= pick(at_top, 0, 3)) & (sub < pick(at_top, 5, 8))
        block = pl.ds(pl.multiple_of(pick(at_top, 0, 16), 8), 8)
        share = mixed[0, block, :]

        @pl.loop(0, FIELDS)
        def _(f):
            rows = rows_in[f]
            for l in range(LEVELS):
                for target, one, two in ((force, 4 * l + 1, 4 * l + 2), (slope, 4 * l + 3, (4 * l + 4) % 8)):
                    filled = jnp.where(first, rows[one : one + 1, :], rows[two : two + 1, :])
                    old = target[LEVELS * f + l, block, :]
                    target[LEVELS * f + l, block, :] = jnp.where(in_zone, share * filled, old)

    ahead = iota((COLS, LANES), 0) - RATIO * iota((COLS, LANES), 1)
    gather = jnp.where((ahead >= 0) & (ahead < RATIO), 1.0, 0.0).astype(jnp.bfloat16)

    def send_means(f):
        @pl.loop(0, 2)
        def _(late):
            target = relay_tile(group + late, middle)

            @pl.when(target != tile)
            def _():
                remote(
                    means.at[f], relay_in.at[f, late, inner], relay_send.at[late], relay_recv.at[f],
                    (target, section),
                ).start()

            @pl.when(target == tile)
            def _():
                pltpu.make_async_copy(means.at[f], relay_in.at[f, late, inner], relay_recv.at[f]).start()

    steps = pick(is_parent, 1, RATIO)

    @pl.loop(0, FIELDS)
    def _(f):
        for l in range(LEVELS):
            work[l] = whole(state[f, l], f, l, side_columns[LEVELS * f + l])

        @pl.loop(0, steps)
        def _(k):
            fraction = (k + 1).astype(jnp.float32)
            pair = [work[l] for l in range(LEVELS)]
            mix = mixed[1]
            for l in range(LEVELS):
                value = pair[l]
                work[l] = (
                    coef[l, 0] * value
                    + coef[l, 1] * pltpu.roll(value, 1, 0)
                    + coef[l, 2] * pltpu.roll(value, TALL - 1, 0)
                    + coef[l, 3] * pltpu.roll(value, 1, 1)
                    + coef[l, 4] * pltpu.roll(value, WIDE - 1, 1)
                    + mix * pair[1 - l]
                    + (force[LEVELS * f + l] + fraction * slope[LEVELS * f + l])
                )

        for l in range(LEVELS):
            out[f, l] = work[l, :ROWS, :COLS]

        @pl.when(is_nest)
        def _():
            for l in range(LEVELS):
                for c in range(RATIO):
                    fine[c, l] = work[l, :ROWS, LANES * c : LANES * (c + 1)]
            sums = [
                sum(fine[c, :, pl.ds(k, COARSE, stride=RATIO), :] for k in range(RATIO))
                .reshape(LEVELS * COARSE, LANES)
                for c in range(RATIO)
            ]
            block = dot_ones(jnp.concatenate(sums, axis=1), gather) * (1.0 / (RATIO * RATIO))
            means[f] = block.reshape(LEVELS, COARSE, LANES)
            send_means(f)

    def mean_copy(f):
        return remote(
            relay_out.at[f], mean_in.at[f, third], mean_send, mean_recv.at[f],
            (q + task, owner),
        )

    @pl.when(is_relay)
    def _():
        @pl.loop(0, FIELDS)
        def _(f):
            full = (task >= 1) & (task < groups)

            @pl.when(full)
            def _():
                whole_wait(relay_in.at[f], relay_recv.at[f])

            @pl.when(jnp.logical_not(full))
            def _():
                whole_wait(relay_in.at[f, 0], relay_recv.at[f])

            for l in range(LEVELS):
                lined = jnp.concatenate(
                    [relay_in[f, late, b, l] for late in (1, 0) for b in range(RATIO)], axis=0
                )
                relay_out[f, l] = pltpu.roll(lined, rest + ROWS, 0)[:ROWS, :]
            mean_copy(f).start()

    @pl.when(under)
    def _():
        coarse_row = ROWS * (tile - q) - rest + iota((ROWS, COLS), 0)
        covered = (coarse_row >= 0) & (coarse_row < ROWS * groups)

        @pl.loop(0, FIELDS)
        def _(f):
            whole_wait(mean_in.at[f], mean_recv.at[f])
            for l in range(LEVELS):
                fed = jnp.concatenate([mean_in[f, c, l] for c in range(RATIO)], axis=1)
                out[f, l] = jnp.where(covered, fed, out[f, l])

    near_wait(near_send, has_left, has_right)

    @pl.when(in_window)
    def _():
        whole_wait(window_in.at[0, 0:4], window_send)

    for_edges(lambda d, aim: whole_wait(edge_in.at[0:RATIO], edge_send.at[d]))

    @pl.when(is_parent)
    def _():
        spread_copy().wait_send()

    @pl.when(row_relay)
    def _():
        whole_wait(rows_out, rows_send)

    @pl.when(is_nest)
    def _():
        @pl.loop(0, 2)
        def _(late):
            @pl.when(relay_tile(group + late, middle) != tile)
            def _():
                whole_wait(means, relay_send.at[late])

    @pl.when(is_relay)
    def _():
        whole_wait(relay_out, mean_send)


def solution(mesh):
    tiles = mesh.shape["tile"]
    sections = mesh.shape["section"]
    choices = max(tiles // 6 - 1, 4) - 1
    vmem = pl.BlockSpec(memory_space=pltpu.VMEM)
    anywhere = pl.BlockSpec(memory_space=pl.ANY)

    def call(q, state, courant, nest_offset):
        def space(*shape):
            return pltpu.VMEM(shape, jnp.float32)

        def copies(*shape):
            return pltpu.SemaphoreType.DMA(shape)

        one = pltpu.SemaphoreType.DMA
        return pl.pallas_call(
            functools.partial(kernel, q, tiles, sections),
            out_shape=jax.ShapeDtypeStruct(state.shape, state.dtype),
            in_specs=[pl.BlockSpec(memory_space=pltpu.SMEM), anywhere, anywhere],
            out_specs=vmem,
            scratch_shapes=[
                space(FIELDS, LEVELS, ROWS, COLS),
                space(2, LEVELS, ROWS, COLS),
                space(2, ROWS, LANES),
                space(2, ROWS + 16, LANES),
                space(2, PLANES, 8, COLS),
                space(2, PLANES, 8, COLS),
                space(PAIRS + 4, TALL, LANES),
                space(4, ROWS, LANES),
                space(2, TALL, LANES),
                space(2, TALL, LANES),
                space(3, PLANES, 8, LANES),
                space(3, 5, PLANES, 8, LANES),
                space(RATIO, FIELDS, 8, WIDE),
                space(FIELDS, 8, WIDE),
                space(LEVELS, 5, TALL, WIDE),
                space(2, TALL, WIDE),
                space(PAIRS, TALL, WIDE),
                space(PAIRS, TALL, WIDE),
                space(LEVELS, TALL, WIDE),
                space(RATIO, LEVELS, ROWS, LANES),
                space(FIELDS, LEVELS, COARSE, LANES),
                space(FIELDS, 2, RATIO, LEVELS, COARSE, LANES),
                space(FIELDS, LEVELS, ROWS, LANES),
                space(FIELDS, RATIO, LEVELS, ROWS, LANES),
                copies(2), copies(3), copies(3), copies(4), one, one, one,
                one, one, one, one, pltpu.SemaphoreType.REGULAR, pltpu.SemaphoreType.REGULAR((RATIO,)),
                copies(2), copies(FIELDS), one, copies(FIELDS),
            ],
            compiler_params=pltpu.CompilerParams(collective_id=q, has_side_effects=True),
            name=f"nested_step_{q}",
        )(nest_offset, state, courant)

    def on_device(state, courant, nest_offset):
        branches = [functools.partial(call, q) for q in range(1, choices + 1)]
        choice = jnp.clip(nest_offset[0] // ROWS - 1, 0, choices - 1)
        return lax.switch(choice, branches, state, courant, nest_offset)

    return jax.shard_map(
        on_device,
        mesh=mesh,
        in_specs=(P(None, None, "tile", "section"), P(None, None, "tile", "section"), P()),
        out_specs=P(None, None, "tile", "section"),
        check_vma=False,
    )
```

```python
import functools

import jax
import jax.numpy as jnp
from jax import lax
from jax.experimental import pallas as pl
from jax.experimental.pallas import tpu as pltpu
from jax.sharding import PartitionSpec as P

RATIO = 3
ZONE = 5
DIFFUSION = 0.02
MIXING = 0.05
FIELDS = 5
LEVELS = 2
ROWS = 24
COLS = 384
LANES = 128
COARSE = ROWS // RATIO
TALL = 32
WIDE = 512
PAIRS = FIELDS * LEVELS
PLANES = FIELDS + 2
MESH = pl.DeviceIdType.MESH

NEAR = ((-1, 0), (1, 0), (0, -1), (-1, -1), (1, -1), (0, 1), (-1, 1), (1, 1))


def iota(shape, dim):
    return lax.broadcasted_iota(jnp.int32, shape, dim)


def pick(flag, one, other):
    return jnp.where(flag, one, other)


def thirds(value):
    high = value.astype(jnp.bfloat16)
    rest = value - high.astype(jnp.float32)
    middle = rest.astype(jnp.bfloat16)
    low = (rest - middle.astype(jnp.float32)).astype(jnp.bfloat16)
    return [high, middle, low]


def dot_ones(value, ones):
    rows = value.shape[0]
    parts = jnp.dot(jnp.concatenate(thirds(value), axis=0), ones, preferred_element_type=jnp.float32)
    return parts[:rows] + parts[rows : 2 * rows] + parts[2 * rows :]


def kernel(
    q, tiles, sections,
    offset_ref, state_in, courant_in, out,
    state, courant, strips, near_strips, slabs, near_slabs, side_columns,
    edge_in, spread, spread_in, stage, window_in, rows_out, rows_in,
    coef, mixed, force, slope, work,
    fine, means, relay_in, relay_out, mean_in,
    load_sem, near_send, near_recv, edge_send, edge_recv, window_send, window_recv,
    spread_send, spread_recv, rows_send, rows_recv, edge_ready, rows_ready,
    relay_send, relay_recv, mean_send, mean_recv,
):
    tile = lax.axis_index("tile")
    section = lax.axis_index("section")
    groups = tiles // RATIO
    is_parent = section < 2
    is_nest = section >= 2
    nest = section - 2
    group = tile // RATIO
    inner = tile - group * RATIO
    rest = offset_ref[0] - q * ROWS
    rim_column = (section == 2) | (section == sections - 1)
    at_top = tile == 0
    at_end = at_top | (tile == tiles - 1)
    rim_row = is_nest & at_end
    top_relay = tile == (RATIO - 1) * groups
    row_relay = is_parent & (top_relay | (tile == groups - 1))
    rows_tile = pick(at_top, (RATIO - 1) * groups, groups - 1)
    rows_to = pick(top_relay, 0, tiles - 1)
    has_left = (section != 0) & (section != 2)
    has_right = (section != 1) & (section != sections - 1)
    low_window = is_parent & (tile >= q - 1) & (tile <= q + 1)
    high_window = is_parent & (tile >= q + groups - 1) & (tile <= q + groups)
    in_window = low_window | high_window
    window_to = pick(low_window, (RATIO - 1) * groups, groups - 1)
    window_slot = pick(low_window, tile - q + 1, tile - q - groups + 1)
    window_first = pick(top_relay, q - 1, q + groups - 1)
    window_count = pick(top_relay, 3, 2)
    under = is_parent & (tile >= q) & (tile <= q + groups)
    third = lax.rem(lax.max(nest, 0), RATIO)
    owner = lax.max(nest, 0) // RATIO

    middle = (section == 4) | (section == 5)

    def relay_tile(a, middle):
        plane = lax.min(a, groups - 1) * RATIO // groups
        plane = pick(middle & (a == 0), 1, pick(middle & (a == groups), 0, plane))
        return plane * groups + lax.rem(q + a, groups)

    turn = lax.rem(tile - q + tiles, groups)
    wrapped = (turn == 0) & (tile // groups == pick(middle, 0, RATIO - 1))
    task = pick(wrapped, groups, turn)
    is_relay = is_nest & (relay_tile(task, middle) == tile)

    def near_peer(step):
        return tile + step[0], section + step[1]

    def for_near(items, act):
        for rows_step in (-1, 0, 1):
            for cols_step in (-1, 0, 1):
                found = [i for i, step in items if step == (rows_step, cols_step)]
                if not found:
                    continue
                exists = has_left if cols_step < 0 else has_right if cols_step > 0 else None
                if rows_step:
                    inside = (tile > 0) if rows_step < 0 else (tile < tiles - 1)
                    exists = inside if exists is None else exists & inside

                @pl.when(exists)
                def _():
                    for i in found:
                        act(i)

    loads = [
        pltpu.make_async_copy(state_in, state, load_sem.at[0]),
        pltpu.make_async_copy(courant_in, courant, load_sem.at[1]),
    ]
    for load in loads:
        load.start()

    @pl.when(row_relay)
    def _():
        @pl.loop(0, 3)
        def _(u):
            @pl.loop(0, 5)
            def _(slot):
                window_in[u, slot] = jnp.zeros((PLANES, 8, LANES), jnp.float32)

    near_strips[...] = jnp.zeros_like(near_strips)
    near_slabs[...] = jnp.zeros_like(near_slabs)

    barrier = pltpu.get_barrier_semaphore()

    def greet(tile_to, section_to):
        pl.semaphore_signal(
            barrier, inc=1, device_id=(tile_to, section_to), device_id_type=MESH
        )

    rim_section = pick(section == 0, sections - 1, 2)

    @pl.when(is_parent)
    def _():
        greet(tile, rim_section)

        @pl.loop(0, 4)
        def _(d):
            greet(q + group + d - 1, 1 - section)

    @pl.when(row_relay)
    def _():
        @pl.loop(0, RATIO)
        def _(k):
            greet(rows_to, 2 + RATIO * section + k)

        @pl.loop(0, window_count)
        def _(u):
            greet(window_first + u, 0)
            greet(window_first + u, 1)

    for_near(list(enumerate(NEAR)), lambda i: greet(*near_peer(NEAR[i])))

    def relay_source(late):
        return (task - late >= 0) & (task - late < groups)

    @pl.when(is_relay)
    def _():
        @pl.loop(0, 2)
        def _(late):
            @pl.when(relay_source(late))
            def _():
                @pl.loop(0, RATIO)
                def _(b):
                    source = (task - late) * RATIO + b

                    @pl.when(source != tile)
                    def _():
                        greet(source, section)

    @pl.when(under)
    def _():
        @pl.loop(0, RATIO)
        def _(third):
            mate = 2 + RATIO * section + third
            greet(relay_tile(tile - q, (mate == 4) | (mate == 5)), mate)

    @pl.loop(0, PAIRS)
    def _(pair):
        force[pair] = jnp.zeros((TALL, WIDE), jnp.float32)
        slope[pair] = jnp.zeros((TALL, WIDE), jnp.float32)

    for load in loads:
        load.wait()

    upper = iota((8, COLS), 0) < 4

    def pack_rows(plane, first, second):
        slabs[0, plane] = jnp.where(upper, first[0:8, :], pltpu.roll(second[0:8, :], 4, 0))
        slabs[1, plane] = jnp.where(upper, pltpu.roll(first[16:24, :], 4, 0), second[16:24, :])

    @pl.loop(0, FIELDS)
    def _(f):
        pack_rows(f, state[f, 0], state[f, 1])

    @pl.loop(0, 2)
    def _(d):
        pack_rows(FIELDS + d, courant[d, 0], courant[d, 1])

    lane = iota((ROWS, LANES), 1)

    def pack_columns(f, packed):
        left, right = packed
        for l in range(LEVELS):
            for kind in range(3):
                g = PAIRS * kind + LEVELS * f + l
                source = state.at[f, l] if kind == 0 else courant.at[kind - 1, l]
                here = (lane >= 3 * g) & (lane < 3 * g + 3)
                left = jnp.where(here, pltpu.roll(source[:, :LANES], 3 * g, 1), left)
                right = jnp.where(here, pltpu.roll(source[:, COLS - LANES :], 3 * g + 3, 1), right)
        return left, right

    blank = jnp.zeros((ROWS, LANES), jnp.float32)
    left, right = lax.fori_loop(0, FIELDS, pack_columns, (blank, blank))
    strips[0] = left
    strips[1] = right

    @pl.when(in_window)
    def _():
        start = rest + pick(low_window, -1 - ROWS * (tile - q), 21 - ROWS * (tile - q - groups + 1))
        sub = iota((8, COLS), 0)

        def window_rows(plane, source):
            value = jnp.zeros((8, COLS), jnp.float32)
            for l in range(LEVELS):
                for j in range(4):
                    row = start + j
                    owned = (row >= 0) & (row < ROWS)
                    line = source(l)[pl.ds(jnp.clip(row, 0, ROWS - 1), 1), :] * jnp.where(owned, 1.0, 0.0)
                    value = jnp.where(sub == 4 * l + j, line, value)
            for k in range(3):
                stage[k, plane] = value[:, LANES * k : LANES * (k + 1)]

        @pl.loop(0, FIELDS)
        def _(f):
            window_rows(f, lambda l: state.at[f, l])

        @pl.loop(0, 2)
        def _(d):
            window_rows(FIELDS + d, lambda l: courant.at[d, l])

    edge_targets = sum(
        jnp.where((tile - q + 1 - d >= 0) & (tile - q + 1 - d < groups), RATIO, 0) for d in range(4)
    )
    window_targets = jnp.where(in_window, 2, 0)
    relay_targets = (
        sum(jnp.where(relay_tile(group + late, middle) != tile, 1, 0) for late in range(2))
        + jnp.where(is_relay, 1, 0)
        + jnp.where(rim_column, 1, 0)
        + jnp.where(rim_row, 1, 0)
    )
    vertical = jnp.where(at_end, 1, 2)
    near_targets = vertical + (1 + vertical) * (jnp.where(has_left, 1, 0) + jnp.where(has_right, 1, 0))
    waited = near_targets + pick(is_parent, edge_targets + window_targets, relay_targets)
    pl.semaphore_wait(barrier, waited)

    @pl.when(rim_column)
    def _():
        pl.semaphore_signal(
            edge_ready, inc=1, device_id=(tile, pick(section == 2, 1, 0)), device_id_type=MESH
        )

    @pl.when(rim_row)
    def _():
        pl.semaphore_signal(rows_ready.at[third], inc=1, device_id=(rows_tile, owner), device_id_type=MESH)

    def remote(source, target, send, recv, device):
        return pltpu.make_async_remote_copy(
            src_ref=source, dst_ref=target, send_sem=send, recv_sem=recv,
            device_id=device, device_id_type=MESH,
        )

    def whole_wait(source, semaphore):
        pltpu.make_async_copy(source, source, semaphore).wait()

    @pl.when(in_window)
    def _():
        remote(
            stage, window_in.at[window_slot, 1:4], window_send, window_recv, (window_to, section)
        ).start()
        remote(
            stage.at[pick(section == 0, 2, 0)], window_in.at[window_slot, pick(section == 0, 0, 4)],
            window_send, window_recv, (window_to, 1 - section),
        ).start()

    def for_edges(act):
        @pl.when(is_parent)
        def _():
            @pl.loop(0, 4)
            def _(d):
                aim = tile - q + 1 - d

                @pl.when((aim >= 0) & (aim < groups))
                def _():
                    act(d, aim)

    def send_edges(d, aim):
        @pl.loop(0, RATIO)
        def _(b):
            remote(
                strips.at[section], edge_in.at[d], edge_send.at[d], edge_recv, (aim * RATIO + b, 1 - section)
            ).start()

    for_edges(send_edges)

    def near_copy(i):
        source, target = (
            (slabs.at[0], near_slabs.at[0]),
            (slabs.at[1], near_slabs.at[1]),
            (strips.at[0], near_strips.at[0, 0:24]),
            (strips.at[0, 0:8], near_strips.at[0, 24:32]),
            (strips.at[0, 16:24], near_strips.at[0, 32:40]),
            (strips.at[1], near_strips.at[1, 0:24]),
            (strips.at[1, 0:8], near_strips.at[1, 24:32]),
            (strips.at[1, 16:24], near_strips.at[1, 32:40]),
        )[i]
        kind = (0, 3, 1, 1, 1, 2, 2, 2)[i]
        return remote(source, target, near_send.at[kind], near_recv.at[kind], near_peer(NEAR[i]))

    for_near([(i, NEAR[i]) for i in (2, 3, 4, 5, 6, 7, 0, 1)], lambda i: near_copy(i).start())

    def near_wait(semaphores, first_side, second_side, first_slab, second_slab):
        for side, exists in ((0, first_side), (1, second_side)):
            @pl.when(exists & at_end)
            def _():
                whole_wait(near_strips.at[side, 0:32], semaphores.at[1 + side])

            @pl.when(exists & jnp.logical_not(at_end))
            def _():
                whole_wait(near_strips.at[side], semaphores.at[1 + side])

        @pl.when(first_slab)
        def _():
            whole_wait(near_slabs.at[0], semaphores.at[0])

        @pl.when(second_slab)
        def _():
            whole_wait(near_slabs.at[1], semaphores.at[3])

    def spread_copy():
        return remote(spread, spread_in, spread_send, spread_recv, (tile, rim_section))

    def rows_copy(k):
        return remote(
            rows_out.at[k], rows_in, rows_send, rows_recv, (rows_to, 2 + RATIO * section + k)
        )

    @pl.when(is_parent)
    def _():
        whole_wait(edge_in, edge_recv)
        shape = (4 * ROWS, LANES)
        value = edge_in[...].reshape(shape)
        speed_y = pltpu.roll(value, LANES - 3 * PAIRS, 1)
        speed_x = pltpu.roll(value, LANES - 6 * PAIRS, 1)
        place = iota(shape, 1)
        trio = (place * 171) >> 9
        within = place - 3 * trio
        partner = jnp.where((trio & 1) == 0, pltpu.roll(value, LANES - 3, 1), pltpu.roll(value, 3, 1))
        change = (
            (jnp.maximum(speed_y, 0.0) + DIFFUSION) * (pltpu.roll(value, 1, 0) - value)
            + (DIFFUSION - jnp.minimum(speed_y, 0.0)) * (pltpu.roll(value, 4 * ROWS - 1, 0) - value)
            + jnp.where(within == 0, 0.0, jnp.maximum(speed_x, 0.0) + DIFFUSION) * (pltpu.roll(value, 1, 1) - value)
            + jnp.where(within == 2, 0.0, DIFFUSION - jnp.minimum(speed_x, 0.0))
            * (pltpu.roll(value, LANES - 1, 1) - value)
            + MIXING * (partner - value)
        ) * (1.0 / RATIO)
        wide = (TALL, 12 * ROWS)
        tall_row = iota(wide, 0)
        tall_row = jnp.where(tall_row < 28, tall_row, tall_row - TALL) + RATIO
        wanted = ((tall_row * 171) >> 9) - 1 + (ROWS + rest + COARSE * inner)
        source = iota(wide, 1)
        select = (source == wanted) | (source == wanted + 4 * ROWS) | (source == wanted + 8 * ROWS)
        both = jnp.concatenate([value, change], axis=1)
        rows = jnp.dot(
            jnp.where(select, 1.0, 0.0).astype(jnp.bfloat16),
            jnp.concatenate(thirds(both), axis=0),
            preferred_element_type=jnp.float32,
        )
        spread[0] = rows[:, :LANES]
        spread[1] = rows[:, LANES:]
    @pl.when(row_relay)
    def _():
        @pl.when(top_relay)
        def _():
            whole_wait(window_in.at[:, 0:4], window_recv)

        @pl.when(jnp.logical_not(top_relay))
        def _():
            whole_wait(window_in.at[0:2, 0:4], window_recv)

        def window(plane):
            return jnp.concatenate([sum(window_in[u, k, plane] for u in range(3)) for k in range(5)], axis=1)

        shape = (8, 5 * LANES)
        speed_y, speed_x = window(FIELDS), window(FIELDS + 1)
        parent_col = iota(shape, 1) + (COLS * section - LANES)
        south = jnp.maximum(speed_y, 0.0) + DIFFUSION
        north = DIFFUSION - jnp.minimum(speed_y, 0.0)
        west = jnp.where(parent_col == 0, 0.0, jnp.maximum(speed_x, 0.0) + DIFFUSION)
        east = jnp.where(parent_col == 2 * COLS - 1, 0.0, DIFFUSION - jnp.minimum(speed_x, 0.0))
        within = iota(shape, 0) & 3
        is_value = (within == 1) | (within == 2)

        @pl.loop(0, FIELDS)
        def _(f):
            value = window(f)
            change = (
                south * (pltpu.roll(value, 1, 0) - value)
                + north * (pltpu.roll(value, 7, 0) - value)
                + west * (pltpu.roll(value, 1, 1) - value)
                + east * (pltpu.roll(value, 5 * LANES - 1, 1) - value)
                + MIXING * (pltpu.roll(value, 4, 0) - value)
            ) * (1.0 / RATIO)
            both = jnp.where(is_value, value, pltpu.roll(change, 2, 0))
            for k in range(RATIO):
                rows_out[k, f, :, 0:COLS] = both[:, LANES * k : LANES * k + COLS]

        stacked = rows_out[:, :, :, 0:COLS].reshape(RATIO * FIELDS * 8, COLS)

        @pl.loop(0, WIDE // LANES)
        def _(k):
            column = iota((COLS, LANES), 1) + LANES * k
            column = jnp.where(column < 448, column, column - WIDE)
            ahead = column - RATIO * (iota((COLS, LANES), 0) - LANES)
            widen = jnp.where((ahead >= 0) & (ahead < RATIO), 1.0, 0.0).astype(jnp.bfloat16)
            lanes = pl.ds(pl.multiple_of(LANES * k, LANES), LANES)
            rows_out[:, :, :, lanes] = dot_ones(stacked, widen).reshape(RATIO, FIELDS, 8, LANES)

    @pl.when(row_relay)
    def _():
        @pl.loop(0, RATIO)
        def _(k):
            pl.semaphore_wait(rows_ready.at[k], 1)
            rows_copy(k).start()

    @pl.when(is_parent)
    def _():
        pl.semaphore_wait(edge_ready, 1)
        spread_copy().start()

    row = iota((TALL, WIDE), 0)
    col = iota((TALL, WIDE), 1)
    row = tile * ROWS + jnp.where(row < 28, row, row - TALL)
    col = pick(is_parent, section, nest) * COLS + jnp.where(col < 448, col, col - WIDE)
    last_row = tiles * ROWS - 1
    last_col = pick(is_parent, 2, 6) * COLS - 1
    depth = jnp.minimum(jnp.minimum(row, last_row - row), jnp.minimum(col, last_col - col))
    strength = pick(is_parent, 0.0, 1.0 / ZONE)
    mixed[0] = jnp.clip(ZONE - depth, 0, ZONE).astype(jnp.float32) * strength

    near_wait(near_recv, has_right, has_left, tile < tiles - 1, tile > 0)

    half = iota((8, LANES), 0) < 4
    beside = []
    for side in range(2):
        corner = jnp.where(half, near_strips[side, 24:32, :], near_strips[side, 32:40, :])
        beside.append(jnp.concatenate([near_strips[side, 0:24, :], corner], axis=0))
    from_right = iota((TALL, LANES), 1) < 64

    @pl.loop(0, PAIRS + 4)
    def _(i):
        g = i + jnp.where(i >= PAIRS + 2, PAIRS - 2, 0)
        right_part = pltpu.roll(beside[0], lax.rem(LANES - 3 * g, LANES), 1)
        left_part = pltpu.roll(beside[1], LANES - 3 * g - 3, 1)
        side_columns[i] = jnp.where(from_right, right_part, left_part)

    def whole(own, plane, l, sides):
        below, above = near_slabs[0, plane], near_slabs[1, plane]
        below = jnp.where(l == 0, below, pltpu.roll(below, 4, 0))
        above = jnp.where(l == 0, pltpu.roll(above, 4, 0), above)
        tall = jnp.concatenate([own, jnp.where(upper, below, above)], axis=0)
        return jnp.concatenate([tall, sides], axis=1)

    @pl.loop(0, LEVELS)
    def _(l):
        keep = 1.0 - mixed[0]
        speed_y, speed_x = (
            whole(courant[d, l], FIELDS + d, l, side_columns[PAIRS + 2 * d + l]) for d in range(2)
        )
        south = jnp.where(row == 0, 0.0, jnp.maximum(speed_y, 0.0) + DIFFUSION) * keep
        north = jnp.where(row == last_row, 0.0, DIFFUSION - jnp.minimum(speed_y, 0.0)) * keep
        west = jnp.where(col == 0, 0.0, jnp.maximum(speed_x, 0.0) + DIFFUSION) * keep
        east = jnp.where(col == last_col, 0.0, DIFFUSION - jnp.minimum(speed_x, 0.0)) * keep
        coef[l, 0] = (1.0 - MIXING) * keep - south - north - west - east
        coef[l, 1] = south
        coef[l, 2] = north
        coef[l, 3] = west
        coef[l, 4] = east
        mixed[1] = MIXING * keep

    @pl.when(rim_column)
    def _():
        pltpu.make_async_copy(spread, spread_in, spread_recv).wait()
        column = iota((TALL, LANES), 1)
        block = pl.ds(pl.multiple_of(pick(section == 2, 0, COLS - LANES), LANES), LANES)
        share = mixed[0, :, block]

        @pl.loop(0, PAIRS)
        def _(pair):
            for which, target in ((0, force), (1, slope)):
                turned = pltpu.roll(spread_in[which], lax.rem(LANES - 3 * pair, LANES), 1)
                lead, middle, trail = (
                    jnp.broadcast_to(turned[:, c : c + 1], (TALL, LANES)) for c in range(3)
                )
                filled = jnp.where(column < 3, lead, jnp.where(column < 125, middle, trail))
                target[pair, :, block] = share * filled

    @pl.when(rim_row)
    def _():
        pltpu.make_async_copy(rows_out.at[0], rows_in, rows_recv).wait()
        sub = iota((8, WIDE), 0)
        first = sub < pick(at_top, 3, 5)
        in_zone = (sub >= pick(at_top, 0, 3)) & (sub < pick(at_top, 5, 8))
        block = pl.ds(pl.multiple_of(pick(at_top, 0, 16), 8), 8)
        share = mixed[0, block, :]

        @pl.loop(0, FIELDS)
        def _(f):
            rows = rows_in[f]
            for l in range(LEVELS):
                for target, one, two in ((force, 4 * l + 1, 4 * l + 2), (slope, 4 * l + 3, (4 * l + 4) % 8)):
                    filled = jnp.where(first, rows[one : one + 1, :], rows[two : two + 1, :])
                    old = target[LEVELS * f + l, block, :]
                    target[LEVELS * f + l, block, :] = jnp.where(in_zone, share * filled, old)

    ahead = iota((COLS, LANES), 0) - RATIO * iota((COLS, LANES), 1)
    gather = jnp.where((ahead >= 0) & (ahead < RATIO), 1.0, 0.0).astype(jnp.bfloat16)

    def send_means(f):
        @pl.loop(0, 2)
        def _(late):
            target = relay_tile(group + late, middle)

            @pl.when(target != tile)
            def _():
                remote(
                    means.at[f], relay_in.at[f, late, inner], relay_send.at[late], relay_recv.at[f],
                    (target, section),
                ).start()

            @pl.when(target == tile)
            def _():
                pltpu.make_async_copy(means.at[f], relay_in.at[f, late, inner], relay_recv.at[f]).start()

    steps = pick(is_parent, 1, RATIO)

    @pl.loop(0, FIELDS)
    def _(f):
        for l in range(LEVELS):
            work[l] = whole(state[f, l], f, l, side_columns[LEVELS * f + l])

        @pl.loop(0, steps)
        def _(k):
            fraction = (k + 1).astype(jnp.float32)
            pair = [work[l] for l in range(LEVELS)]
            mix = mixed[1]
            for l in range(LEVELS):
                value = pair[l]
                work[l] = (
                    coef[l, 0] * value
                    + coef[l, 1] * pltpu.roll(value, 1, 0)
                    + coef[l, 2] * pltpu.roll(value, TALL - 1, 0)
                    + coef[l, 3] * pltpu.roll(value, 1, 1)
                    + coef[l, 4] * pltpu.roll(value, WIDE - 1, 1)
                    + mix * pair[1 - l]
                    + (force[LEVELS * f + l] + fraction * slope[LEVELS * f + l])
                )

        for l in range(LEVELS):
            out[f, l] = work[l, :ROWS, :COLS]

        @pl.when(is_nest)
        def _():
            for l in range(LEVELS):
                for c in range(RATIO):
                    fine[c, l] = work[l, :ROWS, LANES * c : LANES * (c + 1)]
            sums = [
                sum(fine[c, :, pl.ds(k, COARSE, stride=RATIO), :] for k in range(RATIO))
                .reshape(LEVELS * COARSE, LANES)
                for c in range(RATIO)
            ]
            block = dot_ones(jnp.concatenate(sums, axis=1), gather) * (1.0 / (RATIO * RATIO))
            means[f] = block.reshape(LEVELS, COARSE, LANES)
            send_means(f)

    def mean_copy(f):
        return remote(
            relay_out.at[f], mean_in.at[f, third], mean_send, mean_recv.at[f],
            (q + task, owner),
        )

    @pl.when(is_relay)
    def _():
        @pl.loop(0, FIELDS)
        def _(f):
            full = (task >= 1) & (task < groups)

            @pl.when(full)
            def _():
                whole_wait(relay_in.at[f], relay_recv.at[f])

            @pl.when(jnp.logical_not(full))
            def _():
                whole_wait(relay_in.at[f, 0], relay_recv.at[f])

            for l in range(LEVELS):
                lined = jnp.concatenate(
                    [relay_in[f, late, b, l] for late in (1, 0) for b in range(RATIO)], axis=0
                )
                relay_out[f, l] = pltpu.roll(lined, rest + ROWS, 0)[:ROWS, :]
            mean_copy(f).start()

    @pl.when(under)
    def _():
        coarse_row = ROWS * (tile - q) - rest + iota((ROWS, COLS), 0)
        covered = (coarse_row >= 0) & (coarse_row < ROWS * groups)

        @pl.loop(0, FIELDS)
        def _(f):
            whole_wait(mean_in.at[f], mean_recv.at[f])
            for l in range(LEVELS):
                fed = jnp.concatenate([mean_in[f, c, l] for c in range(RATIO)], axis=1)
                out[f, l] = jnp.where(covered, fed, out[f, l])

    near_wait(near_send, has_left, has_right, tile > 0, tile < tiles - 1)

    @pl.when(in_window)
    def _():
        whole_wait(window_in.at[0, 0:4], window_send)

    for_edges(lambda d, aim: whole_wait(edge_in.at[0:RATIO], edge_send.at[d]))

    @pl.when(is_parent)
    def _():
        spread_copy().wait_send()

    @pl.when(row_relay)
    def _():
        whole_wait(rows_out, rows_send)

    @pl.when(is_nest)
    def _():
        @pl.loop(0, 2)
        def _(late):
            @pl.when(relay_tile(group + late, middle) != tile)
            def _():
                whole_wait(means, relay_send.at[late])

    @pl.when(is_relay)
    def _():
        whole_wait(relay_out, mean_send)


def solution(mesh):
    tiles = mesh.shape["tile"]
    sections = mesh.shape["section"]
    choices = max(tiles // 6 - 1, 4) - 1
    vmem = pl.BlockSpec(memory_space=pltpu.VMEM)
    anywhere = pl.BlockSpec(memory_space=pl.ANY)

    def call(q, state, courant, nest_offset):
        def space(*shape):
            return pltpu.VMEM(shape, jnp.float32)

        def copies(*shape):
            return pltpu.SemaphoreType.DMA(shape)

        one = pltpu.SemaphoreType.DMA
        return pl.pallas_call(
            functools.partial(kernel, q, tiles, sections),
            out_shape=jax.ShapeDtypeStruct(state.shape, state.dtype),
            in_specs=[pl.BlockSpec(memory_space=pltpu.SMEM), anywhere, anywhere],
            out_specs=vmem,
            scratch_shapes=[
                space(FIELDS, LEVELS, ROWS, COLS),
                space(2, LEVELS, ROWS, COLS),
                space(2, ROWS, LANES),
                space(2, ROWS + 16, LANES),
                space(2, PLANES, 8, COLS),
                space(2, PLANES, 8, COLS),
                space(PAIRS + 4, TALL, LANES),
                space(4, ROWS, LANES),
                space(2, TALL, LANES),
                space(2, TALL, LANES),
                space(3, PLANES, 8, LANES),
                space(3, 5, PLANES, 8, LANES),
                space(RATIO, FIELDS, 8, WIDE),
                space(FIELDS, 8, WIDE),
                space(LEVELS, 5, TALL, WIDE),
                space(2, TALL, WIDE),
                space(PAIRS, TALL, WIDE),
                space(PAIRS, TALL, WIDE),
                space(LEVELS, TALL, WIDE),
                space(RATIO, LEVELS, ROWS, LANES),
                space(FIELDS, LEVELS, COARSE, LANES),
                space(FIELDS, 2, RATIO, LEVELS, COARSE, LANES),
                space(FIELDS, LEVELS, ROWS, LANES),
                space(FIELDS, RATIO, LEVELS, ROWS, LANES),
                copies(2), copies(4), copies(4), copies(4), one, one, one,
                one, one, one, one, pltpu.SemaphoreType.REGULAR, pltpu.SemaphoreType.REGULAR((RATIO,)),
                copies(2), copies(FIELDS), one, copies(FIELDS),
            ],
            compiler_params=pltpu.CompilerParams(collective_id=q, has_side_effects=True),
            name=f"nested_step_{q}",
        )(nest_offset, state, courant)

    def on_device(state, courant, nest_offset):
        branches = [functools.partial(call, q) for q in range(1, choices + 1)]
        choice = jnp.clip(nest_offset[0] // ROWS - 1, 0, choices - 1)
        return lax.switch(choice, branches, state, courant, nest_offset)

    return jax.shard_map(
        on_device,
        mesh=mesh,
        in_specs=(P(None, None, "tile", "section"), P(None, None, "tile", "section"), P()),
        out_specs=P(None, None, "tile", "section"),
        check_vma=False,
    )
```

```python
import functools

import jax
import jax.numpy as jnp
from jax import lax
from jax.experimental import pallas as pl
from jax.experimental.pallas import tpu as pltpu
from jax.sharding import PartitionSpec as P

RATIO = 3
ZONE = 5
DIFFUSION = 0.02
MIXING = 0.05
FIELDS = 5
LEVELS = 2
ROWS = 24
COLS = 384
LANES = 128
COARSE = ROWS // RATIO
TALL = 32
WIDE = 512
PAIRS = FIELDS * LEVELS
PLANES = FIELDS + 2
MESH = pl.DeviceIdType.MESH

NEAR = ((-1, 0), (1, 0), (0, -1), (-1, -1), (1, -1), (0, 1), (-1, 1), (1, 1))


def iota(shape, dim):
    return lax.broadcasted_iota(jnp.int32, shape, dim)


def pick(flag, one, other):
    return jnp.where(flag, one, other)


def thirds(value):
    high = value.astype(jnp.bfloat16)
    rest = value - high.astype(jnp.float32)
    middle = rest.astype(jnp.bfloat16)
    low = (rest - middle.astype(jnp.float32)).astype(jnp.bfloat16)
    return [high, middle, low]


def dot_ones(value, ones):
    rows = value.shape[0]
    parts = jnp.dot(jnp.concatenate(thirds(value), axis=0), ones, preferred_element_type=jnp.float32)
    return parts[:rows] + parts[rows : 2 * rows] + parts[2 * rows :]


def kernel(
    q, tiles, sections,
    offset_ref, state_in, courant_in, out,
    state, courant, strips, near_strips, slabs, near_slabs, side_columns,
    edge_in, spread, spread_in, stage, window_in, rows_out, rows_in,
    coef, mixed, col_force, row_force, work,
    fine, means, relay_in, relay_out, mean_in,
    load_sem, near_send, near_recv, edge_send, edge_recv, window_send, window_recv,
    spread_send, spread_recv, rows_send, rows_recv, edge_ready, rows_ready,
    relay_send, relay_recv, mean_send, mean_recv,
):
    tile = lax.axis_index("tile")
    section = lax.axis_index("section")
    groups = tiles // RATIO
    is_parent = section < 2
    is_nest = section >= 2
    nest = section - 2
    group = tile // RATIO
    inner = tile - group * RATIO
    rest = offset_ref[0] - q * ROWS
    rim_column = (section == 2) | (section == sections - 1)
    at_top = tile == 0
    at_end = at_top | (tile == tiles - 1)
    rim_row = is_nest & at_end
    top_relay = tile == (RATIO - 1) * groups
    row_relay = is_parent & (top_relay | (tile == groups - 1))
    rows_tile = pick(at_top, (RATIO - 1) * groups, groups - 1)
    rows_to = pick(top_relay, 0, tiles - 1)
    has_left = (section != 0) & (section != 2)
    has_right = (section != 1) & (section != sections - 1)
    low_window = is_parent & (tile >= q - 1) & (tile <= q + 1)
    high_window = is_parent & (tile >= q + groups - 1) & (tile <= q + groups)
    in_window = low_window | high_window
    window_to = pick(low_window, (RATIO - 1) * groups, groups - 1)
    window_slot = pick(low_window, tile - q + 1, tile - q - groups + 1)
    window_first = pick(top_relay, q - 1, q + groups - 1)
    window_count = pick(top_relay, 3, 2)
    under = is_parent & (tile >= q) & (tile <= q + groups)
    third = lax.rem(lax.max(nest, 0), RATIO)
    owner = lax.max(nest, 0) // RATIO

    middle = (section == 4) | (section == 5)

    def relay_tile(a, middle):
        plane = lax.min(a, groups - 1) * RATIO // groups
        plane = pick(middle & (a == 0), 1, pick(middle & (a == groups), 0, plane))
        return plane * groups + lax.rem(q + a, groups)

    turn = lax.rem(tile - q + tiles, groups)
    wrapped = (turn == 0) & (tile // groups == pick(middle, 0, RATIO - 1))
    task = pick(wrapped, groups, turn)
    is_relay = is_nest & (relay_tile(task, middle) == tile)

    def near_peer(step):
        return tile + step[0], section + step[1]

    def for_near(items, act):
        for rows_step in (-1, 0, 1):
            for cols_step in (-1, 0, 1):
                found = [i for i, step in items if step == (rows_step, cols_step)]
                if not found:
                    continue
                exists = has_left if cols_step < 0 else has_right if cols_step > 0 else None
                if rows_step:
                    inside = (tile > 0) if rows_step < 0 else (tile < tiles - 1)
                    exists = inside if exists is None else exists & inside

                @pl.when(exists)
                def _():
                    for i in found:
                        act(i)

    loads = [
        pltpu.make_async_copy(state_in, state, load_sem.at[0]),
        pltpu.make_async_copy(courant_in, courant, load_sem.at[1]),
    ]
    for load in loads:
        load.start()

    @pl.when(row_relay)
    def _():
        @pl.loop(0, 3)
        def _(u):
            @pl.loop(0, 5)
            def _(slot):
                window_in[u, slot] = jnp.zeros((PLANES, 8, LANES), jnp.float32)

    near_strips[...] = jnp.zeros_like(near_strips)
    near_slabs[...] = jnp.zeros_like(near_slabs)

    barrier = pltpu.get_barrier_semaphore()

    def greet(tile_to, section_to):
        pl.semaphore_signal(
            barrier, inc=1, device_id=(tile_to, section_to), device_id_type=MESH
        )

    rim_section = pick(section == 0, sections - 1, 2)

    @pl.when(is_parent)
    def _():
        greet(tile, rim_section)

        @pl.loop(0, 4)
        def _(d):
            greet(q + group + d - 1, 1 - section)

    @pl.when(row_relay)
    def _():
        @pl.loop(0, RATIO)
        def _(k):
            greet(rows_to, 2 + RATIO * section + k)

        @pl.loop(0, window_count)
        def _(u):
            greet(window_first + u, 0)
            greet(window_first + u, 1)

    def relay_source(late):
        return (task - late >= 0) & (task - late < groups)

    @pl.when(is_relay)
    def _():
        @pl.loop(0, 2)
        def _(late):
            @pl.when(relay_source(late))
            def _():
                @pl.loop(0, RATIO)
                def _(b):
                    source = (task - late) * RATIO + b

                    @pl.when(source != tile)
                    def _():
                        greet(source, section)

    for_near(list(enumerate(NEAR)), lambda i: greet(*near_peer(NEAR[i])))

    @pl.when(under)
    def _():
        @pl.loop(0, RATIO)
        def _(third):
            mate = 2 + RATIO * section + third
            greet(relay_tile(tile - q, (mate == 4) | (mate == 5)), mate)

    for load in loads:
        load.wait()

    upper = iota((8, COLS), 0) < 4

    def pack_rows(plane, first, second):
        slabs[0, plane] = jnp.where(upper, first[0:8, :], pltpu.roll(second[0:8, :], 4, 0))
        slabs[1, plane] = jnp.where(upper, pltpu.roll(first[16:24, :], 4, 0), second[16:24, :])

    @pl.loop(0, FIELDS)
    def _(f):
        pack_rows(f, state[f, 0], state[f, 1])

    @pl.loop(0, 2)
    def _(d):
        pack_rows(FIELDS + d, courant[d, 0], courant[d, 1])

    lane = iota((ROWS, LANES), 1)

    def pack_columns(f, packed):
        left, right = packed
        for l in range(LEVELS):
            for kind in range(3):
                g = PAIRS * kind + LEVELS * f + l
                source = state.at[f, l] if kind == 0 else courant.at[kind - 1, l]
                here = (lane >= 3 * g) & (lane < 3 * g + 3)
                left = jnp.where(here, pltpu.roll(source[:, :LANES], 3 * g, 1), left)
                right = jnp.where(here, pltpu.roll(source[:, COLS - LANES :], 3 * g + 3, 1), right)
        return left, right

    blank = jnp.zeros((ROWS, LANES), jnp.float32)
    left, right = lax.fori_loop(0, FIELDS, pack_columns, (blank, blank))
    strips[0] = left
    strips[1] = right

    @pl.when(in_window)
    def _():
        start = rest + pick(low_window, -1 - ROWS * (tile - q), 21 - ROWS * (tile - q - groups + 1))
        sub = iota((8, COLS), 0)

        def window_rows(plane, source):
            value = jnp.zeros((8, COLS), jnp.float32)
            for l in range(LEVELS):
                for j in range(4):
                    row = start + j
                    owned = (row >= 0) & (row < ROWS)
                    line = source(l)[pl.ds(jnp.clip(row, 0, ROWS - 1), 1), :] * jnp.where(owned, 1.0, 0.0)
                    value = jnp.where(sub == 4 * l + j, line, value)
            for k in range(3):
                stage[k, plane] = value[:, LANES * k : LANES * (k + 1)]

        @pl.loop(0, FIELDS)
        def _(f):
            window_rows(f, lambda l: state.at[f, l])

        @pl.loop(0, 2)
        def _(d):
            window_rows(FIELDS + d, lambda l: courant.at[d, l])

    edge_targets = sum(
        jnp.where((tile - q + 1 - d >= 0) & (tile - q + 1 - d < groups), RATIO, 0) for d in range(4)
    )
    window_targets = jnp.where(in_window, 2, 0)
    relay_targets = (
        sum(jnp.where(relay_tile(group + late, middle) != tile, 1, 0) for late in range(2))
        + jnp.where(is_relay, 1, 0)
        + jnp.where(rim_column, 1, 0)
        + jnp.where(rim_row, 1, 0)
    )
    vertical = jnp.where(at_end, 1, 2)
    near_targets = vertical + (1 + vertical) * (jnp.where(has_left, 1, 0) + jnp.where(has_right, 1, 0))
    waited = near_targets + pick(is_parent, edge_targets + window_targets, relay_targets)
    pl.semaphore_wait(barrier, waited)

    @pl.when(rim_column)
    def _():
        pl.semaphore_signal(
            edge_ready, inc=1, device_id=(tile, pick(section == 2, 1, 0)), device_id_type=MESH
        )

    @pl.when(rim_row)
    def _():
        pl.semaphore_signal(rows_ready.at[third], inc=1, device_id=(rows_tile, owner), device_id_type=MESH)

    def remote(source, target, send, recv, device):
        return pltpu.make_async_remote_copy(
            src_ref=source, dst_ref=target, send_sem=send, recv_sem=recv,
            device_id=device, device_id_type=MESH,
        )

    def whole_wait(source, semaphore):
        pltpu.make_async_copy(source, source, semaphore).wait()

    @pl.when(in_window)
    def _():
        remote(
            stage, window_in.at[window_slot, 1:4], window_send, window_recv, (window_to, section)
        ).start()
        remote(
            stage.at[pick(section == 0, 2, 0)], window_in.at[window_slot, pick(section == 0, 0, 4)],
            window_send, window_recv, (window_to, 1 - section),
        ).start()

    def for_edges(act):
        @pl.when(is_parent)
        def _():
            @pl.loop(0, 4)
            def _(d):
                aim = tile - q + 1 - d

                @pl.when((aim >= 0) & (aim < groups))
                def _():
                    act(d, aim)

    def send_edges(d, aim):
        @pl.loop(0, RATIO)
        def _(b):
            remote(
                strips.at[section], edge_in.at[d], edge_send.at[d], edge_recv, (aim * RATIO + b, 1 - section)
            ).start()

    for_edges(send_edges)

    def near_copy(i):
        source, target = (
            (slabs.at[0], near_slabs.at[0]),
            (slabs.at[1], near_slabs.at[1]),
            (strips.at[0], near_strips.at[0, 0:24]),
            (strips.at[0, 0:8], near_strips.at[0, 24:32]),
            (strips.at[0, 16:24], near_strips.at[0, 32:40]),
            (strips.at[1], near_strips.at[1, 0:24]),
            (strips.at[1, 0:8], near_strips.at[1, 24:32]),
            (strips.at[1, 16:24], near_strips.at[1, 32:40]),
        )[i]
        kind = (0, 3, 1, 1, 1, 2, 2, 2)[i]
        return remote(source, target, near_send.at[kind], near_recv.at[kind], near_peer(NEAR[i]))

    for_near([(i, NEAR[i]) for i in (2, 3, 4, 5, 6, 7, 0, 1)], lambda i: near_copy(i).start())

    def near_wait(semaphores, first_side, second_side, first_slab, second_slab):
        for side, exists in ((0, first_side), (1, second_side)):
            @pl.when(exists & at_end)
            def _():
                whole_wait(near_strips.at[side, 0:32], semaphores.at[1 + side])

            @pl.when(exists & jnp.logical_not(at_end))
            def _():
                whole_wait(near_strips.at[side], semaphores.at[1 + side])

        @pl.when(first_slab)
        def _():
            whole_wait(near_slabs.at[0], semaphores.at[0])

        @pl.when(second_slab)
        def _():
            whole_wait(near_slabs.at[1], semaphores.at[3])

    def spread_copy():
        return remote(spread, spread_in, spread_send, spread_recv, (tile, rim_section))

    def rows_copy(k):
        return remote(
            rows_out.at[k], rows_in, rows_send, rows_recv, (rows_to, 2 + RATIO * section + k)
        )

    @pl.when(is_parent)
    def _():
        whole_wait(edge_in, edge_recv)
        shape = (4 * ROWS, LANES)
        value = edge_in[...].reshape(shape)
        speed_y = pltpu.roll(value, LANES - 3 * PAIRS, 1)
        speed_x = pltpu.roll(value, LANES - 6 * PAIRS, 1)
        place = iota(shape, 1)
        trio = (place * 171) >> 9
        within = place - 3 * trio
        partner = jnp.where((trio & 1) == 0, pltpu.roll(value, LANES - 3, 1), pltpu.roll(value, 3, 1))
        change = (
            (jnp.maximum(speed_y, 0.0) + DIFFUSION) * (pltpu.roll(value, 1, 0) - value)
            + (DIFFUSION - jnp.minimum(speed_y, 0.0)) * (pltpu.roll(value, 4 * ROWS - 1, 0) - value)
            + jnp.where(within == 0, 0.0, jnp.maximum(speed_x, 0.0) + DIFFUSION) * (pltpu.roll(value, 1, 1) - value)
            + jnp.where(within == 2, 0.0, DIFFUSION - jnp.minimum(speed_x, 0.0))
            * (pltpu.roll(value, LANES - 1, 1) - value)
            + MIXING * (partner - value)
        ) * (1.0 / RATIO)
        wide = (TALL, 12 * ROWS)
        tall_row = iota(wide, 0)
        tall_row = jnp.where(tall_row < 28, tall_row, tall_row - TALL) + RATIO
        wanted = ((tall_row * 171) >> 9) - 1 + (ROWS + rest + COARSE * inner)
        source = iota(wide, 1)
        select = (source == wanted) | (source == wanted + 4 * ROWS) | (source == wanted + 8 * ROWS)
        both = jnp.concatenate([value, change], axis=1)
        rows = jnp.dot(
            jnp.where(select, 1.0, 0.0).astype(jnp.bfloat16),
            jnp.concatenate(thirds(both), axis=0),
            preferred_element_type=jnp.float32,
        )
        spread[0] = rows[:, :LANES]
        spread[1] = rows[:, LANES:]
    @pl.when(row_relay)
    def _():
        @pl.when(top_relay)
        def _():
            whole_wait(window_in.at[:, 0:4], window_recv)

        @pl.when(jnp.logical_not(top_relay))
        def _():
            whole_wait(window_in.at[0:2, 0:4], window_recv)

        def window(plane):
            return jnp.concatenate([sum(window_in[u, k, plane] for u in range(3)) for k in range(5)], axis=1)

        shape = (8, 5 * LANES)
        speed_y, speed_x = window(FIELDS), window(FIELDS + 1)
        parent_col = iota(shape, 1) + (COLS * section - LANES)
        south = jnp.maximum(speed_y, 0.0) + DIFFUSION
        north = DIFFUSION - jnp.minimum(speed_y, 0.0)
        west = jnp.where(parent_col == 0, 0.0, jnp.maximum(speed_x, 0.0) + DIFFUSION)
        east = jnp.where(parent_col == 2 * COLS - 1, 0.0, DIFFUSION - jnp.minimum(speed_x, 0.0))
        within = iota(shape, 0) & 3
        is_value = (within == 1) | (within == 2)

        @pl.loop(0, FIELDS)
        def _(f):
            value = window(f)
            change = (
                south * (pltpu.roll(value, 1, 0) - value)
                + north * (pltpu.roll(value, 7, 0) - value)
                + west * (pltpu.roll(value, 1, 1) - value)
                + east * (pltpu.roll(value, 5 * LANES - 1, 1) - value)
                + MIXING * (pltpu.roll(value, 4, 0) - value)
            ) * (1.0 / RATIO)
            both = jnp.where(is_value, value, pltpu.roll(change, 2, 0))
            for k in range(RATIO):
                rows_out[k, f, :, 0:COLS] = both[:, LANES * k : LANES * k + COLS]

        stacked = rows_out[:, :, :, 0:COLS].reshape(RATIO * FIELDS * 8, COLS)

        @pl.loop(0, WIDE // LANES)
        def _(k):
            column = iota((COLS, LANES), 1) + LANES * k
            column = jnp.where(column < 448, column, column - WIDE)
            ahead = column - RATIO * (iota((COLS, LANES), 0) - LANES)
            widen = jnp.where((ahead >= 0) & (ahead < RATIO), 1.0, 0.0).astype(jnp.bfloat16)
            lanes = pl.ds(pl.multiple_of(LANES * k, LANES), LANES)
            rows_out[:, :, :, lanes] = dot_ones(stacked, widen).reshape(RATIO, FIELDS, 8, LANES)

    @pl.when(row_relay)
    def _():
        @pl.loop(0, RATIO)
        def _(k):
            pl.semaphore_wait(rows_ready.at[k], 1)
            rows_copy(k).start()

    @pl.when(is_parent)
    def _():
        pl.semaphore_wait(edge_ready, 1)
        spread_copy().start()

    row = iota((TALL, WIDE), 0)
    col = iota((TALL, WIDE), 1)
    row = tile * ROWS + jnp.where(row < 28, row, row - TALL)
    col = pick(is_parent, section, nest) * COLS + jnp.where(col < 448, col, col - WIDE)
    last_row = tiles * ROWS - 1
    last_col = pick(is_parent, 2, 6) * COLS - 1
    depth = jnp.minimum(jnp.minimum(row, last_row - row), jnp.minimum(col, last_col - col))
    strength = pick(is_parent, 0.0, 1.0 / ZONE)
    mixed[0] = jnp.clip(ZONE - depth, 0, ZONE).astype(jnp.float32) * strength

    near_wait(near_recv, has_right, has_left, tile < tiles - 1, tile > 0)

    half = iota((8, LANES), 0) < 4
    beside = []
    for side in range(2):
        corner = jnp.where(half, near_strips[side, 24:32, :], near_strips[side, 32:40, :])
        beside.append(jnp.concatenate([near_strips[side, 0:24, :], corner], axis=0))
    from_right = iota((TALL, LANES), 1) < 64

    @pl.loop(0, PAIRS + 4)
    def _(i):
        g = i + jnp.where(i >= PAIRS + 2, PAIRS - 2, 0)
        right_part = pltpu.roll(beside[0], lax.rem(LANES - 3 * g, LANES), 1)
        left_part = pltpu.roll(beside[1], LANES - 3 * g - 3, 1)
        side_columns[i] = jnp.where(from_right, right_part, left_part)

    def whole(own, plane, l, sides):
        below, above = near_slabs[0, plane], near_slabs[1, plane]
        below = jnp.where(l == 0, below, pltpu.roll(below, 4, 0))
        above = jnp.where(l == 0, pltpu.roll(above, 4, 0), above)
        tall = jnp.concatenate([own, jnp.where(upper, below, above)], axis=0)
        return jnp.concatenate([tall, sides], axis=1)

    @pl.loop(0, LEVELS)
    def _(l):
        keep = 1.0 - mixed[0]
        speed_y, speed_x = (
            whole(courant[d, l], FIELDS + d, l, side_columns[PAIRS + 2 * d + l]) for d in range(2)
        )
        south = jnp.where(row == 0, 0.0, jnp.maximum(speed_y, 0.0) + DIFFUSION) * keep
        north = jnp.where(row == last_row, 0.0, DIFFUSION - jnp.minimum(speed_y, 0.0)) * keep
        west = jnp.where(col == 0, 0.0, jnp.maximum(speed_x, 0.0) + DIFFUSION) * keep
        east = jnp.where(col == last_col, 0.0, DIFFUSION - jnp.minimum(speed_x, 0.0)) * keep
        coef[l, 0] = (1.0 - MIXING) * keep - south - north - west - east
        coef[l, 1] = south
        coef[l, 2] = north
        coef[l, 3] = west
        coef[l, 4] = east
        mixed[1] = MIXING * keep

    col_block = pl.ds(pl.multiple_of(pick(section == 2, 0, COLS - LANES), LANES), LANES)
    row_block = pl.ds(pl.multiple_of(pick(at_top, 0, 16), 8), 8)

    @pl.when(rim_column)
    def _():
        whole_wait(spread_in, spread_recv)
        column = iota((TALL, LANES), 1)
        own_row = tile * ROWS + iota((TALL, LANES), 0)
        zone = (own_row < ZONE) | ((own_row > last_row - ZONE) & (own_row <= last_row))
        share = jnp.where(zone, 0.0, mixed[0, :, col_block])

        @pl.loop(0, PAIRS)
        def _(pair):
            for which in range(2):
                turned = pltpu.roll(spread_in[which], lax.rem(LANES - 3 * pair, LANES), 1)
                lead, middle_one, trail = (
                    jnp.broadcast_to(turned[:, c : c + 1], (TALL, LANES)) for c in range(3)
                )
                filled = jnp.where(column < 3, lead, jnp.where(column < 125, middle_one, trail))
                col_force[which, pair] = share * filled

    @pl.when(rim_row)
    def _():
        whole_wait(rows_in, rows_recv)
        sub = iota((8, WIDE), 0)
        first = sub < pick(at_top, 3, 5)
        in_zone = (sub >= pick(at_top, 0, 3)) & (sub < pick(at_top, 5, 8))
        share = jnp.where(in_zone, mixed[0, row_block, :], 0.0)

        @pl.loop(0, FIELDS)
        def _(f):
            rows = rows_in[f]
            for l in range(LEVELS):
                for which, one, two in ((0, 4 * l + 1, 4 * l + 2), (1, 4 * l + 3, (4 * l + 4) % 8)):
                    filled = jnp.where(first, rows[one : one + 1, :], rows[two : two + 1, :])
                    row_force[which, LEVELS * f + l] = share * filled

    ahead = iota((COLS, LANES), 0) - RATIO * iota((COLS, LANES), 1)
    gather = jnp.where((ahead >= 0) & (ahead < RATIO), 1.0, 0.0).astype(jnp.bfloat16)

    def send_means(f):
        @pl.loop(0, 2)
        def _(late):
            target = relay_tile(group + late, middle)

            @pl.when(target != tile)
            def _():
                remote(
                    means.at[f], relay_in.at[f, late, inner], relay_send.at[late], relay_recv.at[f],
                    (target, section),
                ).start()

            @pl.when(target == tile)
            def _():
                pltpu.make_async_copy(means.at[f], relay_in.at[f, late, inner], relay_recv.at[f]).start()

    steps = pick(is_parent, 1, RATIO)

    @pl.loop(0, FIELDS)
    def _(f):
        for l in range(LEVELS):
            work[l] = whole(state[f, l], f, l, side_columns[LEVELS * f + l])

        @pl.loop(0, steps)
        def _(k):
            fraction = (k + 1).astype(jnp.float32)
            pair = [work[l] for l in range(LEVELS)]
            mix = mixed[1]
            for l in range(LEVELS):
                value = pair[l]
                work[l] = (
                    coef[l, 0] * value
                    + coef[l, 1] * pltpu.roll(value, 1, 0)
                    + coef[l, 2] * pltpu.roll(value, TALL - 1, 0)
                    + coef[l, 3] * pltpu.roll(value, 1, 1)
                    + coef[l, 4] * pltpu.roll(value, WIDE - 1, 1)
                    + mix * pair[1 - l]
                )

            @pl.when(rim_column)
            def _():
                for l in range(LEVELS):
                    added = col_force[0, LEVELS * f + l] + fraction * col_force[1, LEVELS * f + l]
                    work[l, :, col_block] += added

            @pl.when(rim_row)
            def _():
                for l in range(LEVELS):
                    added = row_force[0, LEVELS * f + l] + fraction * row_force[1, LEVELS * f + l]
                    work[l, row_block, :] += added

        for l in range(LEVELS):
            out[f, l] = work[l, :ROWS, :COLS]

        @pl.when(is_nest)
        def _():
            for l in range(LEVELS):
                for c in range(RATIO):
                    fine[c, l] = work[l, :ROWS, LANES * c : LANES * (c + 1)]
            sums = [
                sum(fine[c, :, pl.ds(k, COARSE, stride=RATIO), :] for k in range(RATIO))
                .reshape(LEVELS * COARSE, LANES)
                for c in range(RATIO)
            ]
            block = dot_ones(jnp.concatenate(sums, axis=1), gather) * (1.0 / (RATIO * RATIO))
            means[f] = block.reshape(LEVELS, COARSE, LANES)
            send_means(f)

    def mean_copy(f):
        return remote(
            relay_out.at[f], mean_in.at[f, third], mean_send, mean_recv.at[f],
            (q + task, owner),
        )

    @pl.when(is_relay)
    def _():
        @pl.loop(0, FIELDS)
        def _(f):
            full = (task >= 1) & (task < groups)

            @pl.when(full)
            def _():
                whole_wait(relay_in.at[f], relay_recv.at[f])

            @pl.when(jnp.logical_not(full))
            def _():
                whole_wait(relay_in.at[f, 0], relay_recv.at[f])

            for l in range(LEVELS):
                lined = jnp.concatenate(
                    [relay_in[f, late, b, l] for late in (1, 0) for b in range(RATIO)], axis=0
                )
                relay_out[f, l] = pltpu.roll(lined, rest + ROWS, 0)[:ROWS, :]
            mean_copy(f).start()

    @pl.when(under)
    def _():
        coarse_row = ROWS * (tile - q) - rest + iota((ROWS, COLS), 0)
        covered = (coarse_row >= 0) & (coarse_row < ROWS * groups)

        @pl.loop(0, FIELDS)
        def _(f):
            whole_wait(mean_in.at[f], mean_recv.at[f])
            for l in range(LEVELS):
                fed = jnp.concatenate([mean_in[f, c, l] for c in range(RATIO)], axis=1)
                out[f, l] = jnp.where(covered, fed, out[f, l])

    near_wait(near_send, has_left, has_right, tile > 0, tile < tiles - 1)

    @pl.when(in_window)
    def _():
        whole_wait(window_in.at[0, 0:4], window_send)

    for_edges(lambda d, aim: whole_wait(edge_in.at[0:RATIO], edge_send.at[d]))

    @pl.when(is_parent)
    def _():
        spread_copy().wait_send()

    @pl.when(row_relay)
    def _():
        whole_wait(rows_out, rows_send)

    @pl.when(is_nest)
    def _():
        @pl.loop(0, 2)
        def _(late):
            @pl.when(relay_tile(group + late, middle) != tile)
            def _():
                whole_wait(means, relay_send.at[late])

    @pl.when(is_relay)
    def _():
        whole_wait(relay_out, mean_send)


def solution(mesh):
    tiles = mesh.shape["tile"]
    sections = mesh.shape["section"]
    choices = max(tiles // 6 - 1, 4) - 1
    vmem = pl.BlockSpec(memory_space=pltpu.VMEM)
    anywhere = pl.BlockSpec(memory_space=pl.ANY)

    def call(q, state, courant, nest_offset):
        def space(*shape):
            return pltpu.VMEM(shape, jnp.float32)

        def copies(*shape):
            return pltpu.SemaphoreType.DMA(shape)

        one = pltpu.SemaphoreType.DMA
        return pl.pallas_call(
            functools.partial(kernel, q, tiles, sections),
            out_shape=jax.ShapeDtypeStruct(state.shape, state.dtype),
            in_specs=[pl.BlockSpec(memory_space=pltpu.SMEM), anywhere, anywhere],
            out_specs=vmem,
            scratch_shapes=[
                space(FIELDS, LEVELS, ROWS, COLS),
                space(2, LEVELS, ROWS, COLS),
                space(2, ROWS, LANES),
                space(2, ROWS + 16, LANES),
                space(2, PLANES, 8, COLS),
                space(2, PLANES, 8, COLS),
                space(PAIRS + 4, TALL, LANES),
                space(4, ROWS, LANES),
                space(2, TALL, LANES),
                space(2, TALL, LANES),
                space(3, PLANES, 8, LANES),
                space(3, 5, PLANES, 8, LANES),
                space(RATIO, FIELDS, 8, WIDE),
                space(FIELDS, 8, WIDE),
                space(LEVELS, 5, TALL, WIDE),
                space(2, TALL, WIDE),
                space(2, PAIRS, TALL, LANES),
                space(2, PAIRS, 8, WIDE),
                space(LEVELS, TALL, WIDE),
                space(RATIO, LEVELS, ROWS, LANES),
                space(FIELDS, LEVELS, COARSE, LANES),
                space(FIELDS, 2, RATIO, LEVELS, COARSE, LANES),
                space(FIELDS, LEVELS, ROWS, LANES),
                space(FIELDS, RATIO, LEVELS, ROWS, LANES),
                copies(2), copies(4), copies(4), copies(4), one, one, one,
                one, one, one, one, pltpu.SemaphoreType.REGULAR, pltpu.SemaphoreType.REGULAR((RATIO,)),
                copies(2), copies(FIELDS), one, copies(FIELDS),
            ],
            compiler_params=pltpu.CompilerParams(collective_id=q, has_side_effects=True),
            name=f"nested_step_{q}",
        )(nest_offset, state, courant)

    def on_device(state, courant, nest_offset):
        branches = [functools.partial(call, q) for q in range(1, choices + 1)]
        choice = jnp.clip(nest_offset[0] // ROWS - 1, 0, choices - 1)
        return lax.switch(choice, branches, state, courant, nest_offset)

    return jax.shard_map(
        on_device,
        mesh=mesh,
        in_specs=(P(None, None, "tile", "section"), P(None, None, "tile", "section"), P()),
        out_specs=P(None, None, "tile", "section"),
        check_vma=False,
    )
```
